128 devices in a mesh: ty: 8 (over x_lo, y), tx: 16 (over z, x_hi, core).
Axes of the slice: x: 4 (x_hi: 2, x_lo: 2; x = x_hi * 2 + x_lo), y: 4, z: 4, core: 2. Of those that a mesh axis runs over, the one named last changes fastest.
Arguments:
- object_slices: float32 [2, 2, 2048, 4096], P(None, None, 'ty', 'tx'), may hold values from -5 to 5
- probe: float32 [2, 256, 256], replicated, may hold values from -5 to 5
- position_count: int32 [8, 16], P('ty', 'tx'), may hold values from 1 to 5, as said below
- offsets: int32 [8, 16, 5, 2], P('ty', 'tx'), may hold values from 0 to 128
- intensities: float32 [8, 16, 5, 256, 256], P('ty', 'tx'), may hold values from 0 to 2
Outputs:
- object_new: float32 [2, 2, 2048, 4096], P(None, None, 'ty', 'tx')
- probe_new: float32 [2, 256, 256], replicated
The draws below stay inside these ranges and needn't reach their ends.
Inputs may be any that keep to these rules, and one draw needn't show every extreme that they name: `position_count`: each tile has 1 to 5 positions; some tile has exactly 5.
All inputs are finite; a program needn't handle non-finite values.
Results may differ from the reference program's by a relative error of at most 0.0003.
Values sent between devices are 32-bit elements; how exact they have to be, the bound alone decides.
A program may use at most 128 MiB of HBM per device.

```python
import math
import jax
import jax.numpy as jnp
from jax import lax

PROBE = 256
CORE = 256
MARGIN = 64
MAXPOS = 5
ITERS = 2
NY = 2048
NX = 4096
N_TY = 8
N_TX = 16


def draw_position_count(key, part):
    first = jax.random.fold_in(key, 11)
    second = jax.random.fold_in(key, 23)
    counts = jax.random.randint(first, (N_TY * N_TX,), 1, MAXPOS + 1)
    chosen = jax.random.randint(second, (), 0, N_TY * N_TX)
    counts = counts.at[chosen].set(MAXPOS)
    return counts.reshape(N_TY, N_TX).astype(jnp.int32)


def set_ends(drawn, key, low, top_value):
    dims = drawn.shape
    index_at = [jax.random.randint(jax.random.fold_in(key, axis), (), 0, dims[axis]) for axis in range(len(dims))]
    drawn = drawn.at[tuple(index_at)].set(low)
    longest = dims.index(max(dims))
    index_at[longest] = (index_at[longest] + 1) % dims[longest]
    return drawn.at[tuple(index_at)].set(top_value)


def block_scale(key, shape, cuts, smallest, high):
    gain = 1.0
    for dim, blocks in cuts:
        heights = jax.random.uniform(jax.random.fold_in(jax.random.fold_in(key, 6), dim), (blocks,), jnp.float32, smallest / len(cuts), high / len(cuts))
        gain = gain * jnp.repeat(jnp.exp(heights), shape[dim] // blocks).reshape((-1,) + (1,) * (len(shape) - 1 - dim))
    return gain


def gaussian(stream_key, shape, deviation, reach, shards=(), kind=jnp.bfloat16):
    factor_of = block_scale(stream_key, shape, shards, -0.22, 0.18) if shards else 1.0
    array = jax.random.normal(stream_key, shape, jnp.float32) * deviation * factor_of
    return jnp.minimum(jnp.maximum(array, -reach), reach).astype(kind)


def setup_inputs(seed: int = 0) -> dict:
    key_list = jax.random.split(jax.random.key(seed), 6)
    object_slices = gaussian(key_list[0], (2, 2, NY, NX), 0.7, 5.0, ((2, 8), (3, 16)), jnp.float32)
    probe = gaussian(key_list[1], (2, PROBE, PROBE), 0.7, 5.0, (), jnp.float32)
    position_count = draw_position_count(jax.random.fold_in(key_list[5], 71), 0)
    offsets = set_ends(jax.random.randint(key_list[3], (N_TY, N_TX, MAXPOS, 2), 0, CORE + 2 * MARGIN - PROBE + 1), jax.random.fold_in(key_list[3], 1), 0, CORE + 2 * MARGIN - PROBE).astype(jnp.int32)
    intensities = jnp.clip(2.0 * jax.random.uniform(key_list[4], (N_TY, N_TX, MAXPOS, PROBE, PROBE), jnp.float32) ** block_scale(key_list[4], (N_TY, N_TX, MAXPOS, PROBE, PROBE), ((0, 8), (1, 16)), -0.2, 0.2), 0.0, 2.0)
    return dict(object_slices=object_slices, probe=probe, position_count=position_count, offsets=offsets, intensities=intensities)


chirp_rate = 0.5
object_rate = 0.5
probe_rate = 2.0

def matmul(left, right):
    return jnp.dot(left, right, precision=lax.Precision.HIGHEST, preferred_element_type=jnp.float32)

def complex_product(left_real, left_imag, right_real, right_imag):
    out_real = matmul(left_real, right_real) - matmul(left_imag, right_imag)
    out_imag = matmul(left_real, right_imag) + matmul(left_imag, right_real)
    return (out_real, out_imag)

def dft_tables(size):
    index = lax.iota(jnp.int32, size)
    product = index[:, None] * index[None, :] % size
    angles = product.astype(jnp.float32) * (2.0 * math.pi / size)
    factor = 1.0 / math.sqrt(size)
    four_real = jnp.cos(angles) * factor
    four_imag = -jnp.sin(angles) * factor
    centred = ((index + size // 2) % size - size // 2).astype(jnp.float32)
    phases = centred * centred * (chirp_rate * math.pi / size)
    kernel_real = jnp.cos(phases)
    kernel_imag = -jnp.sin(phases)
    scaled_real = four_real * kernel_real[None, :] + four_imag * kernel_imag[None, :]
    scaled_imag = four_real * kernel_imag[None, :] - four_imag * kernel_real[None, :]
    prop_real, prop_imag = complex_product(scaled_real, scaled_imag, four_real, four_imag)
    return (four_real, four_imag, prop_real, prop_imag)

def forward_pair(mat_real, mat_imag, field_real, field_imag):
    mid_real, mid_imag = complex_product(mat_real, mat_imag, field_real, field_imag)
    return complex_product(mid_real, mid_imag, mat_real.T, mat_imag.T)

def adjoint_pair(mat_real, mat_imag, field_real, field_imag):
    mid_real, mid_imag = complex_product(mat_real.T, -mat_imag.T, field_real, field_imag)
    return complex_product(mid_real, mid_imag, mat_real, -mat_imag)

def position_grad(probe_now, window, measured, tables):
    four_real, four_imag, prop_real, prop_imag = tables
    probe_real, probe_imag = (probe_now[0], probe_now[1])
    one_real, one_imag, two_real, two_imag = (window[0], window[1], window[2], window[3])
    wave_real = probe_real * one_real - probe_imag * one_imag
    wave_imag = probe_real * one_imag + probe_imag * one_real
    moved_real, moved_imag = forward_pair(prop_real, prop_imag, wave_real, wave_imag)
    exit_real = moved_real * two_real - moved_imag * two_imag
    exit_imag = moved_real * two_imag + moved_imag * two_real
    far_real, far_imag = forward_pair(four_real, four_imag, exit_real, exit_imag)
    misfit = far_real * far_real + far_imag * far_imag - measured
    back_real, back_imag = adjoint_pair(four_real, four_imag, misfit * far_real, misfit * far_imag)
    grad_two_real = moved_real * back_real + moved_imag * back_imag
    grad_two_imag = moved_real * back_imag - moved_imag * back_real
    gmove_real = two_real * back_real + two_imag * back_imag
    gmove_imag = two_real * back_imag - two_imag * back_real
    gwave_real, gwave_imag = adjoint_pair(prop_real, prop_imag, gmove_real, gmove_imag)
    grad_one_real = probe_real * gwave_real + probe_imag * gwave_imag
    grad_one_imag = probe_real * gwave_imag - probe_imag * gwave_real
    gprobe_real = one_real * gwave_real + one_imag * gwave_imag
    gprobe_imag = one_real * gwave_imag - one_imag * gwave_real
    object_part = jnp.stack([grad_one_real, grad_one_imag, grad_two_real, grad_two_imag])
    return (object_part, jnp.stack([gprobe_real, gprobe_imag]))

def reference(object_slices, probe, position_count, offsets, intensities):
    tables = dft_tables(PROBE)
    extent = CORE + 2 * MARGIN
    objects = object_slices.reshape(4, NY, NX)
    probe_now = probe
    zero = jnp.int32(0)
    for step in range(ITERS):
        padded = jnp.pad(objects, ((0, 0), (MARGIN, MARGIN), (MARGIN, MARGIN)), mode='wrap')

        def tile(index, carry):
            grads, probe_grad = carry
            row = (index // N_TX).astype(jnp.int32)
            column = (index % N_TX).astype(jnp.int32)
            extended = lax.dynamic_slice(padded, (zero, row * CORE, column * CORE), (4, extent, extent))

            def visit(slot, inner):
                local, local_probe = inner
                top = offsets[row, column, slot, 0].astype(jnp.int32)
                left = offsets[row, column, slot, 1].astype(jnp.int32)
                window = lax.dynamic_slice(extended, (zero, top, left), (4, PROBE, PROBE))
                object_part, probe_part = position_grad(probe_now, window, intensities[row, column, slot], tables)
                current = lax.dynamic_slice(local, (zero, top, left), (4, PROBE, PROBE))
                local = lax.dynamic_update_slice(local, current + object_part, (zero, top, left))
                return (local, local_probe + probe_part)
            start = (jnp.zeros((4, extent, extent), jnp.float32), jnp.zeros((2, PROBE, PROBE), jnp.float32))
            local, local_probe = lax.fori_loop(zero, position_count[row, column].astype(jnp.int32), visit, start)
            current = lax.dynamic_slice(grads, (zero, row * CORE, column * CORE), (4, extent, extent))
            grads = lax.dynamic_update_slice(grads, current + local, (zero, row * CORE, column * CORE))
            return (grads, probe_grad + local_probe)
        begin = (jnp.zeros((4, NY + 2 * MARGIN, NX + 2 * MARGIN), jnp.float32), jnp.zeros((2, PROBE, PROBE), jnp.float32))
        grads, probe_grad = lax.fori_loop(0, N_TY * N_TX, tile, begin)
        rows = grads[:, MARGIN:MARGIN + NY, :]
        rows = rows.at[:, NY - MARGIN:, :].add(grads[:, :MARGIN, :])
        rows = rows.at[:, :MARGIN, :].add(grads[:, NY + MARGIN:, :])
        total = rows[:, :, MARGIN:MARGIN + NX]
        total = total.at[:, :, NX - MARGIN:].add(rows[:, :, :MARGIN])
        total = total.at[:, :, :MARGIN].add(rows[:, :, NX + MARGIN:])
        peak = jnp.max(probe_now[0] * probe_now[0] + probe_now[1] * probe_now[1]) + 1e-06
        objects = objects - object_rate / peak * total
        probe_now = probe_now - probe_rate / (N_TY * N_TX) * probe_grad
    return (objects.reshape(2, 2, NY, NX), probe_now)
```

```python
import functools

import jax
import jax.numpy as jnp
import ml_dtypes
import numpy as np
from jax import lax
from jax.experimental import pallas as pl
from jax.experimental.pallas import tpu as pltpu
from jax.sharding import PartitionSpec as P

PROBE = 256
MAXPOS = 5
ITERS = 2
bf = jnp.bfloat16
f32 = jnp.float32

chirp_rate = 0.5
object_rate = 0.5
probe_rate = 2.0


def tables():
    n = PROBE
    k = np.arange(n)
    four = np.exp(-2j * np.pi * ((k[:, None] * k[None, :]) % n) / n) / np.sqrt(n)
    c = (((k + n // 2) % n) - n // 2).astype(np.float64)
    prop = (np.conj(four) * np.exp(-1j * chirp_rate * np.pi * c * c / n)[None, :]) @ four
    out = []
    for mat in (four, prop):
        real, imag = mat.real, mat.imag
        for part in (real, imag - real, real + imag):
            part = part.astype(np.float32)
            high = part.astype(ml_dtypes.bfloat16)
            out += [high, (part - high.astype(np.float32)).astype(ml_dtypes.bfloat16)]
    return np.stack(out).reshape(2, 3, 2, n, n)


def split(x):
    high = x.astype(bf)
    return high, (x - high.astype(f32)).astype(bf)


def dot(a, b):
    return jnp.dot(a, b, preferred_element_type=f32)


def left(tab, which, j, x):
    high, low = split(x)
    mat = jnp.concatenate([tab[which, j, 0], tab[which, j, 0], tab[which, j, 1]], axis=1)
    return dot(mat, jnp.concatenate([high, low, high], axis=0))


def right(tab, which, j, x):
    high, low = split(x)
    mat = jnp.concatenate([tab[which, j, 0], tab[which, j, 0], tab[which, j, 1]], axis=0)
    return dot(jnp.concatenate([high, low, high], axis=1), mat)


def sandwich(tab, which, real, imag, mid):
    shared = left(tab, which, 0, real + imag)
    mid[1] = shared + left(tab, which, 1, real)
    mid[0] = shared - left(tab, which, 2, imag)
    real, imag = mid[0], mid[1]
    shared = right(tab, which, 0, real + imag)
    return shared - right(tab, which, 2, imag), shared + right(tab, which, 1, real)


def compute_kernel(count_ref, off_ref, ext_ref, probe_ref, int_ref, tab, g_ref, gp_ref, win, moved, mid):
    g_ref[...] = jnp.zeros_like(g_ref)
    gp_ref[...] = jnp.zeros_like(gp_ref)
    lane = lax.broadcasted_iota(jnp.int32, (256, 128), 1)

    def visit(s, carry):
        top, left_col = off_ref[s, 0], off_ref[s, 1]
        inner = left_col >= 64
        t0 = jnp.where(inner, 0, 2)
        t1 = jnp.where(inner, 1, 0)
        t2 = jnp.where(inner, 2, 1)
        shift = jnp.where(inner, left_col - 64, left_col + 64)
        keep = lane < 128 - shift
        rows = pl.ds(top, 256)
        for p in range(4):
            a, b, c = [pltpu.roll(ext_ref[p, t, rows, :], 128 - shift, 1) for t in (t0, t1, t2)]
            win[p, :, 0:128] = jnp.where(keep, a, b)
            win[p, :, 128:256] = jnp.where(keep, b, c)
        pr, pi = probe_ref[0], probe_ref[1]
        moved[0], moved[1] = sandwich(tab, 1, pr * win[0] - pi * win[1], pr * win[1] + pi * win[0], mid)
        er = moved[0] * win[2] - moved[1] * win[3]
        ei = moved[0] * win[3] + moved[1] * win[2]
        fr, fi = sandwich(tab, 0, er, ei, mid)
        misfit = fr * fr + fi * fi - int_ref[s]
        cr, ci = sandwich(tab, 0, misfit * fr, -(misfit * fi), mid)
        g2r = moved[0] * cr - moved[1] * ci
        g2i = -(moved[0] * ci + moved[1] * cr)
        wr, wi = sandwich(tab, 1, win[2] * cr - win[3] * ci, win[2] * ci + win[3] * cr, mid)
        g1r = probe_ref[0] * wr - probe_ref[1] * wi
        g1i = -(probe_ref[0] * wi + probe_ref[1] * wr)
        for h, gp in enumerate((win[0] * wr - win[1] * wi, -(win[0] * wi + win[1] * wr))):
            gp_ref[h, 0] += gp[:, 0:128]
            gp_ref[h, 1] += gp[:, 128:256]
        before = lane < shift
        for p, g in enumerate((g1r, g1i, g2r, g2i)):
            a, b = pltpu.roll(g[:, 0:128], shift, 1), pltpu.roll(g[:, 128:256], shift, 1)
            g_ref[p, t0, rows, :] += jnp.where(before, 0.0, a)
            g_ref[p, t1, rows, :] += jnp.where(before, a, b)
            g_ref[p, t2, rows, :] += jnp.where(before, b, 0.0)
        return carry

    lax.fori_loop(0, count_ref[0], visit, 0)


def compute(count, off, ext, probe, inten, tab):
    vmem = pl.BlockSpec(memory_space=pltpu.VMEM)
    smem = pl.BlockSpec(memory_space=pltpu.SMEM)
    return pl.pallas_call(
        compute_kernel,
        out_shape=(jax.ShapeDtypeStruct((4, 3, 384, 128), f32), jax.ShapeDtypeStruct((2, 2, 256, 128), f32)),
        in_specs=[smem, smem, vmem, vmem, vmem, vmem],
        out_specs=(vmem, vmem),
        scratch_shapes=[pltpu.VMEM((4, 256, 256), f32), pltpu.VMEM((2, 256, 256), f32), pltpu.VMEM((2, 256, 256), f32)],
        compiler_params=pltpu.CompilerParams(vmem_limit_bytes=40 << 20),
        name="positions",
    )(count, off, ext, probe, inten, tab)


NTY, NTX = 8, 16
MESH = pl.DeviceIdType.MESH
DIRS = [(dy, dx) for dy in (-1, 0, 1) for dx in (-1, 0, 1) if (dy, dx) != (0, 0)]
V = pl.BlockSpec(memory_space=pltpu.VMEM)


def half_lanes(shape):
    return lax.broadcasted_iota(jnp.int32, shape, len(shape) - 1) < 64


def pack(x, side):
    rows = x.shape[1] // 2
    first, second = x[:, :rows], x[:, rows:]
    low = half_lanes(first.shape)
    if side > 0:
        return jnp.where(low, pltpu.roll(first, 64, 2), second)
    return jnp.where(low, first, pltpu.roll(second, 64, 2))


def unpack(buf, side):
    turned = pltpu.roll(buf, 64, 2)
    pair = [turned, buf] if side > 0 else [buf, turned]
    return jnp.concatenate(pair, axis=1)


def keep_side(x, side):
    low = half_lanes(x.shape)
    return jnp.where(low, 0.0, x) if side > 0 else jnp.where(low, x, 0.0)


class Place:
    def __init__(self):
        self.ty, self.tx = lax.axis_index("ty"), lax.axis_index("tx")
        self.x_lo, self.y = self.ty // 4, lax.rem(self.ty, 4)
        self.z, self.core = self.tx // 4, lax.rem(self.tx, 2)
        self.x_hi = lax.rem(self.tx // 2, 2)
        self.x = self.x_hi * 2 + self.x_lo
        self.spot = self.y * 4 + self.z

    def neighbour(self, dy, dx):
        return (lax.rem(self.ty + dy + NTY, NTY), lax.rem(self.tx + dx + NTX, NTX))

    def sibling(self):
        return (self.ty, self.tx + 1 - 2 * self.core)

    def plane(self, k):
        y, z = lax.rem(self.y + k // 4, 4), lax.rem(self.z + lax.rem(k, 4), 4)
        return y * 4 + z, (self.x_lo * 4 + y, z * 4 + self.x_hi * 2 + self.core)

    def column(self, k):
        x = lax.rem(self.x + k, 4)
        return x, (lax.rem(x, 2) * 4 + self.y, self.z * 4 + (x // 2) * 2 + self.core)


def remote(src, dst, send, recv, device):
    return pltpu.make_async_remote_copy(
        src_ref=src, dst_ref=dst, send_sem=send, recv_sem=recv, device_id=device, device_id_type=MESH
    )


class Edges:
    def __init__(self, place, rows, cols, corners, sems):
        self.place, self.rows, self.cols, self.corners = place, rows, cols, corners
        self.send, self.recv = sems

    def slot(self, bufs, dy, dx):
        if dx == 0:
            return bufs[0].at[(dy + 1) // 2]
        if dy == 0:
            return bufs[1].at[(dx + 1) // 2]
        return bufs[2].at[(dy + 1) + (dx + 1) // 2]

    def out(self, dy, dx):
        return self.slot((self.rows[0], self.cols[0], self.corners[0]), dy, dx)

    def inc(self, dy, dx):
        return self.slot((self.rows[1], self.cols[1], self.corners[1]), dy, dx)

    def copy(self, dy, dx):
        i = DIRS.index((dy, dx))
        return remote(self.out(dy, dx), self.inc(dy, dx), self.send.at[i], self.recv.at[i], self.place.neighbour(dy, dx))


ORDER = [(0, 1), (0, -1), (1, 0), (-1, 0), (1, 1), (1, -1), (-1, 1), (-1, -1)]


def pack_halo(e, core):
    for dy, dx in ORDER:
        r0, r1 = {-1: (0, 64), 0: (0, 256), 1: (192, 256)}[dy]
        if dx == 0:
            for t in range(2):
                e.out(dy, dx)[:, t] = core(t, r0, r1)
        else:
            e.out(dy, dx)[...] = pack(core((dx + 1) // 2, r0, r1), dx)


def unpack_halo(e, ext):
    for dy, dx in ORDER:
        e.copy(dy, dx).wait_recv()
    for dy in (-1, 1):
        r0 = 320 if dy < 0 else 0
        for t in range(2):
            ext[:, t, r0 : r0 + 64] = e.inc(dy, 0)[:, t]
    for dy in (-1, 0, 1):
        r0, r1 = {-1: (320, 384), 0: (64, 320), 1: (0, 64)}[dy]
        left, right = unpack(e.inc(dy, -1)[...], -1), unpack(e.inc(dy, 1)[...], 1)
        ext[:, 2, r0:r1] = jnp.where(half_lanes(left.shape), left, right)


def pack_fold(e, g):
    for dy, dx in ORDER:
        r0, r1 = {-1: (0, 64), 0: (64, 320), 1: (320, 384)}[dy]
        if dx == 0:
            for t in range(2):
                e.out(dy, dx)[:, t] = g[:, t, r0:r1]
        else:
            e.out(dy, dx)[...] = pack(g[:, 2, r0:r1], -dx)


def fold(e, g, total):
    for dy, dx in ORDER:
        e.copy(dy, dx).wait_recv()
    for t in range(2):
        total[:, t] = g[:, t, 64:320]
    for dy, dx in ORDER:
        r0, r1 = {-1: (192, 256), 0: (0, 256), 1: (0, 64)}[dy]
        if dx == 0:
            for t in range(2):
                total[:, t, r0:r1] += e.inc(dy, dx)[:, t]
        else:
            t = (1 - dx) // 2
            total[:, t, r0:r1] += keep_side(unpack(e.inc(dy, dx)[...], -dx), -dx)


def start_all(e):
    for dy, dx in ORDER:
        e.copy(dy, dx).start()


def wait_sent(e):
    for dy, dx in ORDER:
        e.copy(dy, dx).wait_send()


class Summer:
    def __init__(self, place, gp, pair, ready, plane, cross, whole, sems):
        self.p, self.gp, self.pair, self.ready, self.pl = place, gp, pair, ready, plane
        self.cross, self.whole, self.sems = cross, whole, sems

    def pair_copy(self, j):
        return remote(self.gp.at[1 - self.p.core, j], self.pair.at[j], self.sems[0].at[j], self.sems[1].at[j], self.p.sibling())

    def plane_copy(self, k):
        j, device = self.p.plane(k)
        return j, remote(self.ready.at[j], self.pl.at[k], self.sems[2].at[k], self.sems[3].at[k], device)

    def cross_copy(self, k):
        x, device = self.p.column(k)
        return remote(self.cross.at[self.p.x], self.cross.at[self.p.x], self.sems[4].at[k], self.sems[5].at[k], device)

    def cross_wait(self, k):
        self.cross_copy(k).wait_recv()

    def spread_copy(self, k):
        j, device = self.p.plane(k)
        own = self.whole.at[self.p.core, self.p.spot]
        return remote(own, own, self.sems[6].at[k], self.sems[7].at[k], device)

    def forward_copy(self, k):
        j, _ = self.p.plane(self.back(k))
        own = self.whole.at[self.p.core, j]
        return remote(own, own, self.sems[8].at[k], self.sems[9].at[k], self.p.sibling())

    def back(self, k):
        return lax.rem(4 - k // 4, 4) * 4 + lax.rem(4 - lax.rem(k, 4), 4)

    def begin(self):
        lax.fori_loop(0, 16, lambda k, c: (self.pair_copy(self.p.plane(k)[0]).start(), c)[1], 0)

    def scatter(self):
        def step(k, c):
            j, copy = self.plane_copy(k)
            self.pair_copy(j).wait_recv()
            self.ready[j] = self.gp[self.p.core, j] + self.pair[j]
            copy.start()
            return c

        lax.fori_loop(1, 16, step, 0)
        me = self.p.spot
        self.pair_copy(me).wait_recv()
        self.ready[me] = self.gp[self.p.core, me] + self.pair[me]

    def across(self):
        total = self.ready[self.p.spot]

        def step(k, c):
            self.plane_copy(k)[1].wait_recv()
            return c + self.pl[k]

        total = lax.fori_loop(1, 16, step, total)
        self.cross[self.p.x] = total
        lax.fori_loop(1, 4, lambda k, c: (self.cross_copy(k).start(), c)[1], 0)

    def spread(self):
        lax.fori_loop(1, 4, lambda k, c: (self.cross_copy(k).wait_recv(), c)[1], 0)
        self.whole[self.p.core, self.p.spot] = (self.cross[0] + self.cross[1]) + (self.cross[2] + self.cross[3])
        lax.fori_loop(1, 16, lambda k, c: (self.spread_copy(k).start(), c)[1], 0)
        self.forward_copy(0).start()

    def forward(self):
        def step(k, c):
            self.spread_copy(k).wait_recv()
            self.forward_copy(k).start()
            return c

        lax.fori_loop(1, 16, step, 0)

    def finish(self):
        lax.fori_loop(0, 16, lambda k, c: (self.forward_copy(k).wait_recv(), c)[1], 0)

    def sent(self):
        def step(k, c):
            self.pair_copy(self.p.plane(k)[0]).wait_send()
            self.forward_copy(k).wait_send()
            return c

        lax.fori_loop(0, 16, step, 0)

        def more(k, c):
            self.plane_copy(k)[1].wait_send()
            self.spread_copy(k).wait_send()
            return c

        lax.fori_loop(1, 16, more, 0)
        lax.fori_loop(1, 4, lambda k, c: (self.cross_copy(k).wait_send(), c)[1], 0)


def greet(p, summing):
    barrier = pltpu.get_barrier_semaphore()

    def hello(device):
        pl.semaphore_signal(barrier, inc=1, device_id=device, device_id_type=MESH)

    for dy, dx in DIRS:
        hello(p.neighbour(dy, dx))
    count = 8
    if summing:
        hello(p.sibling())
        lax.fori_loop(1, 16, lambda k, c: (hello(p.plane(k)[1]), c)[1], 0)
        lax.fori_loop(1, 4, lambda k, c: (hello(p.column(k)[1]), c)[1], 0)
        count += 19
    return lambda: pl.semaphore_wait(barrier, count)


def edge_scratch():
    return [
        pltpu.VMEM((2, 2, 4, 2, 64, 128), f32),
        pltpu.VMEM((2, 2, 4, 128, 128), f32),
        pltpu.VMEM((2, 4, 4, 32, 128), f32),
        pltpu.SemaphoreType.DMA((2, 8)),
    ]


def make_edges(p, rows, cols, corners, sems):
    pair = lambda ref: (ref.at[0], ref.at[1])
    return Edges(p, pair(rows), pair(cols), pair(corners), pair(sems))


def sum_scratch():
    return [
        pltpu.VMEM((16, 32, 128), f32),
        pltpu.VMEM((16, 32, 128), f32),
        pltpu.VMEM((16, 32, 128), f32),
        pltpu.VMEM((4, 32, 128), f32),
        pltpu.VMEM((2, 16, 32, 128), f32),
        pltpu.SemaphoreType.DMA((10, 16)),
    ]


def halo_kernel(obj, ext, rows, cols, corners, sems):
    p = Place()
    ready = greet(p, False)
    e = make_edges(p, rows, cols, corners, sems)
    core = lambda t, r0, r1: obj[:, r0:r1, t * 128 : t * 128 + 128]
    pack_halo(e, core)
    ready()
    start_all(e)
    for t in range(2):
        ext[:, t, 64:320] = core(t, 0, 256)
    unpack_halo(e, ext)
    wait_sent(e)


def step_size(probe):
    power = probe[0] * probe[0] + probe[1] * probe[1]
    peak = jnp.max(power, axis=(0, 1), keepdims=True) + 1e-06
    return object_rate / peak


def probe_update(probe, whole, out):
    for h in range(2):
        for t in range(2):
            cols = slice(t * 128, t * 128 + 128)
            grad = whole[h, 8 * t : 8 * t + 8].reshape(256, 128)
            out[h, :, cols] = probe[h, :, cols] - (probe_rate / (NTY * NTX)) * grad


def step_kernel(last, g, gp, old, probe, *refs):
    obj_out, probe_out, total = refs[:3]
    p = Place()
    ready = greet(p, True)
    f = make_edges(p, *refs[3:7])
    s = Summer(p, gp, *refs[7:12], [refs[12].at[i] for i in range(10)])
    pack_fold(f, g)
    ready()
    start_all(f)
    s.begin()
    s.scatter()
    rate = step_size(probe)
    fold(f, g, total)
    if last:
        for t in range(2):
            obj_out[:, :, t * 128 : t * 128 + 128] = old[:, t, 64:320] - rate * total[:, t]
    else:
        for t in range(2):
            obj_out[:, t, 64:320] = old[:, t, 64:320] - rate * total[:, t]
        e = make_edges(p, *refs[13:17])
        pack_halo(e, lambda t, r0, r1: obj_out[:, t, 64 + r0 : 64 + r1])
        start_all(e)
    s.across()
    s.spread()
    s.forward()
    if not last:
        unpack_halo(e, obj_out)
    s.finish()
    probe_update(probe, s.whole, probe_out)
    wait_sent(f)
    s.sent()
    if not last:
        wait_sent(e)


def halo(obj):
    return pl.pallas_call(
        halo_kernel,
        out_shape=jax.ShapeDtypeStruct((4, 3, 384, 128), f32),
        in_specs=[V],
        out_specs=V,
        scratch_shapes=edge_scratch(),
        compiler_params=pltpu.CompilerParams(collective_id=0, has_side_effects=True, vmem_limit_bytes=40 << 20),
        name="halo",
    )(obj)


def step(last, g, gp, old, probe):
    obj_shape = (4, 256, 256) if last else (4, 3, 384, 128)
    scratch = [pltpu.VMEM((4, 2, 256, 128), f32)] + edge_scratch() + sum_scratch()
    if not last:
        scratch += edge_scratch()
    return pl.pallas_call(
        functools.partial(step_kernel, last),
        out_shape=(jax.ShapeDtypeStruct(obj_shape, f32), jax.ShapeDtypeStruct((2, 256, 256), f32)),
        in_specs=[V] * 4,
        out_specs=(V, V),
        scratch_shapes=scratch,
        compiler_params=pltpu.CompilerParams(
            collective_id=2 if last else 1, has_side_effects=True, vmem_limit_bytes=48 << 20
        ),
        name="final_step" if last else "middle_step",
    )(g, gp.reshape(2, 16, 32, 128), old, probe)


def body(object_slices, probe, position_count, offsets, intensities):
    tab = jnp.asarray(tables())
    count, off = position_count[0], offsets[0, 0]
    inten = intensities[0, 0]
    ext = halo(object_slices.reshape(4, 256, 256))
    g, gp = compute(count, off, ext, probe, inten, tab)
    ext, probe = step(False, g, gp, ext, probe)
    g, gp = compute(count, off, ext, probe, inten, tab)
    core, probe = step(True, g, gp, ext, probe)
    return core.reshape(2, 2, 256, 256), probe


def solution(mesh):
    placed = (
        P(None, None, "ty", "tx"),
        P(),
        P("ty", "tx"),
        P("ty", "tx", None, None),
        P("ty", "tx", None, None, None),
    )
    return jax.shard_map(
        body,
        mesh=mesh,
        in_specs=placed,
        out_specs=(P(None, None, "ty", "tx"), P()),
        check_vma=False,
    )
```

```python
import functools

import jax
import jax.numpy as jnp
import ml_dtypes
import numpy as np
from jax import lax
from jax.experimental import pallas as pl
from jax.experimental.pallas import tpu as pltpu
from jax.sharding import PartitionSpec as P

PROBE = 256
MAXPOS = 5
ITERS = 2
bf = jnp.bfloat16
f32 = jnp.float32

chirp_rate = 0.5
object_rate = 0.5
probe_rate = 2.0


def tables():
    n = PROBE
    k = np.arange(n)
    four = np.exp(-2j * np.pi * ((k[:, None] * k[None, :]) % n) / n) / np.sqrt(n)
    c = (((k + n // 2) % n) - n // 2).astype(np.float64)
    prop = (np.conj(four) * np.exp(-1j * chirp_rate * np.pi * c * c / n)[None, :]) @ four
    out = []
    for mat in (four, prop):
        real, imag = mat.real, mat.imag
        for part in (real, imag - real, real + imag):
            part = part.astype(np.float32)
            high = part.astype(ml_dtypes.bfloat16)
            out += [high, (part - high.astype(np.float32)).astype(ml_dtypes.bfloat16)]
    return np.stack(out).reshape(2, 3, 2, n, n)


def split(x):
    high = x.astype(bf)
    return high, (x - high.astype(f32)).astype(bf)


def dot(a, b):
    return jnp.dot(a, b, preferred_element_type=f32)


def left(tab, which, j, x):
    high, low = split(x)
    mat = jnp.concatenate([tab[which, j, 0], tab[which, j, 0], tab[which, j, 1]], axis=1)
    return dot(mat, jnp.concatenate([high, low, high], axis=0))


def right(tab, which, j, x):
    high, low = split(x)
    mat = jnp.concatenate([tab[which, j, 0], tab[which, j, 0], tab[which, j, 1]], axis=0)
    return dot(jnp.concatenate([high, low, high], axis=1), mat)


def sandwich(tab, which, real, imag, mid):
    shared = left(tab, which, 0, real + imag)
    mid[1] = shared + left(tab, which, 1, real)
    mid[0] = shared - left(tab, which, 2, imag)
    real, imag = mid[0], mid[1]
    shared = right(tab, which, 0, real + imag)
    return shared - right(tab, which, 2, imag), shared + right(tab, which, 1, real)


NTY, NTX = 8, 16
MESH = pl.DeviceIdType.MESH
DIRS = [(dy, dx) for dy in (-1, 0, 1) for dx in (-1, 0, 1) if (dy, dx) != (0, 0)]
V = pl.BlockSpec(memory_space=pltpu.VMEM)


def half_lanes(shape):
    return lax.broadcasted_iota(jnp.int32, shape, len(shape) - 1) < 64


def pack(x, side):
    rows = x.shape[1] // 2
    first, second = x[:, :rows], x[:, rows:]
    low = half_lanes(first.shape)
    if side > 0:
        return jnp.where(low, pltpu.roll(first, 64, 2), second)
    return jnp.where(low, first, pltpu.roll(second, 64, 2))


def unpack(buf, side):
    turned = pltpu.roll(buf, 64, 2)
    pair = [turned, buf] if side > 0 else [buf, turned]
    return jnp.concatenate(pair, axis=1)


def keep_side(x, side):
    low = half_lanes(x.shape)
    return jnp.where(low, 0.0, x) if side > 0 else jnp.where(low, x, 0.0)


class Place:
    def __init__(self):
        self.ty, self.tx = lax.axis_index("ty"), lax.axis_index("tx")
        self.x_lo, self.y = self.ty // 4, lax.rem(self.ty, 4)
        self.z, self.core = self.tx // 4, lax.rem(self.tx, 2)
        self.x_hi = lax.rem(self.tx // 2, 2)
        self.x = self.x_hi * 2 + self.x_lo
        self.spot = self.y * 4 + self.z

    def neighbour(self, dy, dx):
        return (lax.rem(self.ty + dy + NTY, NTY), lax.rem(self.tx + dx + NTX, NTX))

    def sibling(self):
        return (self.ty, self.tx + 1 - 2 * self.core)

    def plane(self, k):
        y, z = lax.rem(self.y + k // 4, 4), lax.rem(self.z + lax.rem(k, 4), 4)
        return y * 4 + z, (self.x_lo * 4 + y, z * 4 + self.x_hi * 2 + self.core)

    def column(self, k):
        x = lax.rem(self.x + k, 4)
        return x, (lax.rem(x, 2) * 4 + self.y, self.z * 4 + (x // 2) * 2 + self.core)


def remote(src, dst, send, recv, device):
    return pltpu.make_async_remote_copy(
        src_ref=src, dst_ref=dst, send_sem=send, recv_sem=recv, device_id=device, device_id_type=MESH
    )


class Edges:
    def __init__(self, place, rows, cols, corners, sems):
        self.place, self.rows, self.cols, self.corners = place, rows, cols, corners
        self.send, self.recv = sems

    def slot(self, bufs, dy, dx):
        if dx == 0:
            return bufs[0].at[(dy + 1) // 2]
        if dy == 0:
            return bufs[1].at[(dx + 1) // 2]
        return bufs[2].at[(dy + 1) + (dx + 1) // 2]

    def out(self, dy, dx):
        return self.slot((self.rows[0], self.cols[0], self.corners[0]), dy, dx)

    def inc(self, dy, dx):
        return self.slot((self.rows[1], self.cols[1], self.corners[1]), dy, dx)

    def copy(self, dy, dx):
        i = DIRS.index((dy, dx))
        return remote(self.out(dy, dx), self.inc(dy, dx), self.send.at[i], self.recv.at[i], self.place.neighbour(dy, dx))


ORDER = [(0, 1), (0, -1), (1, 0), (-1, 0), (1, 1), (1, -1), (-1, 1), (-1, -1)]


def pack_halo(e, core):
    for dy, dx in ORDER:
        r0, r1 = {-1: (0, 64), 0: (0, 256), 1: (192, 256)}[dy]
        if dx == 0:
            for t in range(2):
                e.out(dy, dx)[:, t] = core(t, r0, r1)
        else:
            e.out(dy, dx)[...] = pack(core((dx + 1) // 2, r0, r1), dx)


def unpack_halo(e, ext):
    for dy, dx in ORDER:
        e.copy(dy, dx).wait_recv()
    for dy in (-1, 1):
        r0 = 320 if dy < 0 else 0
        for t in range(2):
            ext[:, t, r0 : r0 + 64] = e.inc(dy, 0)[:, t]
    for dy in (-1, 0, 1):
        r0, r1 = {-1: (320, 384), 0: (64, 320), 1: (0, 64)}[dy]
        left, right = unpack(e.inc(dy, -1)[...], -1), unpack(e.inc(dy, 1)[...], 1)
        ext[:, 2, r0:r1] = jnp.where(half_lanes(left.shape), left, right)


def pack_fold(e, g):
    for dy, dx in ORDER:
        r0, r1 = {-1: (0, 64), 0: (64, 320), 1: (320, 384)}[dy]
        if dx == 0:
            for t in range(2):
                e.out(dy, dx)[:, t] = g[:, t, r0:r1]
        else:
            e.out(dy, dx)[...] = pack(g[:, 2, r0:r1], -dx)


def fold(e, g, total):
    for dy, dx in ORDER:
        e.copy(dy, dx).wait_recv()
    for t in range(2):
        total[:, t] = g[:, t, 64:320]
    for dy, dx in ORDER:
        r0, r1 = {-1: (192, 256), 0: (0, 256), 1: (0, 64)}[dy]
        if dx == 0:
            for t in range(2):
                total[:, t, r0:r1] += e.inc(dy, dx)[:, t]
        else:
            t = (1 - dx) // 2
            total[:, t, r0:r1] += keep_side(unpack(e.inc(dy, dx)[...], -dx), -dx)


def start_all(e):
    for dy, dx in ORDER:
        e.copy(dy, dx).start()


def wait_sent(e):
    for dy, dx in ORDER:
        e.copy(dy, dx).wait_send()


class Summer:
    def __init__(self, place, gp, pair, ready, plane, cross, whole, sems):
        self.p, self.gp, self.pair, self.ready, self.pl = place, gp, pair, ready, plane
        self.cross, self.whole, self.sems = cross, whole, sems

    def pair_copy(self, j):
        return remote(self.gp.at[1 - self.p.core, j], self.pair.at[j], self.sems[0].at[j], self.sems[1].at[j], self.p.sibling())

    def plane_copy(self, k):
        j, device = self.p.plane(k)
        return j, remote(self.ready.at[j], self.pl.at[k], self.sems[2].at[k], self.sems[3].at[k], device)

    def cross_copy(self, k):
        x, device = self.p.column(k)
        return remote(self.cross.at[self.p.x], self.cross.at[self.p.x], self.sems[4].at[k], self.sems[5].at[k], device)

    def cross_wait(self, k):
        self.cross_copy(k).wait_recv()

    def spread_copy(self, k):
        j, device = self.p.plane(k)
        own = self.whole.at[self.p.core, self.p.spot]
        return remote(own, own, self.sems[6].at[k], self.sems[7].at[k], device)

    def forward_copy(self, k):
        j, _ = self.p.plane(self.back(k))
        own = self.whole.at[self.p.core, j]
        return remote(own, own, self.sems[8].at[k], self.sems[9].at[k], self.p.sibling())

    def back(self, k):
        return lax.rem(4 - k // 4, 4) * 4 + lax.rem(4 - lax.rem(k, 4), 4)

    def begin(self):
        lax.fori_loop(0, 16, lambda k, c: (self.pair_copy(self.p.plane(k)[0]).start(), c)[1], 0)

    def scatter(self):
        def step(k, c):
            j, copy = self.plane_copy(k)
            self.pair_copy(j).wait_recv()
            self.ready[j] = self.gp[self.p.core, j] + self.pair[j]
            copy.start()
            return c

        lax.fori_loop(1, 16, step, 0)
        me = self.p.spot
        self.pair_copy(me).wait_recv()
        self.ready[me] = self.gp[self.p.core, me] + self.pair[me]

    def across(self):
        total = self.ready[self.p.spot]

        def step(k, c):
            self.plane_copy(k)[1].wait_recv()
            return c + self.pl[k]

        total = lax.fori_loop(1, 16, step, total)
        self.cross[self.p.x] = total
        lax.fori_loop(1, 4, lambda k, c: (self.cross_copy(k).start(), c)[1], 0)

    def spread(self):
        lax.fori_loop(1, 4, lambda k, c: (self.cross_copy(k).wait_recv(), c)[1], 0)
        self.whole[self.p.core, self.p.spot] = (self.cross[0] + self.cross[1]) + (self.cross[2] + self.cross[3])
        lax.fori_loop(1, 16, lambda k, c: (self.spread_copy(k).start(), c)[1], 0)
        self.forward_copy(0).start()

    def forward(self):
        def step(k, c):
            self.spread_copy(k).wait_recv()
            self.forward_copy(k).start()
            return c

        lax.fori_loop(1, 16, step, 0)

    def finish(self):
        lax.fori_loop(0, 16, lambda k, c: (self.forward_copy(k).wait_recv(), c)[1], 0)

    def sent(self):
        def step(k, c):
            self.pair_copy(self.p.plane(k)[0]).wait_send()
            self.forward_copy(k).wait_send()
            return c

        lax.fori_loop(0, 16, step, 0)

        def more(k, c):
            self.plane_copy(k)[1].wait_send()
            self.spread_copy(k).wait_send()
            return c

        lax.fori_loop(1, 16, more, 0)
        lax.fori_loop(1, 4, lambda k, c: (self.cross_copy(k).wait_send(), c)[1], 0)


def greet(p, summing):
    barrier = pltpu.get_barrier_semaphore()

    def hello(device):
        pl.semaphore_signal(barrier, inc=1, device_id=device, device_id_type=MESH)

    for dy, dx in DIRS:
        hello(p.neighbour(dy, dx))
    count = 8
    if summing:
        hello(p.sibling())
        lax.fori_loop(1, 16, lambda k, c: (hello(p.plane(k)[1]), c)[1], 0)
        lax.fori_loop(1, 4, lambda k, c: (hello(p.column(k)[1]), c)[1], 0)
        count += 19
    return lambda: pl.semaphore_wait(barrier, count)


EXCHANGES = 8
SUMS = ITERS


def exchange(p, refs, i):
    rows, cols, corners, sems = [ref.at[i] for ref in refs]
    pair = lambda ref: (ref.at[0], ref.at[1])
    return Edges(p, pair(rows), pair(cols), pair(corners), pair(sems))


def shifts(off_ref, s):
    top, left_col = off_ref[s, 0], off_ref[s, 1]
    inner = left_col >= 64
    first = jnp.where(inner, 0, 2)
    second = jnp.where(inner, 1, 0)
    third = jnp.where(inner, 2, 1)
    return top, jnp.where(inner, left_col - 64, left_col + 64), (first, second, third)


def take_window(off_ref, s, ext, win):
    top, shift, tiles = shifts(off_ref, s)
    keep = lax.broadcasted_iota(jnp.int32, (256, 128), 1) < 128 - shift
    for p in range(2):
        a, b, c = [pltpu.roll(ext[p, t, pl.ds(top, 256), :], 128 - shift, 1) for t in tiles]
        win[s, p, :, 0:128] = jnp.where(keep, a, b)
        win[s, p, :, 128:256] = jnp.where(keep, b, c)


def add_window(off_ref, count_ref, s, pair, slide, acc):
    top, shift, (first, second, third) = shifts(off_ref, s)
    lane = lax.broadcasted_iota(jnp.int32, (256, 128), 1)
    before = lane < shift
    active = lane * 0 + s < count_ref[0]
    for p in range(2):
        a, b = [
            pltpu.roll(jnp.where(active, pair[p][:, t * 128 : t * 128 + 128], 0.0), shift, 1) for t in range(2)
        ]
        slide[p, 0, 128:384] = jnp.where(before, 0.0, a)
        slide[p, 1, 128:384] = jnp.where(before, a, b)
        slide[p, 2, 128:384] = jnp.where(before, b, 0.0)
    inner = first == 0
    source = (jnp.where(inner, 0, 1), jnp.where(inner, 1, 2), jnp.where(inner, 2, 0))
    for p in range(2):
        for t in range(3):
            acc[p, t] += slide[p, source[t], pl.ds(128 - top, 384), :]


def program_kernel(
    count_ref, off_ref, obj, probe_in, inten_hbm, tab_hbm, obj_out, probe_out,
    tab, inten, ext1, ext2, acc1, acc2, gp, slide, win1, win2, moved, back, mid, total, probe,
    rows, cols, corners, edge_sems, pair, made, plane, cross, whole, sum_sems, local_sems,
):
    p = Place()
    ready = greet(p, True)
    edges = (rows, cols, corners, edge_sems)
    tab_copy = pltpu.make_async_copy(tab_hbm, tab, local_sems.at[0])
    inten_copy = pltpu.make_async_copy(inten_hbm, inten, local_sems.at[1])
    tab_copy.start()
    inten_copy.start()
    halo1, halo2 = exchange(p, edges, 0), exchange(p, edges, 1)
    for k, e in enumerate((halo1, halo2)):
        pack_halo(e, lambda t, r0, r1: obj[2 * k : 2 * k + 2, r0:r1, t * 128 : t * 128 + 128])
    ready()
    start_all(halo1)
    start_all(halo2)
    for t in range(2):
        ext1[:, t, 64:320] = obj[0:2, :, t * 128 : t * 128 + 128]
        ext2[:, t, 64:320] = obj[2:4, :, t * 128 : t * 128 + 128]
    slide[...] = jnp.zeros_like(slide)
    probe[...] = probe_in[...]
    tab_copy.wait()
    inten_copy.wait()
    unpack_halo(halo1, ext1)

    for it in range(ITERS):
        last = it == ITERS - 1
        acc1[...] = jnp.zeros_like(acc1)
        acc2[...] = jnp.zeros_like(acc2)
        gp[...] = jnp.zeros_like(gp)

        def forward(s, carry):
            take_window(off_ref, s, ext1, win1)
            pr, pi, wr, wi = probe[0], probe[1], win1[s, 0], win1[s, 1]
            moved[s, 0], moved[s, 1] = sandwich(tab, 1, pr * wr - pi * wi, pr * wi + pi * wr, mid)
            return carry

        lax.fori_loop(0, MAXPOS, forward, 0)
        unpack_halo(halo2, ext2)

        def detector(s, carry):
            take_window(off_ref, s, ext2, win2)
            er = moved[s, 0] * win2[s, 0] - moved[s, 1] * win2[s, 1]
            ei = moved[s, 0] * win2[s, 1] + moved[s, 1] * win2[s, 0]
            fr, fi = sandwich(tab, 0, er, ei, mid)
            misfit = fr * fr + fi * fi - inten[s]
            cr, ci = sandwich(tab, 0, misfit * fr, -(misfit * fi), mid)
            back[s, 0] = win2[s, 0] * cr - win2[s, 1] * ci
            back[s, 1] = win2[s, 0] * ci + win2[s, 1] * cr
            g2 = (moved[s, 0] * cr - moved[s, 1] * ci, -(moved[s, 0] * ci + moved[s, 1] * cr))
            add_window(off_ref, count_ref, s, g2, slide, acc2)
            return carry

        lax.fori_loop(0, MAXPOS, detector, 0)
        fold2 = exchange(p, edges, 4 * it + 2)
        pack_fold(fold2, acc2)
        start_all(fold2)

        def adjoint(s, carry):
            wr, wi = sandwich(tab, 1, back[s, 0], back[s, 1], mid)
            g1 = (probe[0] * wr - probe[1] * wi, -(probe[0] * wi + probe[1] * wr))
            add_window(off_ref, count_ref, s, g1, slide, acc1)
            active = lax.broadcasted_iota(jnp.int32, (256, 128), 1) * 0 + s < count_ref[0]
            parts = (win1[s, 0] * wr - win1[s, 1] * wi, -(win1[s, 0] * wi + win1[s, 1] * wr))
            for h in range(2):
                for t in range(2):
                    part = jnp.where(active, parts[h][:, t * 128 : t * 128 + 128], 0.0)
                    gp[h, 8 * t : 8 * t + 8] += part.reshape(8, 32, 128)
            return carry

        lax.fori_loop(0, MAXPOS, adjoint, 0)
        s = Summer(p, gp, *[ref.at[it] for ref in (pair, made, plane, cross, whole)], [sum_sems.at[it, i] for i in range(10)])
        s.begin()
        fold1 = exchange(p, edges, 4 * it + 3)
        pack_fold(fold1, acc1)
        start_all(fold1)
        s.scatter()
        rate = step_size(probe)
        fold(fold2, acc2, total)
        if last:
            for t in range(2):
                obj_out[2:4, :, t * 128 : t * 128 + 128] = ext2[:, t, 64:320] - rate * total[:, t]
        else:
            for t in range(2):
                ext2[:, t, 64:320] -= rate * total[:, t]
        s.across()
        fold(fold1, acc1, total)
        if last:
            for t in range(2):
                obj_out[0:2, :, t * 128 : t * 128 + 128] = ext1[:, t, 64:320] - rate * total[:, t]
            s.spread()
        else:
            for t in range(2):
                ext1[:, t, 64:320] -= rate * total[:, t]
            halo1, halo2 = exchange(p, edges, 4), exchange(p, edges, 5)
            pack_halo(halo1, lambda t, r0, r1: ext1[:, t, 64 + r0 : 64 + r1])
            start_all(halo1)
            s.spread()
            pack_halo(halo2, lambda t, r0, r1: ext2[:, t, 64 + r0 : 64 + r1])
            start_all(halo2)
        s.forward()
        if not last:
            unpack_halo(halo1, ext1)
        s.finish()
        probe_update(probe, s.whole, probe_out if last else probe)
        s.sent()
    for i in range(EXCHANGES):
        wait_sent(exchange(p, edges, i))


def step_size(probe):
    power = probe[0] * probe[0] + probe[1] * probe[1]
    peak = jnp.max(power, axis=(0, 1), keepdims=True) + 1e-06
    return object_rate / peak


def probe_update(probe, whole, out):
    for h in range(2):
        for t in range(2):
            cols = slice(t * 128, t * 128 + 128)
            grad = whole[h, 8 * t : 8 * t + 8].reshape(256, 128)
            out[h, :, cols] = probe[h, :, cols] - (probe_rate / (NTY * NTX)) * grad


def run(count, off, obj, probe, inten, tab):
    smem = pl.BlockSpec(memory_space=pltpu.SMEM)
    anywhere = pl.BlockSpec(memory_space=pl.ANY)
    vm = pltpu.VMEM
    slots = vm((MAXPOS, 2, 256, 256), f32)
    return pl.pallas_call(
        program_kernel,
        out_shape=(jax.ShapeDtypeStruct((4, 256, 256), f32), jax.ShapeDtypeStruct((2, 256, 256), f32)),
        in_specs=[smem, smem, V, V, anywhere, anywhere],
        out_specs=(V, V),
        scratch_shapes=[
            vm((2, 3, 2, 256, 256), bf),
            vm((MAXPOS, 256, 256), f32),
            vm((2, 3, 384, 128), f32),
            vm((2, 3, 384, 128), f32),
            vm((2, 3, 384, 128), f32),
            vm((2, 3, 384, 128), f32),
            vm((2, 16, 32, 128), f32),
            vm((2, 3, 512, 128), f32),
            slots,
            slots,
            slots,
            slots,
            vm((2, 256, 256), f32),
            vm((2, 2, 256, 128), f32),
            vm((2, 256, 256), f32),
            vm((EXCHANGES, 2, 2, 2, 2, 64, 128), f32),
            vm((EXCHANGES, 2, 2, 2, 128, 128), f32),
            vm((EXCHANGES, 2, 4, 2, 32, 128), f32),
            pltpu.SemaphoreType.DMA((EXCHANGES, 2, 8)),
            vm((SUMS, 16, 32, 128), f32),
            vm((SUMS, 16, 32, 128), f32),
            vm((SUMS, 16, 32, 128), f32),
            vm((SUMS, 4, 32, 128), f32),
            vm((SUMS, 2, 16, 32, 128), f32),
            pltpu.SemaphoreType.DMA((SUMS, 10, 16)),
            pltpu.SemaphoreType.DMA((2,)),
        ],
        compiler_params=pltpu.CompilerParams(collective_id=0, has_side_effects=True, vmem_limit_bytes=58 << 20),
        name="iterations",
    )(count, off, obj, probe, inten, tab)


def body(object_slices, probe, position_count, offsets, intensities):
    obj, probe = run(
        position_count[0],
        offsets[0, 0],
        object_slices.reshape(4, 256, 256),
        probe,
        intensities[0, 0],
        jnp.asarray(tables()),
    )
    return obj.reshape(2, 2, 256, 256), probe


def solution(mesh):
    placed = (
        P(None, None, "ty", "tx"),
        P(),
        P("ty", "tx"),
        P("ty", "tx", None, None),
        P("ty", "tx", None, None, None),
    )
    return jax.shard_map(
        body,
        mesh=mesh,
        in_specs=placed,
        out_specs=(P(None, None, "ty", "tx"), P()),
        check_vma=False,
    )
```

```python
import functools

import jax
import jax.numpy as jnp
import ml_dtypes
import numpy as np
from jax import lax
from jax.experimental import pallas as pl
from jax.experimental.pallas import tpu as pltpu
from jax.sharding import PartitionSpec as P

PROBE = 256
MAXPOS = 5
ITERS = 2
bf = jnp.bfloat16
f32 = jnp.float32

chirp_rate = 0.5
object_rate = 0.5
probe_rate = 2.0


def tables():
    n = PROBE
    k = np.arange(n)
    four = np.exp(-2j * np.pi * ((k[:, None] * k[None, :]) % n) / n) / np.sqrt(n)
    c = (((k + n // 2) % n) - n // 2).astype(np.float64)
    prop = (np.conj(four) * np.exp(-1j * chirp_rate * np.pi * c * c / n)[None, :]) @ four
    out = []
    for mat in (four, prop):
        real, imag = mat.real, mat.imag
        for part in (real, imag - real, real + imag):
            part = part.astype(np.float32)
            high = part.astype(ml_dtypes.bfloat16)
            out += [high, (part - high.astype(np.float32)).astype(ml_dtypes.bfloat16)]
    return np.stack(out).reshape(2, 3, 2, n, n)


def split(x):
    high = x.astype(bf)
    return high, (x - high.astype(f32)).astype(bf)


def dot(a, b):
    return jnp.dot(a, b, preferred_element_type=f32)


def left(tab, which, j, x):
    high, low = split(x)
    mat = jnp.concatenate([tab[which, j, 0], tab[which, j, 0], tab[which, j, 1]], axis=1)
    return dot(mat, jnp.concatenate([high, low, high], axis=0))


def right(tab, which, j, x):
    high, low = split(x)
    mat = jnp.concatenate([tab[which, j, 0], tab[which, j, 0], tab[which, j, 1]], axis=0)
    return dot(jnp.concatenate([high, low, high], axis=1), mat)


def sandwich(tab, which, real, imag, mid):
    shared = left(tab, which, 0, real + imag)
    mid[1] = shared + left(tab, which, 1, real)
    mid[0] = shared - left(tab, which, 2, imag)
    real, imag = mid[0], mid[1]
    shared = right(tab, which, 0, real + imag)
    return shared - right(tab, which, 2, imag), shared + right(tab, which, 1, real)


NTY, NTX = 8, 16
MESH = pl.DeviceIdType.MESH
DIRS = [(dy, dx) for dy in (-1, 0, 1) for dx in (-1, 0, 1) if (dy, dx) != (0, 0)]
V = pl.BlockSpec(memory_space=pltpu.VMEM)


def half_lanes(shape):
    return lax.broadcasted_iota(jnp.int32, shape, len(shape) - 1) < 64


def pack(x, side):
    rows = x.shape[1] // 2
    first, second = x[:, :rows], x[:, rows:]
    low = half_lanes(first.shape)
    if side > 0:
        return jnp.where(low, pltpu.roll(first, 64, 2), second)
    return jnp.where(low, first, pltpu.roll(second, 64, 2))


def unpack(buf, side):
    turned = pltpu.roll(buf, 64, 2)
    pair = [turned, buf] if side > 0 else [buf, turned]
    return jnp.concatenate(pair, axis=1)


def keep_side(x, side):
    low = half_lanes(x.shape)
    return jnp.where(low, 0.0, x) if side > 0 else jnp.where(low, x, 0.0)


class Place:
    def __init__(self):
        self.ty, self.tx = lax.axis_index("ty"), lax.axis_index("tx")
        self.x_lo, self.y = self.ty // 4, lax.rem(self.ty, 4)
        self.z, self.core = self.tx // 4, lax.rem(self.tx, 2)
        self.x_hi = lax.rem(self.tx // 2, 2)
        self.x = self.x_hi * 2 + self.x_lo

    def neighbour(self, dy, dx):
        return (lax.rem(self.ty + dy + NTY, NTY), lax.rem(self.tx + dx + NTX, NTX))

    def sibling(self):
        return (self.ty, self.tx + 1 - 2 * self.core)

    def turn(self, axis, k):
        x, y, z = self.x, self.y, self.z
        if axis == "x":
            x = lax.rem(x + k, 4)
        elif axis == "y":
            y = lax.rem(y + k, 4)
        else:
            z = lax.rem(z + k, 4)
        spot = {"x": x, "y": y, "z": z}[axis]
        return spot, (lax.rem(x, 2) * 4 + y, z * 4 + (x // 2) * 2 + self.core)


def remote(src, dst, send, recv, device):
    return pltpu.make_async_remote_copy(
        src_ref=src, dst_ref=dst, send_sem=send, recv_sem=recv, device_id=device, device_id_type=MESH
    )


class Edges:
    def __init__(self, place, rows, cols, corners, sems):
        self.place, self.rows, self.cols, self.corners = place, rows, cols, corners
        self.send, self.recv = sems

    def slot(self, bufs, dy, dx):
        if dx == 0:
            return bufs[0].at[(dy + 1) // 2]
        if dy == 0:
            return bufs[1].at[(dx + 1) // 2]
        return bufs[2].at[(dy + 1) + (dx + 1) // 2]

    def out(self, dy, dx):
        return self.slot((self.rows[0], self.cols[0], self.corners[0]), dy, dx)

    def inc(self, dy, dx):
        return self.slot((self.rows[1], self.cols[1], self.corners[1]), dy, dx)

    def copy(self, dy, dx):
        i = DIRS.index((dy, dx))
        return remote(self.out(dy, dx), self.inc(dy, dx), self.send.at[i], self.recv.at[i], self.place.neighbour(dy, dx))


ORDER = [(0, 1), (0, -1), (1, 0), (-1, 0), (1, 1), (1, -1), (-1, 1), (-1, -1)]


def pack_halo(e, core):
    for dy, dx in ORDER:
        r0, r1 = {-1: (0, 64), 0: (0, 256), 1: (192, 256)}[dy]
        if dx == 0:
            for t in range(2):
                e.out(dy, dx)[:, t] = core(t, r0, r1)
        else:
            e.out(dy, dx)[...] = pack(core((dx + 1) // 2, r0, r1), dx)


def unpack_halo(e, ext):
    for dy, dx in ORDER:
        e.copy(dy, dx).wait_recv()
    for dy in (-1, 1):
        r0 = 320 if dy < 0 else 0
        for t in range(2):
            ext[:, t, r0 : r0 + 64] = e.inc(dy, 0)[:, t]
    for dy in (-1, 0, 1):
        r0, r1 = {-1: (320, 384), 0: (64, 320), 1: (0, 64)}[dy]
        left, right = unpack(e.inc(dy, -1)[...], -1), unpack(e.inc(dy, 1)[...], 1)
        ext[:, 2, r0:r1] = jnp.where(half_lanes(left.shape), left, right)


def pack_fold(e, g):
    for dy, dx in ORDER:
        r0, r1 = {-1: (0, 64), 0: (64, 320), 1: (320, 384)}[dy]
        if dx == 0:
            for t in range(2):
                e.out(dy, dx)[:, t] = g[:, t, r0:r1]
        else:
            e.out(dy, dx)[...] = pack(g[:, 2, r0:r1], -dx)


def fold(e, g, total):
    for dy, dx in ORDER:
        e.copy(dy, dx).wait_recv()
    for t in range(2):
        total[:, t] = g[:, t, 64:320]
    for dy, dx in ORDER:
        r0, r1 = {-1: (192, 256), 0: (0, 256), 1: (0, 64)}[dy]
        if dx == 0:
            for t in range(2):
                total[:, t, r0:r1] += e.inc(dy, dx)[:, t]
        else:
            t = (1 - dx) // 2
            total[:, t, r0:r1] += keep_side(unpack(e.inc(dy, dx)[...], -dx), -dx)


def start_all(e):
    for dy, dx in ORDER:
        e.copy(dy, dx).start()


def wait_sent(e):
    for dy, dx in ORDER:
        e.copy(dy, dx).wait_send()


class Summer:
    def __init__(self, place, gp, bufs, sems):
        self.p, self.gp = place, gp
        self.pair, self.made, self.zin, self.ysum, self.yin, self.cross, self.whole = bufs
        self.send, self.recv = sems
        self.zs = [place.turn("z", k) for k in range(4)]
        self.ys = [place.turn("y", k) for k in range(4)]
        self.xs = [place.turn("x", k) for k in range(4)]

    def copy(self, phase, k, src, dst, device):
        return remote(src, dst, self.send.at[phase, k], self.recv.at[phase, k], device)

    def pair_copy(self, k):
        z = self.zs[k][0]
        return self.copy(0, k, self.gp.at[1 - self.p.core, z], self.pair.at[z], self.p.sibling())

    def z_copy(self, k):
        z, device = self.zs[k]
        return self.copy(1, k, self.made.at[k], self.zin.at[k], device)

    def y_copy(self, k):
        y, device = self.ys[k]
        return self.copy(2, k, self.ysum.at[y], self.yin.at[k], device)

    def x_copy(self, k):
        own = self.cross.at[self.p.x]
        return self.copy(3, k, own, own, self.xs[k][1])

    def y_back(self, k):
        own = self.whole.at[self.p.core, self.p.z, self.p.y]
        return self.copy(4, k, own, own, self.ys[k][1])

    def z_back(self, k):
        own = self.whole.at[self.p.core, self.p.z]
        return self.copy(5, k, own, own, self.zs[k][1])

    def forward_copy(self, k):
        own = self.whole.at[self.p.core, self.zs[(4 - k) % 4][0]]
        return self.copy(6, k, own, own, self.p.sibling())

    def begin(self):
        for k in (1, 2, 3, 0):
            self.pair_copy(k).start()

    def over_z(self):
        for k in (1, 2, 3, 0):
            z = self.zs[k][0]
            self.pair_copy(k).wait_recv()
            self.made[k] = self.gp[self.p.core, z] + self.pair[z]
            if k:
                self.z_copy(k).start()

    def over_y(self):
        for k in (1, 2, 3):
            self.z_copy(k).wait_recv()
        self.ysum[...] = (self.made[0] + self.zin[1]) + (self.zin[2] + self.zin[3])
        for k in (1, 2, 3):
            self.y_copy(k).start()

    def over_x(self):
        for k in (1, 2, 3):
            self.y_copy(k).wait_recv()
        self.cross[self.p.x] = (self.ysum[self.p.y] + self.yin[1]) + (self.yin[2] + self.yin[3])
        for k in (1, 2, 3):
            self.x_copy(k).start()

    def gather_y(self):
        for k in (1, 2, 3):
            self.x_copy(k).wait_recv()
        own = (self.cross[0] + self.cross[1]) + (self.cross[2] + self.cross[3])
        self.whole[self.p.core, self.p.z, self.p.y] = own
        for k in (1, 2, 3):
            self.y_back(k).start()

    def gather_z(self):
        for k in (1, 2, 3):
            self.y_back(k).wait_recv()
        for k in (1, 2, 3):
            self.z_back(k).start()
        self.forward_copy(0).start()

    def gather_pair(self):
        for k in (1, 2, 3):
            self.z_back(k).wait_recv()
            self.forward_copy(k).start()

    def finish(self):
        for k in range(4):
            self.forward_copy(k).wait_recv()

    def sent(self):
        for k in range(4):
            self.pair_copy(k).wait_send()
            self.forward_copy(k).wait_send()
        for k in (1, 2, 3):
            for copy in (self.z_copy, self.y_copy, self.x_copy, self.y_back, self.z_back):
                copy(k).wait_send()


def greet(p):
    barrier = pltpu.get_barrier_semaphore()
    devices = [p.neighbour(dy, dx) for dy, dx in DIRS] + [p.sibling()]
    devices += [p.turn(axis, k)[1] for axis in "xyz" for k in (1, 2, 3)]
    for device in devices:
        pl.semaphore_signal(barrier, inc=1, device_id=device, device_id_type=MESH)
    return lambda: pl.semaphore_wait(barrier, len(devices))


EXCHANGES = 8
SUMS = ITERS


def exchange(p, refs, i):
    rows, cols, corners, sems = [ref.at[i] for ref in refs]
    pair = lambda ref: (ref.at[0], ref.at[1])
    return Edges(p, pair(rows), pair(cols), pair(corners), pair(sems))


def shifts(off_ref, s):
    top, left_col = off_ref[0, s], off_ref[1, s]
    inner = left_col >= 64
    first = jnp.where(inner, 0, 2)
    second = jnp.where(inner, 1, 0)
    third = jnp.where(inner, 2, 1)
    return top, jnp.where(inner, left_col - 64, left_col + 64), (first, second, third)


def take_window(off_ref, s, ext, win):
    top, shift, tiles = shifts(off_ref, s)
    keep = lax.broadcasted_iota(jnp.int32, (256, 128), 1) < 128 - shift
    for p in range(2):
        a, b, c = [pltpu.roll(ext[p, t, pl.ds(top, 256), :], 128 - shift, 1) for t in tiles]
        win[s, p, :, 0:128] = jnp.where(keep, a, b)
        win[s, p, :, 128:256] = jnp.where(keep, b, c)


def add_window(off_ref, count_ref, s, pair, slide, acc):
    top, shift, (first, second, third) = shifts(off_ref, s)
    lane = lax.broadcasted_iota(jnp.int32, (256, 128), 1)
    before = lane < shift
    active = lane * 0 + s < count_ref[0, 0]
    for p in range(2):
        a, b = [
            pltpu.roll(jnp.where(active, pair[p][:, t * 128 : t * 128 + 128], 0.0), shift, 1) for t in range(2)
        ]
        slide[p, 0, 128:384] = jnp.where(before, 0.0, a)
        slide[p, 1, 128:384] = jnp.where(before, a, b)
        slide[p, 2, 128:384] = jnp.where(before, b, 0.0)
    inner = first == 0
    source = (jnp.where(inner, 0, 1), jnp.where(inner, 1, 2), jnp.where(inner, 2, 0))
    for p in range(2):
        for t in range(3):
            acc[p, t] += slide[p, source[t], pl.ds(128 - top, 384), :]


def each_slot(fn):
    for s in range(MAXPOS):
        fn(s)


def program_kernel(
    count_ref, off_ref, obj, probe_in, inten_hbm, tab_hbm, obj_out, probe_out,
    tab, inten, ext1, ext2, acc1, acc2, gp, slides, win1, win2, moved, back, mids, total, probe,
    rows, cols, corners, edge_sems, pair, made, zin, ysum, yin, cross, whole, sum_sems, local_sems,
):
    p = Place()
    ready = greet(p)
    edges = (rows, cols, corners, edge_sems)
    tab_copy = pltpu.make_async_copy(tab_hbm, tab, local_sems.at[0])
    inten_copy = pltpu.make_async_copy(inten_hbm, inten, local_sems.at[1])
    tab_copy.start()
    inten_copy.start()
    halo1, halo2 = exchange(p, edges, 0), exchange(p, edges, 1)
    pack_halo(halo1, lambda t, r0, r1: obj[0:2, r0:r1, t * 128 : t * 128 + 128])
    ready()
    start_all(halo1)
    pack_halo(halo2, lambda t, r0, r1: obj[2:4, r0:r1, t * 128 : t * 128 + 128])
    start_all(halo2)
    for t in range(2):
        ext1[:, t, 64:320] = obj[0:2, :, t * 128 : t * 128 + 128]
        ext2[:, t, 64:320] = obj[2:4, :, t * 128 : t * 128 + 128]
    slides[...] = jnp.zeros_like(slides)
    obj_out[...] = jnp.zeros_like(obj_out)
    probe_out[...] = jnp.zeros_like(probe_out)
    probe[...] = probe_in[...]
    tab_copy.wait()
    inten_copy.wait()
    unpack_halo(halo1, ext1)

    def iteration(it, carry):
        acc1[...] = jnp.zeros_like(acc1)
        acc2[...] = jnp.zeros_like(acc2)
        gp[...] = jnp.zeros_like(gp)

        def forward(s):
            take_window(off_ref, s, ext1, win1)
            pr, pi, wr, wi = probe[0], probe[1], win1[s, 0], win1[s, 1]
            moved[s, 0], moved[s, 1] = sandwich(tab, 1, pr * wr - pi * wi, pr * wi + pi * wr, mids.at[s])

        def detector(s):
            take_window(off_ref, s, ext2, win2)
            er = moved[s, 0] * win2[s, 0] - moved[s, 1] * win2[s, 1]
            ei = moved[s, 0] * win2[s, 1] + moved[s, 1] * win2[s, 0]
            fr, fi = sandwich(tab, 0, er, ei, mids.at[s])
            misfit = fr * fr + fi * fi - inten[s]
            cr, ci = sandwich(tab, 0, misfit * fr, -(misfit * fi), mids.at[s])
            back[s, 0] = win2[s, 0] * cr - win2[s, 1] * ci
            back[s, 1] = win2[s, 0] * ci + win2[s, 1] * cr
            g2 = (moved[s, 0] * cr - moved[s, 1] * ci, -(moved[s, 0] * ci + moved[s, 1] * cr))
            add_window(off_ref, count_ref, s, g2, slides.at[s % 2], acc2)

        def adjoint(s):
            wr, wi = sandwich(tab, 1, back[s, 0], back[s, 1], mids.at[s])
            g1 = (probe[0] * wr - probe[1] * wi, -(probe[0] * wi + probe[1] * wr))
            add_window(off_ref, count_ref, s, g1, slides.at[s % 2], acc1)
            active = lax.broadcasted_iota(jnp.int32, (256, 128), 1) * 0 + s < count_ref[0, 0]
            parts = (win1[s, 0] * wr - win1[s, 1] * wi, -(win1[s, 0] * wi + win1[s, 1] * wr))
            for h in range(2):
                for t in range(2):
                    part = jnp.where(active, parts[h][:, t * 128 : t * 128 + 128], 0.0)
                    gp[h, 2 * t : 2 * t + 2] += part.reshape(2, 4, 32, 128)

        each_slot(forward)
        unpack_halo(exchange(p, edges, 4 * it + 1), ext2)
        each_slot(detector)
        fold2, fold1 = exchange(p, edges, 4 * it + 2), exchange(p, edges, 4 * it + 3)
        pack_fold(fold2, acc2)
        start_all(fold2)
        each_slot(adjoint)

        bufs = [ref.at[it] for ref in (pair, made, zin, ysum, yin, cross, whole)]
        s = Summer(p, gp, bufs, (sum_sems.at[it, 0], sum_sems.at[it, 1]))
        s.begin()
        pack_fold(fold1, acc1)
        start_all(fold1)
        s.over_z()
        rate = step_size(probe)

        def update(e, acc, ext, first):
            fold(e, acc, total)
            for t in range(2):
                change = rate * total[:, t]
                ext[:, t, 64:320] -= change
                obj_out[first : first + 2, :, t * 128 : t * 128 + 128] += change

        update(fold2, acc2, ext2, 2)
        s.over_y()
        s.over_x()
        update(fold1, acc1, ext1, 0)

        @pl.when(it == 0)
        def _():
            halo = exchange(p, edges, 4)
            pack_halo(halo, lambda t, r0, r1: ext1[:, t, 64 + r0 : 64 + r1])
            start_all(halo)

        s.gather_y()

        @pl.when(it == 0)
        def _():
            halo = exchange(p, edges, 5)
            pack_halo(halo, lambda t, r0, r1: ext2[:, t, 64 + r0 : 64 + r1])
            start_all(halo)

        s.gather_z()
        s.gather_pair()

        @pl.when(it == 0)
        def _():
            unpack_halo(exchange(p, edges, 4), ext1)

        s.finish()
        for h in range(2):
            for t in range(2):
                lanes = slice(t * 128, t * 128 + 128)
                change = (probe_rate / (NTY * NTX)) * s.whole[h, 2 * t : 2 * t + 2].reshape(256, 128)
                probe[h, :, lanes] -= change
                probe_out[h, :, lanes] += change
        s.sent()
        return carry

    lax.fori_loop(0, ITERS, iteration, 0)
    for i in range(EXCHANGES):
        wait_sent(exchange(p, edges, i))


def step_size(probe):
    power = probe[0] * probe[0] + probe[1] * probe[1]
    peak = jnp.max(power, axis=(0, 1), keepdims=True) + 1e-06
    return object_rate / peak


def run(count, off, obj, probe, inten, tab):
    smem = pl.BlockSpec(memory_space=pltpu.SMEM)
    anywhere = pl.BlockSpec(memory_space=pl.ANY)
    vm = pltpu.VMEM
    slots = vm((MAXPOS, 2, 256, 256), f32)
    return pl.pallas_call(
        program_kernel,
        out_shape=(jax.ShapeDtypeStruct((4, 256, 256), f32), jax.ShapeDtypeStruct((2, 256, 256), f32)),
        in_specs=[smem, smem, V, V, anywhere, anywhere],
        out_specs=(V, V),
        scratch_shapes=[
            vm((2, 3, 2, 256, 256), bf),
            vm((MAXPOS, 256, 256), f32),
            vm((2, 3, 384, 128), f32),
            vm((2, 3, 384, 128), f32),
            vm((2, 3, 384, 128), f32),
            vm((2, 3, 384, 128), f32),
            vm((2, 4, 4, 32, 128), f32),
            vm((2, 2, 3, 512, 128), f32),
            slots,
            slots,
            slots,
            slots,
            slots,
            vm((2, 2, 256, 128), f32),
            vm((2, 256, 256), f32),
            vm((EXCHANGES, 2, 2, 2, 2, 64, 128), f32),
            vm((EXCHANGES, 2, 2, 2, 128, 128), f32),
            vm((EXCHANGES, 2, 4, 2, 32, 128), f32),
            pltpu.SemaphoreType.DMA((EXCHANGES, 2, 8)),
            vm((SUMS, 4, 4, 32, 128), f32),
            vm((SUMS, 4, 4, 32, 128), f32),
            vm((SUMS, 4, 4, 32, 128), f32),
            vm((SUMS, 4, 32, 128), f32),
            vm((SUMS, 4, 32, 128), f32),
            vm((SUMS, 4, 32, 128), f32),
            vm((SUMS, 2, 4, 4, 32, 128), f32),
            pltpu.SemaphoreType.DMA((SUMS, 2, 7, 4)),
            pltpu.SemaphoreType.DMA((2,)),
        ],
        compiler_params=pltpu.CompilerParams(collective_id=0, has_side_effects=True, vmem_limit_bytes=50 << 20),
        name="iterations",
    )(count, off, obj, probe, inten, tab)


def body(object_slices, probe, position_count, offsets, intensities):
    obj_change, probe_change = run(
        position_count,
        offsets[0, 0].T,
        object_slices.reshape(4, 256, 256),
        probe,
        intensities[0, 0],
        jnp.asarray(tables()),
    )
    return object_slices - obj_change.reshape(2, 2, 256, 256), probe - probe_change


def solution(mesh):
    placed = (
        P(None, None, "ty", "tx"),
        P(),
        P("ty", "tx"),
        P("ty", "tx", None, None),
        P("ty", "tx", None, None, None),
    )
    return jax.shard_map(
        body,
        mesh=mesh,
        in_specs=placed,
        out_specs=(P(None, None, "ty", "tx"), P()),
        check_vma=False,
    )
```

```python
import functools

import jax
import jax.numpy as jnp
import ml_dtypes
import numpy as np
from jax import lax
from jax.experimental import pallas as pl
from jax.experimental.pallas import tpu as pltpu
from jax.sharding import PartitionSpec as P

PROBE = 256
MAXPOS = 5
ITERS = 2
bf = jnp.bfloat16
f32 = jnp.float32

chirp_rate = 0.5
object_rate = 0.5
probe_rate = 2.0


def tables():
    n = PROBE
    k = np.arange(n)
    angle = 2 * np.pi * ((k[:, None] * k[None, :]) % n) / n
    four = np.exp(-1j * angle) / np.sqrt(n)
    c = (((k + n // 2) % n) - n // 2).astype(np.float64)
    prop = (np.conj(four) * np.exp(-1j * chirp_rate * np.pi * c * c / n)[None, :]) @ four
    order = np.concatenate([k[: n // 2], [n // 2], k[: n // 2 : -1]])
    hartley = ((np.cos(angle) + np.sin(angle)) / np.sqrt(2 * n))[order]
    swap = np.eye(n)[order]
    out = []
    for part in (prop.real, prop.imag - prop.real, prop.real + prop.imag, hartley, hartley.T):
        part = part.astype(np.float32)
        high = part.astype(ml_dtypes.bfloat16)
        out.append(np.stack([high, (part - high.astype(np.float32)).astype(ml_dtypes.bfloat16)]))
    out.append(np.stack([swap, swap.T]).astype(ml_dtypes.bfloat16))
    return np.stack(out)


def split(x):
    high = x.astype(bf)
    return high, (x - high.astype(f32)).astype(bf)


def dot(a, b):
    return jnp.dot(a, b, preferred_element_type=f32)


def left(tab, j, x):
    high, low = split(x)
    mat = jnp.concatenate([tab[j, 0], tab[j, 0], tab[j, 1]], axis=1)
    return dot(mat, jnp.concatenate([high, low, high], axis=0))


def right(tab, j, x):
    high, low = split(x)
    mat = jnp.concatenate([tab[j, 0], tab[j, 0], tab[j, 1]], axis=0)
    return dot(jnp.concatenate([high, low, high], axis=1), mat)


def propagate(tab, real, imag, mid):
    shared = left(tab, 0, real + imag)
    mid[1] = shared + left(tab, 1, real)
    mid[0] = shared - left(tab, 2, imag)
    real, imag = mid[0], mid[1]
    shared = right(tab, 0, real + imag)
    return shared - right(tab, 2, imag), shared + right(tab, 1, real)


def hartley(tab, j, real, imag, mid):
    mid[0], mid[1] = left(tab, j, real), left(tab, j, imag)
    return right(tab, 7 - j, mid[0]), right(tab, 7 - j, mid[1])


def mirror_rows(z):
    top, bottom = z[:128], z[128:]
    first = lax.broadcasted_iota(jnp.int32, (8, 256), 0) == 0
    new_top = jnp.where(first, top[:8], bottom[:8])
    new_bottom = jnp.where(first, bottom[:8], top[:8])
    return jnp.concatenate([new_top, bottom[8:], new_bottom, top[8:]], axis=0)


def mirror_columns(z):
    near, far = z[:, :128], z[:, 128:]
    first = lax.broadcasted_iota(jnp.int32, (256, 128), 1) == 0
    return jnp.concatenate([jnp.where(first, near, far), jnp.where(first, far, near)], axis=1)


def combine(real, imag):
    pairs = []
    for z in (real, imag):
        across = mirror_columns(z)
        pairs.append((mirror_rows(z) + across, z - mirror_rows(across)))
    (even_r, odd_r), (even_i, odd_i) = pairs
    return even_r + odd_i, even_i - odd_r


def into_paired_order(tab, x):
    for side in range(2):
        high, low = split(x)
        rest = (x - high.astype(f32) - low.astype(f32)).astype(bf)
        if side == 0:
            x = dot(tab[5, 0], high) + dot(tab[5, 0], low) + dot(tab[5, 0], rest)
        else:
            x = dot(high, tab[5, 1]) + dot(low, tab[5, 1]) + dot(rest, tab[5, 1])
    return x


NTY, NTX = 8, 16
MESH = pl.DeviceIdType.MESH
DIRS = [(dy, dx) for dy in (-1, 0, 1) for dx in (-1, 0, 1) if (dy, dx) != (0, 0)]
V = pl.BlockSpec(memory_space=pltpu.VMEM)


def half_lanes(shape):
    return lax.broadcasted_iota(jnp.int32, shape, len(shape) - 1) < 64


def pack(x, side):
    rows = x.shape[1] // 2
    first, second = x[:, :rows], x[:, rows:]
    low = half_lanes(first.shape)
    if side > 0:
        return jnp.where(low, pltpu.roll(first, 64, 2), second)
    return jnp.where(low, first, pltpu.roll(second, 64, 2))


def unpack(buf, side):
    turned = pltpu.roll(buf, 64, 2)
    pair = [turned, buf] if side > 0 else [buf, turned]
    return jnp.concatenate(pair, axis=1)


def keep_side(x, side):
    low = half_lanes(x.shape)
    return jnp.where(low, 0.0, x) if side > 0 else jnp.where(low, x, 0.0)


class Place:
    def __init__(self):
        self.ty, self.tx = lax.axis_index("ty"), lax.axis_index("tx")
        self.x_lo, self.y = self.ty // 4, lax.rem(self.ty, 4)
        self.z, self.core = self.tx // 4, lax.rem(self.tx, 2)
        self.x_hi = lax.rem(self.tx // 2, 2)
        self.x = self.x_hi * 2 + self.x_lo

    def neighbour(self, dy, dx):
        return (lax.rem(self.ty + dy + NTY, NTY), lax.rem(self.tx + dx + NTX, NTX))

    def sibling(self):
        return (self.ty, self.tx + 1 - 2 * self.core)

    def turn(self, axis, k):
        x, y, z = self.x, self.y, self.z
        if axis == "x":
            x = lax.rem(x + k, 4)
        elif axis == "y":
            y = lax.rem(y + k, 4)
        else:
            z = lax.rem(z + k, 4)
        spot = {"x": x, "y": y, "z": z}[axis]
        return spot, (lax.rem(x, 2) * 4 + y, z * 4 + (x // 2) * 2 + self.core)


def remote(src, dst, send, recv, device):
    return pltpu.make_async_remote_copy(
        src_ref=src, dst_ref=dst, send_sem=send, recv_sem=recv, device_id=device, device_id_type=MESH
    )


class Edges:
    def __init__(self, place, rows, cols, corners, sems):
        self.place, self.rows, self.cols, self.corners = place, rows, cols, corners
        self.send, self.recv = sems

    def slot(self, bufs, dy, dx):
        if dx == 0:
            return bufs[0].at[(dy + 1) // 2]
        if dy == 0:
            return bufs[1].at[(dx + 1) // 2]
        return bufs[2].at[(dy + 1) + (dx + 1) // 2]

    def out(self, dy, dx):
        return self.slot((self.rows[0], self.cols[0], self.corners[0]), dy, dx)

    def inc(self, dy, dx):
        return self.slot((self.rows[1], self.cols[1], self.corners[1]), dy, dx)

    def copy(self, dy, dx):
        i = DIRS.index((dy, dx))
        return remote(self.out(dy, dx), self.inc(dy, dx), self.send.at[i], self.recv.at[i], self.place.neighbour(dy, dx))


ORDER = [(1, 1), (1, -1), (-1, 1), (-1, -1), (0, 1), (0, -1), (1, 0), (-1, 0)]


def send_halo(e, core, ready=None):
    for dy, dx in ORDER:
        r0, r1 = {-1: (0, 64), 0: (0, 256), 1: (192, 256)}[dy]
        if dx == 0:
            for t in range(2):
                e.out(dy, dx)[:, t] = core(t, r0, r1)
        else:
            e.out(dy, dx)[...] = pack(core((dx + 1) // 2, r0, r1), dx)
        if ready is None:
            e.copy(dy, dx).start()
    if ready is not None:
        ready()
        for dy, dx in ORDER:
            e.copy(dy, dx).start()


def unpack_halo(e, ext):
    for dy in (-1, 1):
        e.copy(dy, 0).wait_recv()
        r0 = 320 if dy < 0 else 0
        for t in range(2):
            ext[:, t, r0 : r0 + 64] = e.inc(dy, 0)[:, t]
    for dy in (0, -1, 1):
        e.copy(dy, -1).wait_recv()
        e.copy(dy, 1).wait_recv()
        r0, r1 = {-1: (320, 384), 0: (64, 320), 1: (0, 64)}[dy]
        left, right = unpack(e.inc(dy, -1)[...], -1), unpack(e.inc(dy, 1)[...], 1)
        ext[:, 2, r0:r1] = jnp.where(half_lanes(left.shape), left, right)


def send_fold(e, g):
    for dy, dx in ORDER:
        r0, r1 = {-1: (0, 64), 0: (64, 320), 1: (320, 384)}[dy]
        if dx == 0:
            for t in range(2):
                e.out(dy, dx)[:, t] = g[:, t, r0:r1]
        else:
            e.out(dy, dx)[...] = pack(g[:, 2, r0:r1], -dx)
        e.copy(dy, dx).start()


def step_down(ext, t, r0, r1, change):
    ext[:, t, 64 + r0 : 64 + r1] -= change


def descend_own(g, ext, rate):
    for t in range(2):
        step_down(ext, t, 0, 256, rate * g[:, t, 64:320])


def descend(e, ext, rate):
    for dy, dx in ORDER[4:] + ORDER[:4]:
        e.copy(dy, dx).wait_recv()
        r0, r1 = {-1: (192, 256), 0: (0, 256), 1: (0, 64)}[dy]
        if dx == 0:
            for t in range(2):
                step_down(ext, t, r0, r1, rate * e.inc(dy, dx)[:, t])
        else:
            values = keep_side(unpack(e.inc(dy, dx)[...], -dx), -dx)
            step_down(ext, (1 - dx) // 2, r0, r1, rate * values)


def wait_sent(e):
    for dy, dx in ORDER:
        e.copy(dy, dx).wait_send()


class Summer:
    def __init__(self, place, gp, bufs, sems):
        self.p, self.gp = place, gp
        self.pair, self.made, self.parts, self.cross, self.whole = bufs
        self.send, self.recv = sems
        self.zs = [place.turn("z", k)[0] for k in range(4)]
        self.ys = [place.turn("y", k)[0] for k in range(4)]
        self.xs = [place.turn("x", k)[1] for k in range(4)]

    def copy(self, i, src, dst, device):
        return remote(src, dst, self.send.at[i], self.recv.at[i], device)

    def device(self, k, j):
        return (self.p.x_lo * 4 + self.ys[j], self.zs[k] * 4 + self.p.x_hi * 2 + self.p.core)

    def pair_copy(self, k):
        z = self.zs[k]
        return self.copy(k, self.gp.at[1 - self.p.core, z], self.pair.at[z], self.p.sibling())

    def plane_copy(self, k, j):
        return self.copy(8 + 4 * k + j, self.made.at[k, self.ys[j]], self.parts.at[k, j], self.device(k, j))

    def x_copy(self, k):
        own = self.cross.at[self.p.x]
        return self.copy(40 + k, own, own, self.xs[k])

    def back_copy(self, k, j):
        own = self.whole.at[self.p.core, self.p.z, self.p.y]
        return self.copy(24 + 4 * k + j, own, own, self.device(k, j))

    def forward_copy(self, k):
        own = self.whole.at[self.p.core, self.zs[(4 - k) % 4]]
        return self.copy(4 + k, own, own, self.p.sibling())

    def begin(self):
        for k in (2, 1, 3, 0):
            self.pair_copy(k).start()

    def over_plane(self):
        for k in (2, 1, 3, 0):
            z = self.zs[k]
            self.pair_copy(k).wait_recv()
            self.made[k] = self.gp[self.p.core, z] + self.pair[z]
            for j in (2, 1, 3, 0):
                if k or j:
                    self.plane_copy(k, j).start()

    def over_x(self):
        total = self.made[0, self.p.y]
        for k in (0, 1, 3, 2):
            for j in (0, 1, 3, 2):
                if k or j:
                    self.plane_copy(k, j).wait_recv()
                    total = total + self.parts[k, j]
        self.cross[self.p.x] = total
        for k in (2, 1, 3):
            self.x_copy(k).start()

    def spread(self):
        for k in (1, 3, 2):
            self.x_copy(k).wait_recv()
        own = (self.cross[0] + self.cross[1]) + (self.cross[2] + self.cross[3])
        self.whole[self.p.core, self.p.z, self.p.y] = own
        for k in (2, 1, 3, 0):
            for j in (2, 1, 3, 0):
                if k or j:
                    self.back_copy(k, j).start()

    def gather_pair(self):
        for k in (0, 1, 3, 2):
            for j in range(4):
                if k or j:
                    self.back_copy(k, j).wait_recv()
            self.forward_copy(k).start()

    def finish(self):
        for k in range(4):
            self.forward_copy(k).wait_recv()
            self.pair_copy(k).wait_send()

    def sent(self):
        for k in range(4):
            self.forward_copy(k).wait_send()
            for j in range(4):
                if k or j:
                    self.plane_copy(k, j).wait_send()
                    self.back_copy(k, j).wait_send()
        for k in (1, 2, 3):
            self.x_copy(k).wait_send()


def greet(p):
    barrier = pltpu.get_barrier_semaphore()
    devices = [p.neighbour(dy, dx) for dy, dx in DIRS] + [p.sibling()]
    devices += [p.turn("x", k)[1] for k in (1, 2, 3)]
    for k in range(4):
        z = p.turn("z", k)[0]
        for j in range(4):
            if k or j:
                devices.append((p.x_lo * 4 + p.turn("y", j)[0], z * 4 + p.x_hi * 2 + p.core))
    for device in devices:
        pl.semaphore_signal(barrier, inc=1, device_id=device, device_id_type=MESH)
    return lambda: pl.semaphore_wait(barrier, len(devices))


EXCHANGES = 8
SUMS = ITERS


def exchange(p, refs, i):
    rows, cols, corners, sems = [ref.at[i] for ref in refs]
    pair = lambda ref: (ref.at[0], ref.at[1])
    return Edges(p, pair(rows), pair(cols), pair(corners), pair(sems))


def shifts(off_ref, s):
    top, left_col = off_ref[0, s], off_ref[1, s]
    inner = left_col >= 64
    first = jnp.where(inner, 0, 2)
    second = jnp.where(inner, 1, 0)
    third = jnp.where(inner, 2, 1)
    return top, jnp.where(inner, left_col - 64, left_col + 64), (first, second, third)


def take_window(off_ref, s, ext, win):
    top, shift, tiles = shifts(off_ref, s)
    keep = lax.broadcasted_iota(jnp.int32, (256, 128), 1) < 128 - shift
    for p in range(2):
        a, b, c = [pltpu.roll(ext[p, t, pl.ds(top, 256), :], 128 - shift, 1) for t in tiles]
        win[s, p, :, 0:128] = jnp.where(keep, a, b)
        win[s, p, :, 128:256] = jnp.where(keep, b, c)


def add_window(off_ref, count_ref, s, pair, slide, acc):
    top, shift, (first, second, third) = shifts(off_ref, s)
    lane = lax.broadcasted_iota(jnp.int32, (256, 128), 1)
    before = lane < shift
    active = lane * 0 + s < count_ref[0, 0]
    for p in range(2):
        a, b = [
            pltpu.roll(jnp.where(active, pair[p][:, t * 128 : t * 128 + 128], 0.0), shift, 1) for t in range(2)
        ]
        slide[p, 0, 128:384] = jnp.where(before, 0.0, a)
        slide[p, 1, 128:384] = jnp.where(before, a, b)
        slide[p, 2, 128:384] = jnp.where(before, b, 0.0)
    inner = first == 0
    source = (jnp.where(inner, 0, 1), jnp.where(inner, 1, 2), jnp.where(inner, 2, 0))
    for p in range(2):
        for t in range(3):
            acc[p, t] += slide[p, source[t], pl.ds(128 - top, 384), :]


def each_slot(fn):
    for s in range(MAXPOS):
        fn(s)


def program_kernel(
    count_ref, off_hbm, obj_hbm, probe_hbm, inten_hbm, tab_hbm, obj_out, probe_out,
    tab, inten, ext1, ext2, acc1, acc2, gp, slides, win1, win2, moved, back, mids, probe,
    rows, cols, corners, edge_sems, pair, made, parts, cross, whole, sum_sems, local_sems, off_ref, obj0, probe0,
):
    p = Place()
    ready = greet(p)
    edges = (rows, cols, corners, edge_sems)
    loads = []
    for k, ext in enumerate((ext1, ext2)):
        for t in range(2):
            src = obj_hbm.at[2 * k : 2 * k + 2, :, t * 128 : t * 128 + 128]
            loads.append(pltpu.make_async_copy(src, ext.at[:, t, 64:320], local_sems.at[2 * k + t]))
    loads.append(pltpu.make_async_copy(probe_hbm, probe, local_sems.at[4]))
    loads.append(pltpu.make_async_copy(tab_hbm, tab, local_sems.at[5]))
    loads.append(pltpu.make_async_copy(inten_hbm, inten, local_sems.at[6]))
    loads.append(pltpu.make_async_copy(off_hbm, off_ref, local_sems.at[7]))
    loads.append(pltpu.make_async_copy(obj_hbm, obj0, local_sems.at[8]))
    loads.append(pltpu.make_async_copy(probe_hbm, probe0, local_sems.at[9]))
    for load in loads:
        load.start()
    core1 = lambda t, r0, r1: ext1[:, t, 64 + r0 : 64 + r1]
    core2 = lambda t, r0, r1: ext2[:, t, 64 + r0 : 64 + r1]
    loads[0].wait()
    loads[1].wait()
    send_halo(exchange(p, edges, 0), core1, ready)
    loads[2].wait()
    loads[3].wait()
    send_halo(exchange(p, edges, 1), core2)
    slides[...] = jnp.zeros_like(slides)
    for load in loads[4:]:
        load.wait()

    def reorder(s, carry):
        inten[s] = into_paired_order(tab, inten[s])
        return carry

    lax.fori_loop(0, MAXPOS, reorder, 0)
    unpack_halo(exchange(p, edges, 0), ext1)

    def iteration(it, carry):
        acc1[...] = jnp.zeros_like(acc1)
        acc2[...] = jnp.zeros_like(acc2)
        gp[...] = jnp.zeros_like(gp)

        def forward(s):
            take_window(off_ref, s, ext1, win1)
            pr, pi, wr, wi = probe[0], probe[1], win1[s, 0], win1[s, 1]
            moved[s, 0], moved[s, 1] = propagate(tab, pr * wr - pi * wi, pr * wi + pi * wr, mids.at[s])

        def detector(s):
            take_window(off_ref, s, ext2, win2)
            er = moved[s, 0] * win2[s, 0] - moved[s, 1] * win2[s, 1]
            ei = moved[s, 0] * win2[s, 1] + moved[s, 1] * win2[s, 0]
            fr, fi = combine(*hartley(tab, 3, er, ei, mids.at[s]))
            misfit = fr * fr + fi * fi - inten[s]
            wr, wi = combine(misfit * fr, -(misfit * fi))
            cr, ci = hartley(tab, 4, wr, wi, mids.at[s])
            back[s, 0] = win2[s, 0] * cr - win2[s, 1] * ci
            back[s, 1] = win2[s, 0] * ci + win2[s, 1] * cr
            g2 = (moved[s, 0] * cr - moved[s, 1] * ci, -(moved[s, 0] * ci + moved[s, 1] * cr))
            add_window(off_ref, count_ref, s, g2, slides.at[s % 2], acc2)

        def adjoint(s):
            wr, wi = propagate(tab, back[s, 0], back[s, 1], mids.at[s])
            back[s, 0], back[s, 1] = wr, wi
            active = lax.broadcasted_iota(jnp.int32, (256, 128), 1) * 0 + s < count_ref[0, 0]
            sums = (win1[s, 0] * wr - win1[s, 1] * wi, -(win1[s, 0] * wi + win1[s, 1] * wr))
            for h in range(2):
                for t in range(2):
                    part = jnp.where(active, sums[h][:, t * 128 : t * 128 + 128], 0.0)
                    gp[h, 2 * t : 2 * t + 2] += part.reshape(2, 4, 32, 128)

        def first_slice(s):
            wr, wi = back[s, 0], back[s, 1]
            g1 = (probe[0] * wr - probe[1] * wi, -(probe[0] * wi + probe[1] * wr))
            add_window(off_ref, count_ref, s, g1, slides.at[s % 2], acc1)

        each_slot(forward)
        unpack_halo(exchange(p, edges, 4 * it + 1), ext2)
        each_slot(detector)
        fold2, fold1 = exchange(p, edges, 4 * it + 2), exchange(p, edges, 4 * it + 3)
        send_fold(fold2, acc2)
        each_slot(adjoint)

        bufs = [ref.at[it] for ref in (pair, made, parts, cross, whole)]
        s = Summer(p, gp, bufs, (sum_sems.at[it, 0], sum_sems.at[it, 1]))
        s.begin()
        each_slot(first_slice)
        s.over_plane()
        send_fold(fold1, acc1)
        rate = step_size(probe)
        descend_own(acc2, ext2, rate)
        descend_own(acc1, ext1, rate)
        descend(fold2, ext2, rate)
        s.over_x()
        s.spread()
        descend(fold1, ext1, rate)

        @pl.when(it == 0)
        def _():
            send_halo(exchange(p, edges, 4), core1)
            send_halo(exchange(p, edges, 5), core2)

        s.gather_pair()

        @pl.when(it == 0)
        def _():
            unpack_halo(exchange(p, edges, 4), ext1)

        s.finish()
        for h in range(2):
            for t in range(2):
                lanes = slice(t * 128, t * 128 + 128)
                change = (probe_rate / (NTY * NTX)) * s.whole[h, 2 * t : 2 * t + 2].reshape(256, 128)
                probe[h, :, lanes] -= change
        return carry

    lax.fori_loop(0, ITERS, iteration, 0)
    for t in range(2):
        lanes = slice(t * 128, t * 128 + 128)
        obj_out[0:2, :, lanes] = obj0[0:2, :, lanes] - ext1[:, t, 64:320]
        obj_out[2:4, :, lanes] = obj0[2:4, :, lanes] - ext2[:, t, 64:320]
    probe_out[...] = probe0[...] - probe[...]
    for it in range(SUMS):
        bufs = [ref.at[it] for ref in (pair, made, parts, cross, whole)]
        Summer(p, gp, bufs, (sum_sems.at[it, 0], sum_sems.at[it, 1])).sent()
    for i in range(EXCHANGES):
        wait_sent(exchange(p, edges, i))


def step_size(probe):
    power = probe[0] * probe[0] + probe[1] * probe[1]
    peak = jnp.max(power, axis=(0, 1), keepdims=True) + 1e-06
    return object_rate / peak


def run(count, off, obj, probe, inten, tab):
    smem = pl.BlockSpec(memory_space=pltpu.SMEM)
    anywhere = pl.BlockSpec(memory_space=pltpu.HBM)
    vm = pltpu.VMEM
    slots = vm((MAXPOS, 2, 256, 256), f32)
    return pl.pallas_call(
        program_kernel,
        out_shape=(jax.ShapeDtypeStruct((4, 256, 256), f32), jax.ShapeDtypeStruct((2, 256, 256), f32)),
        in_specs=[smem] + [anywhere] * 5,
        out_specs=(V, V),
        scratch_shapes=[
            vm((6, 2, 256, 256), bf),
            vm((MAXPOS, 256, 256), f32),
            vm((2, 3, 384, 128), f32),
            vm((2, 3, 384, 128), f32),
            vm((2, 3, 384, 128), f32),
            vm((2, 3, 384, 128), f32),
            vm((2, 4, 4, 32, 128), f32),
            vm((2, 2, 3, 512, 128), f32),
            slots,
            slots,
            slots,
            slots,
            slots,
            vm((2, 256, 256), f32),
            vm((EXCHANGES, 2, 2, 2, 2, 64, 128), f32),
            vm((EXCHANGES, 2, 2, 2, 128, 128), f32),
            vm((EXCHANGES, 2, 4, 2, 32, 128), f32),
            pltpu.SemaphoreType.DMA((EXCHANGES, 2, 8)),
            vm((SUMS, 4, 4, 32, 128), f32),
            vm((SUMS, 4, 4, 32, 128), f32),
            vm((SUMS, 4, 4, 32, 128), f32),
            vm((SUMS, 4, 32, 128), f32),
            vm((SUMS, 2, 4, 4, 32, 128), f32),
            pltpu.SemaphoreType.DMA((SUMS, 2, 48)),
            pltpu.SemaphoreType.DMA((10,)),
            pltpu.SMEM((2, MAXPOS), jnp.int32),
            vm((4, 256, 256), f32),
            vm((2, 256, 256), f32),
        ],
        compiler_params=pltpu.CompilerParams(collective_id=0, has_side_effects=True, vmem_limit_bytes=60 << 20),
        name="iterations",
    )(count, off, obj, probe, inten, tab)


def body(object_slices, probe, position_count, offsets, intensities):
    obj_change, probe_change = run(
        position_count,
        offsets[0, 0].T,
        object_slices.reshape(4, 256, 256),
        probe,
        intensities[0, 0],
        jnp.asarray(tables()),
    )
    return object_slices - obj_change.reshape(2, 2, 256, 256), probe - probe_change


def solution(mesh):
    placed = (
        P(None, None, "ty", "tx"),
        P(),
        P("ty", "tx"),
        P("ty", "tx", None, None),
        P("ty", "tx", None, None, None),
    )
    return jax.shard_map(
        body,
        mesh=mesh,
        in_specs=placed,
        out_specs=(P(None, None, "ty", "tx"), P()),
        check_vma=False,
    )
```

```python
import functools

import jax
import jax.numpy as jnp
import ml_dtypes
import numpy as np
from jax import lax
from jax.experimental import pallas as pl
from jax.experimental.pallas import tpu as pltpu
from jax.sharding import PartitionSpec as P

PROBE = 256
MAXPOS = 5
ITERS = 2
bf = jnp.bfloat16
f32 = jnp.float32

chirp_rate = 0.5
object_rate = 0.5
probe_rate = 2.0


def tables():
    n = PROBE
    k = np.arange(n)
    angle = 2 * np.pi * ((k[:, None] * k[None, :]) % n) / n
    four = np.exp(-1j * angle) / np.sqrt(n)
    c = (((k + n // 2) % n) - n // 2).astype(np.float64)
    prop = (np.conj(four) * np.exp(-1j * chirp_rate * np.pi * c * c / n)[None, :]) @ four
    order = np.concatenate([k[: n // 2], [n // 2], k[: n // 2 : -1]])
    hartley = ((np.cos(angle) + np.sin(angle)) / np.sqrt(2 * n))[order]
    swap = np.eye(n)[order]
    out = []
    for part in (prop.real, prop.imag - prop.real, prop.real + prop.imag, hartley, hartley.T):
        part = part.astype(np.float32)
        high = part.astype(ml_dtypes.bfloat16)
        out.append(np.stack([high, (part - high.astype(np.float32)).astype(ml_dtypes.bfloat16)]))
    out.append(np.stack([swap, swap.T]).astype(ml_dtypes.bfloat16))
    return np.stack(out)


def split(x):
    high = x.astype(bf)
    return high, (x - high.astype(f32)).astype(bf)


def dot(a, b):
    return jnp.dot(a, b, preferred_element_type=f32)


def left(tab, j, x):
    high, low = split(x)
    mat = jnp.concatenate([tab[j, 0], tab[j, 0], tab[j, 1]], axis=1)
    return dot(mat, jnp.concatenate([high, low, high], axis=0))


def right(tab, j, x):
    high, low = split(x)
    mat = jnp.concatenate([tab[j, 0], tab[j, 0], tab[j, 1]], axis=0)
    return dot(jnp.concatenate([high, low, high], axis=1), mat)


def propagate(tab, real, imag, mid):
    shared = left(tab, 0, real + imag)
    mid[1] = shared + left(tab, 1, real)
    mid[0] = shared - left(tab, 2, imag)
    real, imag = mid[0], mid[1]
    shared = right(tab, 0, real + imag)
    return shared - right(tab, 2, imag), shared + right(tab, 1, real)


def hartley(tab, j, real, imag, mid):
    mid[0], mid[1] = left(tab, j, real), left(tab, j, imag)
    return right(tab, 7 - j, mid[0]), right(tab, 7 - j, mid[1])


def mirror_rows(z):
    top, bottom = z[:128], z[128:]
    first = lax.broadcasted_iota(jnp.int32, (8, 256), 0) == 0
    new_top = jnp.where(first, top[:8], bottom[:8])
    new_bottom = jnp.where(first, bottom[:8], top[:8])
    return jnp.concatenate([new_top, bottom[8:], new_bottom, top[8:]], axis=0)


def mirror_columns(z):
    near, far = z[:, :128], z[:, 128:]
    first = lax.broadcasted_iota(jnp.int32, (256, 128), 1) == 0
    return jnp.concatenate([jnp.where(first, near, far), jnp.where(first, far, near)], axis=1)


def combine(real, imag):
    pairs = []
    for z in (real, imag):
        across = mirror_columns(z)
        pairs.append((mirror_rows(z) + across, z - mirror_rows(across)))
    (even_r, odd_r), (even_i, odd_i) = pairs
    return even_r + odd_i, even_i - odd_r


def into_paired_order(tab, x):
    for side in range(2):
        high, low = split(x)
        rest = (x - high.astype(f32) - low.astype(f32)).astype(bf)
        if side == 0:
            x = dot(tab[5, 0], high) + dot(tab[5, 0], low) + dot(tab[5, 0], rest)
        else:
            x = dot(high, tab[5, 1]) + dot(low, tab[5, 1]) + dot(rest, tab[5, 1])
    return x


NTY, NTX = 8, 16
MESH = pl.DeviceIdType.MESH
DIRS = [(dy, dx) for dy in (-1, 0, 1) for dx in (-1, 0, 1) if (dy, dx) != (0, 0)]
V = pl.BlockSpec(memory_space=pltpu.VMEM)


def half_lanes(shape):
    return lax.broadcasted_iota(jnp.int32, shape, len(shape) - 1) < 64


def pack(x, side):
    rows = x.shape[1] // 2
    first, second = x[:, :rows], x[:, rows:]
    low = half_lanes(first.shape)
    if side > 0:
        return jnp.where(low, pltpu.roll(first, 64, 2), second)
    return jnp.where(low, first, pltpu.roll(second, 64, 2))


def unpack(buf, side):
    turned = pltpu.roll(buf, 64, 2)
    pair = [turned, buf] if side > 0 else [buf, turned]
    return jnp.concatenate(pair, axis=1)


def keep_side(x, side):
    low = half_lanes(x.shape)
    return jnp.where(low, 0.0, x) if side > 0 else jnp.where(low, x, 0.0)


class Place:
    def __init__(self):
        self.ty, self.tx = lax.axis_index("ty"), lax.axis_index("tx")
        self.x_lo, self.y = self.ty // 4, lax.rem(self.ty, 4)
        self.z, self.core = self.tx // 4, lax.rem(self.tx, 2)
        self.x_hi = lax.rem(self.tx // 2, 2)
        self.x = self.x_hi * 2 + self.x_lo

    def neighbour(self, dy, dx):
        return (lax.rem(self.ty + dy + NTY, NTY), lax.rem(self.tx + dx + NTX, NTX))

    def sibling(self):
        return (self.ty, self.tx + 1 - 2 * self.core)

    def turn(self, axis, k):
        x, y, z = self.x, self.y, self.z
        if axis == "x":
            x = lax.rem(x + k, 4)
        elif axis == "y":
            y = lax.rem(y + k, 4)
        else:
            z = lax.rem(z + k, 4)
        spot = {"x": x, "y": y, "z": z}[axis]
        return spot, (lax.rem(x, 2) * 4 + y, z * 4 + (x // 2) * 2 + self.core)


def remote(src, dst, send, recv, device):
    return pltpu.make_async_remote_copy(
        src_ref=src, dst_ref=dst, send_sem=send, recv_sem=recv, device_id=device, device_id_type=MESH
    )


class Edges:
    def __init__(self, place, rows, cols, corners, sems):
        self.place, self.rows, self.cols, self.corners = place, rows, cols, corners
        self.send, self.recv = sems

    def slot(self, bufs, dy, dx):
        if dx == 0:
            return bufs[0].at[(dy + 1) // 2]
        if dy == 0:
            return bufs[1].at[(dx + 1) // 2]
        return bufs[2].at[(dy + 1) + (dx + 1) // 2]

    def out(self, dy, dx):
        return self.slot((self.rows[0], self.cols[0], self.corners[0]), dy, dx)

    def inc(self, dy, dx):
        return self.slot((self.rows[1], self.cols[1], self.corners[1]), dy, dx)

    def copy(self, dy, dx):
        i = DIRS.index((dy, dx))
        return remote(self.out(dy, dx), self.inc(dy, dx), self.send.at[i], self.recv.at[i], self.place.neighbour(dy, dx))


ORDER = [(1, 1), (1, -1), (-1, 1), (-1, -1), (0, 1), (0, -1), (1, 0), (-1, 0)]


def send_halo(e, core, ready=None):
    for dy, dx in ORDER:
        r0, r1 = {-1: (0, 64), 0: (0, 256), 1: (192, 256)}[dy]
        if dx == 0:
            for t in range(2):
                e.out(dy, dx)[:, t] = core(t, r0, r1)
        else:
            e.out(dy, dx)[...] = pack(core((dx + 1) // 2, r0, r1), dx)
        if ready is None:
            e.copy(dy, dx).start()
    if ready is not None:
        ready()
        for dy, dx in ORDER:
            e.copy(dy, dx).start()


def unpack_halo(e, ext):
    for dy in (-1, 1):
        e.copy(dy, 0).wait_recv()
        r0 = 320 if dy < 0 else 0
        for t in range(2):
            ext[:, t, r0 : r0 + 64] = e.inc(dy, 0)[:, t]
    for dy in (0, -1, 1):
        e.copy(dy, -1).wait_recv()
        e.copy(dy, 1).wait_recv()
        r0, r1 = {-1: (320, 384), 0: (64, 320), 1: (0, 64)}[dy]
        left, right = unpack(e.inc(dy, -1)[...], -1), unpack(e.inc(dy, 1)[...], 1)
        ext[:, 2, r0:r1] = jnp.where(half_lanes(left.shape), left, right)


def send_fold(e, g):
    for dy, dx in ORDER:
        r0, r1 = {-1: (0, 64), 0: (64, 320), 1: (320, 384)}[dy]
        if dx == 0:
            for t in range(2):
                e.out(dy, dx)[:, t] = g[:, t, r0:r1]
        else:
            e.out(dy, dx)[...] = pack(g[:, 2, r0:r1], -dx)
        e.copy(dy, dx).start()


def step_down(ext, t, r0, r1, change):
    ext[:, t, 64 + r0 : 64 + r1] -= change


def descend_own(g, ext, rate):
    for t in range(2):
        step_down(ext, t, 0, 256, rate * g[:, t, 64:320])


def descend(e, ext, rate):
    for dy, dx in ORDER[4:] + ORDER[:4]:
        e.copy(dy, dx).wait_recv()
        r0, r1 = {-1: (192, 256), 0: (0, 256), 1: (0, 64)}[dy]
        if dx == 0:
            for t in range(2):
                step_down(ext, t, r0, r1, rate * e.inc(dy, dx)[:, t])
        else:
            values = keep_side(unpack(e.inc(dy, dx)[...], -dx), -dx)
            step_down(ext, (1 - dx) // 2, r0, r1, rate * values)


def wait_sent(e):
    for dy, dx in ORDER:
        e.copy(dy, dx).wait_send()


class Summer:
    def __init__(self, place, gp, bufs, sems):
        self.p, self.gp = place, gp
        self.pair, self.made, self.parts, self.cross, self.whole = bufs
        self.send, self.recv = sems
        self.zs = [place.turn("z", k)[0] for k in range(4)]
        self.ys = [place.turn("y", k)[0] for k in range(4)]
        self.xs = [place.turn("x", k)[1] for k in range(4)]

    def copy(self, i, src, dst, device):
        return remote(src, dst, self.send.at[i], self.recv.at[i], device)

    def device(self, k, j):
        return (self.p.x_lo * 4 + self.ys[j], self.zs[k] * 4 + self.p.x_hi * 2 + self.p.core)

    def pair_copy(self, k):
        z = self.zs[k]
        return self.copy(k, self.gp.at[1 - self.p.core, z], self.pair.at[z], self.p.sibling())

    def plane_copy(self, k, j):
        return self.copy(8 + 4 * k + j, self.made.at[k, self.ys[j]], self.parts.at[k, j], self.device(k, j))

    def x_copy(self, k):
        own = self.cross.at[self.p.x]
        return self.copy(40 + k, own, own, self.xs[k])

    def back_copy(self, k, j):
        own = self.whole.at[self.p.core, self.p.z, self.p.y]
        return self.copy(24 + 4 * k + j, own, own, self.device(k, j))

    def forward_copy(self, k):
        own = self.whole.at[self.p.core, self.zs[(4 - k) % 4]]
        return self.copy(4 + k, own, own, self.p.sibling())

    def begin(self):
        for k in (2, 1, 3, 0):
            self.pair_copy(k).start()

    def over_plane(self):
        for k in (2, 1, 3, 0):
            z = self.zs[k]
            self.pair_copy(k).wait_recv()
            self.made[k] = self.gp[self.p.core, z] + self.pair[z]
            for j in (2, 1, 3, 0):
                if k or j:
                    self.plane_copy(k, j).start()

    def over_x(self):
        total = self.made[0, self.p.y]
        for k in (0, 1, 3, 2):
            for j in (0, 1, 3, 2):
                if k or j:
                    self.plane_copy(k, j).wait_recv()
                    total = total + self.parts[k, j]
        self.cross[self.p.x] = total
        for k in (2, 1, 3):
            self.x_copy(k).start()
        for k in range(4):
            self.pair_copy(k).wait_send()
            for j in range(4):
                if k or j:
                    self.plane_copy(k, j).wait_send()

    def spread(self):
        for k in (1, 3, 2):
            self.x_copy(k).wait_recv()
        own = (self.cross[0] + self.cross[1]) + (self.cross[2] + self.cross[3])
        self.whole[self.p.core, self.p.z, self.p.y] = own
        for k in (2, 1, 3, 0):
            for j in (2, 1, 3, 0):
                if k or j:
                    self.back_copy(k, j).start()

    def gather_pair(self):
        for k in (1, 2, 3):
            self.x_copy(k).wait_send()
        for k in (0, 1, 3, 2):
            for j in range(4):
                if k or j:
                    self.back_copy(k, j).wait_recv()
            self.forward_copy(k).start()
        for k in range(4):
            for j in range(4):
                if k or j:
                    self.back_copy(k, j).wait_send()

    def finish(self):
        for k in range(4):
            self.forward_copy(k).wait_recv()

    def sent(self):
        for k in range(4):
            self.forward_copy(k).wait_send()


def greet(p):
    barrier = pltpu.get_barrier_semaphore()
    devices = [p.neighbour(dy, dx) for dy, dx in DIRS] + [p.sibling()]
    devices += [p.turn("x", k)[1] for k in (1, 2, 3)]
    for k in range(4):
        z = p.turn("z", k)[0]
        for j in range(4):
            if k or j:
                devices.append((p.x_lo * 4 + p.turn("y", j)[0], z * 4 + p.x_hi * 2 + p.core))
    for device in devices:
        pl.semaphore_signal(barrier, inc=1, device_id=device, device_id_type=MESH)
    return lambda: pl.semaphore_wait(barrier, len(devices))


EXCHANGES = 8
SUMS = ITERS


def exchange(p, refs, i):
    rows, cols, corners, sems = [ref.at[i] for ref in refs]
    pair = lambda ref: (ref.at[0], ref.at[1])
    return Edges(p, pair(rows), pair(cols), pair(corners), pair(sems))


def shifts(off_ref, s):
    top, left_col = off_ref[0, s], off_ref[1, s]
    inner = left_col >= 64
    first = jnp.where(inner, 0, 2)
    second = jnp.where(inner, 1, 0)
    third = jnp.where(inner, 2, 1)
    return top, jnp.where(inner, left_col - 64, left_col + 64), (first, second, third)


def take_window(off_ref, s, ext, win):
    top, shift, tiles = shifts(off_ref, s)
    keep = lax.broadcasted_iota(jnp.int32, (256, 128), 1) < 128 - shift
    for p in range(2):
        a, b, c = [pltpu.roll(ext[p, t, pl.ds(top, 256), :], 128 - shift, 1) for t in tiles]
        win[s, p, :, 0:128] = jnp.where(keep, a, b)
        win[s, p, :, 128:256] = jnp.where(keep, b, c)


def add_window(off_ref, count_ref, s, pair, slide, acc):
    top, shift, (first, second, third) = shifts(off_ref, s)
    lane = lax.broadcasted_iota(jnp.int32, (256, 128), 1)
    before = lane < shift
    active = lane * 0 + s < count_ref[0, 0]
    for p in range(2):
        a, b = [
            pltpu.roll(jnp.where(active, pair[p][:, t * 128 : t * 128 + 128], 0.0), shift, 1) for t in range(2)
        ]
        slide[p, 0, 128:384] = jnp.where(before, 0.0, a)
        slide[p, 1, 128:384] = jnp.where(before, a, b)
        slide[p, 2, 128:384] = jnp.where(before, b, 0.0)
    inner = first == 0
    source = (jnp.where(inner, 0, 1), jnp.where(inner, 1, 2), jnp.where(inner, 2, 0))
    for p in range(2):
        for t in range(3):
            acc[p, t] += slide[p, source[t], pl.ds(128 - top, 384), :]


def each_slot(fn):
    for s in range(MAXPOS):
        fn(s)


def program_kernel(
    count_ref, off_hbm, obj_hbm, probe_hbm, inten_hbm, tab_hbm, obj_out, probe_out,
    tab, inten, ext1, ext2, acc1, acc2, gp, slides, win1, win2, moved, back, mids, probe,
    rows, cols, corners, edge_sems, pair, made, parts, cross, whole, sum_sems, local_sems, off_ref,
):
    p = Place()
    ready = greet(p)
    edges = (rows, cols, corners, edge_sems)
    loads = []
    for k, ext in enumerate((ext1, ext2)):
        for t in range(2):
            src = obj_hbm.at[2 * k : 2 * k + 2, :, t * 128 : t * 128 + 128]
            loads.append(pltpu.make_async_copy(src, ext.at[:, t, 64:320], local_sems.at[2 * k + t]))
    loads.append(pltpu.make_async_copy(probe_hbm, probe, local_sems.at[4]))
    loads.append(pltpu.make_async_copy(tab_hbm, tab, local_sems.at[5]))
    loads.append(pltpu.make_async_copy(inten_hbm, inten, local_sems.at[6]))
    loads.append(pltpu.make_async_copy(off_hbm, off_ref, local_sems.at[7]))
    for load in loads:
        load.start()
    core1 = lambda t, r0, r1: ext1[:, t, 64 + r0 : 64 + r1]
    core2 = lambda t, r0, r1: ext2[:, t, 64 + r0 : 64 + r1]
    loads[0].wait()
    loads[1].wait()
    send_halo(exchange(p, edges, 0), core1, ready)
    loads[2].wait()
    loads[3].wait()
    send_halo(exchange(p, edges, 1), core2)
    for ref in (slides, acc1, acc2, gp):
        ref[...] = jnp.zeros_like(ref)
    for load in loads[4:]:
        load.wait()

    def reorder(s, carry):
        inten[s] = into_paired_order(tab, inten[s])
        return carry

    lax.fori_loop(0, MAXPOS, reorder, 0)
    unpack_halo(exchange(p, edges, 0), ext1)

    stores = []
    for k, ext in enumerate((ext1, ext2)):
        for t in range(2):
            dst = obj_out.at[2 * k : 2 * k + 2, :, t * 128 : t * 128 + 128]
            stores.append(pltpu.make_async_copy(ext.at[:, t, 64:320], dst, local_sems.at[8 + 2 * k + t]))

    def iteration(it, carry):

        def forward(s):
            take_window(off_ref, s, ext1, win1)
            pr, pi, wr, wi = probe[0], probe[1], win1[s, 0], win1[s, 1]
            moved[s, 0], moved[s, 1] = propagate(tab, pr * wr - pi * wi, pr * wi + pi * wr, mids.at[s])

        def detector(s):
            take_window(off_ref, s, ext2, win2)
            er = moved[s, 0] * win2[s, 0] - moved[s, 1] * win2[s, 1]
            ei = moved[s, 0] * win2[s, 1] + moved[s, 1] * win2[s, 0]
            fr, fi = combine(*hartley(tab, 3, er, ei, mids.at[s]))
            misfit = fr * fr + fi * fi - inten[s]
            wr, wi = combine(misfit * fr, -(misfit * fi))
            cr, ci = hartley(tab, 4, wr, wi, mids.at[s])
            back[s, 0] = win2[s, 0] * cr - win2[s, 1] * ci
            back[s, 1] = win2[s, 0] * ci + win2[s, 1] * cr
            g2 = (moved[s, 0] * cr - moved[s, 1] * ci, -(moved[s, 0] * ci + moved[s, 1] * cr))
            add_window(off_ref, count_ref, s, g2, slides.at[s % 2], acc2)

        def adjoint(s):
            wr, wi = propagate(tab, back[s, 0], back[s, 1], mids.at[s])
            back[s, 0], back[s, 1] = wr, wi
            active = lax.broadcasted_iota(jnp.int32, (256, 128), 1) * 0 + s < count_ref[0, 0]
            sums = (win1[s, 0] * wr - win1[s, 1] * wi, -(win1[s, 0] * wi + win1[s, 1] * wr))
            for h in range(2):
                for t in range(2):
                    part = jnp.where(active, sums[h][:, t * 128 : t * 128 + 128], 0.0)
                    gp[h, 2 * t : 2 * t + 2] += part.reshape(2, 4, 32, 128)

        def first_slice(s):
            wr, wi = back[s, 0], back[s, 1]
            g1 = (probe[0] * wr - probe[1] * wi, -(probe[0] * wi + probe[1] * wr))
            add_window(off_ref, count_ref, s, g1, slides.at[s % 2], acc1)

        each_slot(forward)
        unpack_halo(exchange(p, edges, 4 * it + 1), ext2)
        each_slot(detector)
        fold2, fold1 = exchange(p, edges, 4 * it + 2), exchange(p, edges, 4 * it + 3)
        send_fold(fold2, acc2)
        each_slot(adjoint)

        bufs = [ref.at[it] for ref in (pair, made, parts, cross, whole)]
        s = Summer(p, gp, bufs, (sum_sems.at[it, 0], sum_sems.at[it, 1]))
        s.begin()
        each_slot(first_slice)
        s.over_plane()
        send_fold(fold1, acc1)
        rate = step_size(probe)
        descend_own(acc2, ext2, rate)
        descend_own(acc1, ext1, rate)
        acc1[...] = jnp.zeros_like(acc1)
        acc2[...] = jnp.zeros_like(acc2)
        for i in range(3):
            wait_sent(exchange(p, edges, 4 * it + i))
        descend(fold2, ext2, rate)

        @pl.when(it == ITERS - 1)
        def _():
            stores[2].start()
            stores[3].start()

        s.over_x()
        s.spread()
        descend(fold1, ext1, rate)

        @pl.when(it == 0)
        def _():
            send_halo(exchange(p, edges, 4), core1)
            send_halo(exchange(p, edges, 5), core2)

        @pl.when(it == ITERS - 1)
        def _():
            stores[0].start()
            stores[1].start()

        wait_sent(fold1)
        s.gather_pair()

        @pl.when(it == 0)
        def _():
            unpack_halo(exchange(p, edges, 4), ext1)

        gp[...] = jnp.zeros_like(gp)
        s.finish()
        for h in range(2):
            for t in range(2):
                lanes = slice(t * 128, t * 128 + 128)
                change = (probe_rate / (NTY * NTX)) * s.whole[h, 2 * t : 2 * t + 2].reshape(256, 128)
                probe[h, :, lanes] -= change
        s.sent()
        return carry

    lax.fori_loop(0, ITERS, iteration, 0)
    probe_out[...] = probe[...]
    for store in stores:
        store.wait()


def step_size(probe):
    power = probe[0] * probe[0] + probe[1] * probe[1]
    peak = jnp.max(power, axis=(0, 1), keepdims=True) + 1e-06
    return object_rate / peak


def run(count, off, obj, probe, inten, tab):
    smem = pl.BlockSpec(memory_space=pltpu.SMEM)
    anywhere = pl.BlockSpec(memory_space=pltpu.HBM)
    vm = pltpu.VMEM
    slots = vm((MAXPOS, 2, 256, 256), f32)
    return pl.pallas_call(
        program_kernel,
        out_shape=(jax.ShapeDtypeStruct((4, 256, 256), f32), jax.ShapeDtypeStruct((2, 256, 256), f32)),
        in_specs=[smem] + [anywhere] * 5,
        out_specs=(anywhere, V),
        scratch_shapes=[
            vm((6, 2, 256, 256), bf),
            vm((MAXPOS, 256, 256), f32),
            vm((2, 3, 384, 128), f32),
            vm((2, 3, 384, 128), f32),
            vm((2, 3, 384, 128), f32),
            vm((2, 3, 384, 128), f32),
            vm((2, 4, 4, 32, 128), f32),
            vm((2, 2, 3, 512, 128), f32),
            slots,
            slots,
            slots,
            slots,
            slots,
            vm((2, 256, 256), f32),
            vm((EXCHANGES, 2, 2, 2, 2, 64, 128), f32),
            vm((EXCHANGES, 2, 2, 2, 128, 128), f32),
            vm((EXCHANGES, 2, 4, 2, 32, 128), f32),
            pltpu.SemaphoreType.DMA((EXCHANGES, 2, 8)),
            vm((SUMS, 4, 4, 32, 128), f32),
            vm((SUMS, 4, 4, 32, 128), f32),
            vm((SUMS, 4, 4, 32, 128), f32),
            vm((SUMS, 4, 32, 128), f32),
            vm((SUMS, 2, 4, 4, 32, 128), f32),
            pltpu.SemaphoreType.DMA((SUMS, 2, 48)),
            pltpu.SemaphoreType.DMA((12,)),
            pltpu.SMEM((2, MAXPOS), jnp.int32),
        ],
        compiler_params=pltpu.CompilerParams(collective_id=0, has_side_effects=True, vmem_limit_bytes=60 << 20),
        name="iterations",
    )(count, off, obj, probe, inten, tab)


def body(object_slices, probe, position_count, offsets, intensities):
    obj, probe = run(
        position_count,
        offsets[0, 0].T,
        object_slices.reshape(4, 256, 256),
        probe,
        intensities[0, 0],
        jnp.asarray(tables()),
    )
    return obj.reshape(2, 2, 256, 256), probe


def solution(mesh):
    placed = (
        P(None, None, "ty", "tx"),
        P(),
        P("ty", "tx"),
        P("ty", "tx", None, None),
        P("ty", "tx", None, None, None),
    )
    return jax.shard_map(
        body,
        mesh=mesh,
        in_specs=placed,
        out_specs=(P(None, None, "ty", "tx"), P()),
        check_vma=False,
    )
```

```python
import functools

import jax
import jax.numpy as jnp
import ml_dtypes
import numpy as np
from jax import lax
from jax.experimental import pallas as pl
from jax.experimental.pallas import tpu as pltpu
from jax.sharding import PartitionSpec as P

PROBE = 256
MAXPOS = 5
ITERS = 2
bf = jnp.bfloat16
f32 = jnp.float32

chirp_rate = 0.5
object_rate = 0.5
probe_rate = 2.0


def tables():
    n = PROBE
    k = np.arange(n)
    angle = 2 * np.pi * ((k[:, None] * k[None, :]) % n) / n
    four = np.exp(-1j * angle) / np.sqrt(n)
    c = (((k + n // 2) % n) - n // 2).astype(np.float64)
    prop = (np.conj(four) * np.exp(-1j * chirp_rate * np.pi * c * c / n)[None, :]) @ four
    order = np.concatenate([k[: n // 2], [n // 2], k[: n // 2 : -1]])
    hartley = ((np.cos(angle) + np.sin(angle)) / np.sqrt(2 * n))[order]
    swap = np.eye(n)[order]
    out = []
    for part in (prop.real, prop.imag - prop.real, prop.real + prop.imag, hartley, hartley.T):
        part = part.astype(np.float32)
        high = part.astype(ml_dtypes.bfloat16)
        out.append(np.stack([high, (part - high.astype(np.float32)).astype(ml_dtypes.bfloat16)]))
    out.append(np.stack([swap, swap.T]).astype(ml_dtypes.bfloat16))
    return np.stack(out)


def split(x):
    high = x.astype(bf)
    return high, (x - high.astype(f32)).astype(bf)


def dot(a, b):
    return jnp.dot(a, b, preferred_element_type=f32)


def left(tab, j, x):
    high, low = split(x)
    mat = jnp.concatenate([tab[j, 0], tab[j, 0], tab[j, 1]], axis=1)
    return dot(mat, jnp.concatenate([high, low, high], axis=0))


def right(tab, j, x):
    high, low = split(x)
    mat = jnp.concatenate([tab[j, 0], tab[j, 0], tab[j, 1]], axis=0)
    return dot(jnp.concatenate([high, low, high], axis=1), mat)


def propagate(tab, real, imag, mid):
    shared = left(tab, 0, real + imag)
    mid[1] = shared + left(tab, 1, real)
    mid[0] = shared - left(tab, 2, imag)
    real, imag = mid[0], mid[1]
    shared = right(tab, 0, real + imag)
    return shared - right(tab, 2, imag), shared + right(tab, 1, real)


def hartley(tab, j, real, imag, mid):
    mid[0], mid[1] = left(tab, j, real), left(tab, j, imag)
    return right(tab, 7 - j, mid[0]), right(tab, 7 - j, mid[1])


def mirror_rows(z):
    top, bottom = z[:128], z[128:]
    first = lax.broadcasted_iota(jnp.int32, (8, 256), 0) == 0
    new_top = jnp.where(first, top[:8], bottom[:8])
    new_bottom = jnp.where(first, bottom[:8], top[:8])
    return jnp.concatenate([new_top, bottom[8:], new_bottom, top[8:]], axis=0)


def mirror_columns(z):
    near, far = z[:, :128], z[:, 128:]
    first = lax.broadcasted_iota(jnp.int32, (256, 128), 1) == 0
    return jnp.concatenate([jnp.where(first, near, far), jnp.where(first, far, near)], axis=1)


def combine(real, imag):
    pairs = []
    for z in (real, imag):
        across = mirror_columns(z)
        pairs.append((mirror_rows(z) + across, z - mirror_rows(across)))
    (even_r, odd_r), (even_i, odd_i) = pairs
    return even_r + odd_i, even_i - odd_r


def into_paired_order(tab, x):
    for side in range(2):
        high, low = split(x)
        rest = (x - high.astype(f32) - low.astype(f32)).astype(bf)
        if side == 0:
            x = dot(tab[5, 0], high) + dot(tab[5, 0], low) + dot(tab[5, 0], rest)
        else:
            x = dot(high, tab[5, 1]) + dot(low, tab[5, 1]) + dot(rest, tab[5, 1])
    return x


NTY, NTX = 8, 16
MESH = pl.DeviceIdType.MESH
DIRS = [(dy, dx) for dy in (-1, 0, 1) for dx in (-1, 0, 1) if (dy, dx) != (0, 0)]
V = pl.BlockSpec(memory_space=pltpu.VMEM)


def half_lanes(shape):
    return lax.broadcasted_iota(jnp.int32, shape, len(shape) - 1) < 64


def pack(x, side):
    rows = x.shape[1] // 2
    first, second = x[:, :rows], x[:, rows:]
    low = half_lanes(first.shape)
    if side > 0:
        return jnp.where(low, pltpu.roll(first, 64, 2), second)
    return jnp.where(low, first, pltpu.roll(second, 64, 2))


def unpack(buf, side):
    turned = pltpu.roll(buf, 64, 2)
    pair = [turned, buf] if side > 0 else [buf, turned]
    return jnp.concatenate(pair, axis=1)


def keep_side(x, side):
    low = half_lanes(x.shape)
    return jnp.where(low, 0.0, x) if side > 0 else jnp.where(low, x, 0.0)


class Place:
    def __init__(self):
        self.ty, self.tx = lax.axis_index("ty"), lax.axis_index("tx")
        self.x_lo, self.y = self.ty // 4, lax.rem(self.ty, 4)
        self.z, self.core = self.tx // 4, lax.rem(self.tx, 2)
        self.x_hi = lax.rem(self.tx // 2, 2)
        self.x = self.x_hi * 2 + self.x_lo

    def neighbour(self, dy, dx):
        return (lax.rem(self.ty + dy + NTY, NTY), lax.rem(self.tx + dx + NTX, NTX))

    def sibling(self):
        return (self.ty, self.tx + 1 - 2 * self.core)

    def turn(self, axis, k):
        x, y, z = self.x, self.y, self.z
        if axis == "x":
            x = lax.rem(x + k, 4)
        elif axis == "y":
            y = lax.rem(y + k, 4)
        else:
            z = lax.rem(z + k, 4)
        spot = {"x": x, "y": y, "z": z}[axis]
        return spot, (lax.rem(x, 2) * 4 + y, z * 4 + (x // 2) * 2 + self.core)


def remote(src, dst, send, recv, device):
    return pltpu.make_async_remote_copy(
        src_ref=src, dst_ref=dst, send_sem=send, recv_sem=recv, device_id=device, device_id_type=MESH
    )


class Edges:
    def __init__(self, place, rows, cols, corners, sems):
        self.place, self.rows, self.cols, self.corners = place, rows, cols, corners
        self.send, self.recv = sems

    def slot(self, bufs, dy, dx):
        if dx == 0:
            return bufs[0].at[(dy + 1) // 2]
        if dy == 0:
            return bufs[1].at[(dx + 1) // 2]
        return bufs[2].at[(dy + 1) + (dx + 1) // 2]

    def out(self, dy, dx):
        return self.slot((self.rows[0], self.cols[0], self.corners[0]), dy, dx)

    def inc(self, dy, dx):
        return self.slot((self.rows[1], self.cols[1], self.corners[1]), dy, dx)

    def copy(self, dy, dx):
        i = DIRS.index((dy, dx))
        return remote(self.out(dy, dx), self.inc(dy, dx), self.send.at[i], self.recv.at[i], self.place.neighbour(dy, dx))


ORDER = [(1, 1), (1, -1), (-1, 1), (-1, -1), (0, 1), (0, -1), (1, 0), (-1, 0)]


def send_halo(e, core, ready=None):
    for dy, dx in ORDER:
        r0, r1 = {-1: (0, 64), 0: (0, 256), 1: (192, 256)}[dy]
        if dx == 0:
            for t in range(2):
                e.out(dy, dx)[:, t] = core(t, r0, r1)
        else:
            e.out(dy, dx)[...] = pack(core((dx + 1) // 2, r0, r1), dx)
        if ready is None:
            e.copy(dy, dx).start()
    if ready is not None:
        ready()
        for dy, dx in ORDER:
            e.copy(dy, dx).start()


def unpack_halo(e, ext):
    for dy in (-1, 1):
        e.copy(dy, 0).wait_recv()
        r0 = 320 if dy < 0 else 0
        for t in range(2):
            ext[:, t, r0 : r0 + 64] = e.inc(dy, 0)[:, t]
    for dy in (0, -1, 1):
        e.copy(dy, -1).wait_recv()
        e.copy(dy, 1).wait_recv()
        r0, r1 = {-1: (320, 384), 0: (64, 320), 1: (0, 64)}[dy]
        left, right = unpack(e.inc(dy, -1)[...], -1), unpack(e.inc(dy, 1)[...], 1)
        ext[:, 2, r0:r1] = jnp.where(half_lanes(left.shape), left, right)


def send_fold(e, g):
    for dy, dx in ORDER:
        r0, r1 = {-1: (0, 64), 0: (64, 320), 1: (320, 384)}[dy]
        if dx == 0:
            for t in range(2):
                e.out(dy, dx)[:, t] = g[:, t, r0:r1]
        else:
            e.out(dy, dx)[...] = pack(g[:, 2, r0:r1], -dx)
        e.copy(dy, dx).start()


def step_down(ext, t, r0, r1, change):
    ext[:, t, 64 + r0 : 64 + r1] -= change


def descend_own(g, ext, rate):
    for t in range(2):
        step_down(ext, t, 0, 256, rate * g[:, t, 64:320])


def descend(e, ext, rate):
    for dy, dx in ORDER[4:] + ORDER[:4]:
        e.copy(dy, dx).wait_recv()
        r0, r1 = {-1: (192, 256), 0: (0, 256), 1: (0, 64)}[dy]
        if dx == 0:
            for t in range(2):
                step_down(ext, t, r0, r1, rate * e.inc(dy, dx)[:, t])
        else:
            values = keep_side(unpack(e.inc(dy, dx)[...], -dx), -dx)
            step_down(ext, (1 - dx) // 2, r0, r1, rate * values)


def wait_sent(e):
    for dy, dx in ORDER:
        e.copy(dy, dx).wait_send()


class Summer:
    def __init__(self, place, gp, bufs, sems):
        self.p, self.gp = place, gp
        self.pair, self.made, self.parts, self.cross, self.whole = bufs
        self.send, self.recv = sems
        self.zs = [place.turn("z", k)[0] for k in range(4)]
        self.ys = [place.turn("y", k)[0] for k in range(4)]
        self.xs = [place.turn("x", k)[1] for k in range(4)]

    def copy(self, i, src, dst, device):
        return remote(src, dst, self.send.at[i], self.recv.at[i], device)

    def device(self, k, j):
        return (self.p.x_lo * 4 + self.ys[j], self.zs[k] * 4 + self.p.x_hi * 2 + self.p.core)

    def pair_copy(self, k):
        z = self.zs[k]
        return self.copy(k, self.gp.at[1 - self.p.core, z], self.pair.at[z], self.p.sibling())

    def plane_copy(self, k, j):
        return self.copy(8 + 4 * k + j, self.made.at[k, self.ys[j]], self.parts.at[k, j], self.device(k, j))

    def x_copy(self, k):
        own = self.cross.at[self.p.x]
        return self.copy(40 + k, own, own, self.xs[k])

    def back_copy(self, k, j):
        own = self.whole.at[self.p.core, self.p.z, self.p.y]
        return self.copy(24 + 4 * k + j, own, own, self.device(k, j))

    def forward_copy(self, k):
        own = self.whole.at[self.p.core, self.zs[(4 - k) % 4]]
        return self.copy(4 + k, own, own, self.p.sibling())

    def begin(self):
        for k in (2, 1, 3, 0):
            self.pair_copy(k).start()

    def over_plane(self):
        for k in (2, 1, 3, 0):
            z = self.zs[k]
            self.pair_copy(k).wait_recv()
            self.made[k] = self.gp[self.p.core, z] + self.pair[z]
            for j in (2, 1, 3, 0):
                if k or j:
                    self.plane_copy(k, j).start()

    def over_x(self):
        total = self.made[0, self.p.y]
        for k in (0, 1, 3, 2):
            for j in (0, 1, 3, 2):
                if k or j:
                    self.plane_copy(k, j).wait_recv()
                    total = total + self.parts[k, j]
        self.cross[self.p.x] = total
        for k in (2, 1, 3):
            self.x_copy(k).start()
        for k in range(4):
            self.pair_copy(k).wait_send()
            for j in range(4):
                if k or j:
                    self.plane_copy(k, j).wait_send()

    def spread(self):
        for k in (1, 3, 2):
            self.x_copy(k).wait_recv()
        own = (self.cross[0] + self.cross[1]) + (self.cross[2] + self.cross[3])
        self.whole[self.p.core, self.p.z, self.p.y] = own
        for k in (2, 1, 3, 0):
            for j in (2, 1, 3, 0):
                if k or j:
                    self.back_copy(k, j).start()

    def gather_pair(self):
        for k in (1, 2, 3):
            self.x_copy(k).wait_send()
        for k in (0, 1, 3, 2):
            for j in range(4):
                if k or j:
                    self.back_copy(k, j).wait_recv()
            self.forward_copy(k).start()
        for k in range(4):
            for j in range(4):
                if k or j:
                    self.back_copy(k, j).wait_send()

    def finish(self):
        for k in range(4):
            self.forward_copy(k).wait_recv()

    def sent(self):
        for k in range(4):
            self.forward_copy(k).wait_send()


def greet(p):
    barrier = pltpu.get_barrier_semaphore()
    devices = [p.neighbour(dy, dx) for dy, dx in DIRS] + [p.sibling()]
    devices += [p.turn("x", k)[1] for k in (1, 2, 3)]
    for k in range(4):
        z = p.turn("z", k)[0]
        for j in range(4):
            if k or j:
                devices.append((p.x_lo * 4 + p.turn("y", j)[0], z * 4 + p.x_hi * 2 + p.core))
    for device in devices:
        pl.semaphore_signal(barrier, inc=1, device_id=device, device_id_type=MESH)
    return lambda: pl.semaphore_wait(barrier, len(devices))


EXCHANGES = 8
SUMS = ITERS


def exchange(p, refs, i):
    rows, cols, corners, sems = [ref.at[i] for ref in refs]
    pair = lambda ref: (ref.at[0], ref.at[1])
    return Edges(p, pair(rows), pair(cols), pair(corners), pair(sems))


def shifts(off_ref, s):
    top, left_col = off_ref[0, s], off_ref[1, s]
    inner = left_col >= 64
    first = jnp.where(inner, 0, 2)
    second = jnp.where(inner, 1, 0)
    third = jnp.where(inner, 2, 1)
    return top, jnp.where(inner, left_col - 64, left_col + 64), (first, second, third)


def take_window(off_ref, s, ext, win):
    top, shift, tiles = shifts(off_ref, s)
    keep = lax.broadcasted_iota(jnp.int32, (256, 128), 1) < 128 - shift
    for p in range(2):
        a, b, c = [pltpu.roll(ext[p, t, pl.ds(top, 256), :], 128 - shift, 1) for t in tiles]
        win[s, p, :, 0:128] = jnp.where(keep, a, b)
        win[s, p, :, 128:256] = jnp.where(keep, b, c)


def add_window(off_ref, count_ref, s, pair, slide, acc):
    top, shift, (first, second, third) = shifts(off_ref, s)
    lane = lax.broadcasted_iota(jnp.int32, (256, 128), 1)
    before = lane < shift
    active = lane * 0 + s < count_ref[0, 0]
    for p in range(2):
        a, b = [
            pltpu.roll(jnp.where(active, pair[p][:, t * 128 : t * 128 + 128], 0.0), shift, 1) for t in range(2)
        ]
        slide[p, 0, 128:384] = jnp.where(before, 0.0, a)
        slide[p, 1, 128:384] = jnp.where(before, a, b)
        slide[p, 2, 128:384] = jnp.where(before, b, 0.0)
    inner = first == 0
    source = (jnp.where(inner, 0, 1), jnp.where(inner, 1, 2), jnp.where(inner, 2, 0))
    for p in range(2):
        for t in range(3):
            acc[p, t] += slide[p, source[t], pl.ds(128 - top, 384), :]


def each_slot(fn):
    for s in range(MAXPOS):
        fn(s)


def program_kernel(
    count_ref, off_hbm, obj_hbm, probe_hbm, inten_hbm, tab_hbm, obj_out, probe_out,
    tab, inten, ext1, ext2, acc1, acc2, gp, slides, win1, win2, moved, back, mids, probe,
    rows, cols, corners, edge_sems, pair, made, parts, cross, whole, sum_sems, local_sems, off_ref,
):
    p = Place()
    ready = greet(p)
    edges = (rows, cols, corners, edge_sems)
    loads = []
    for k, ext in enumerate((ext1, ext2)):
        for t in range(2):
            src = obj_hbm.at[2 * k : 2 * k + 2, :, t * 128 : t * 128 + 128]
            loads.append(pltpu.make_async_copy(src, ext.at[:, t, 64:320], local_sems.at[2 * k + t]))
    loads.append(pltpu.make_async_copy(probe_hbm, probe, local_sems.at[4]))
    loads.append(pltpu.make_async_copy(tab_hbm, tab, local_sems.at[5]))
    loads.append(pltpu.make_async_copy(inten_hbm, inten, local_sems.at[6]))
    loads.append(pltpu.make_async_copy(off_hbm, off_ref, local_sems.at[7]))
    for load in loads:
        load.start()
    core1 = lambda t, r0, r1: ext1[:, t, 64 + r0 : 64 + r1]
    core2 = lambda t, r0, r1: ext2[:, t, 64 + r0 : 64 + r1]
    loads[0].wait()
    loads[1].wait()
    send_halo(exchange(p, edges, 0), core1, ready)
    loads[2].wait()
    loads[3].wait()
    send_halo(exchange(p, edges, 1), core2)
    for ref in (slides, acc1, acc2, gp):
        ref[...] = jnp.zeros_like(ref)
    for load in loads[4:]:
        load.wait()

    def reorder(s, carry):
        inten[s] = into_paired_order(tab, inten[s])
        return carry

    lax.fori_loop(0, MAXPOS, reorder, 0)
    unpack_halo(exchange(p, edges, 0), ext1)

    stores = []
    for k, ext in enumerate((ext1, ext2)):
        for t in range(2):
            dst = obj_out.at[2 * k : 2 * k + 2, :, t * 128 : t * 128 + 128]
            stores.append(pltpu.make_async_copy(ext.at[:, t, 64:320], dst, local_sems.at[8 + 2 * k + t]))

    def iteration(it, carry):

        def forward(s):
            take_window(off_ref, s, ext1, win1)
            pr, pi, wr, wi = probe[0], probe[1], win1[s, 0], win1[s, 1]
            moved[s, 0], moved[s, 1] = propagate(tab, pr * wr - pi * wi, pr * wi + pi * wr, mids.at[s])

        def detector(s):
            take_window(off_ref, s, ext2, win2)
            er = moved[s, 0] * win2[s, 0] - moved[s, 1] * win2[s, 1]
            ei = moved[s, 0] * win2[s, 1] + moved[s, 1] * win2[s, 0]
            fr, fi = combine(*hartley(tab, 3, er, ei, mids.at[s]))
            misfit = fr * fr + fi * fi - inten[s]
            wr, wi = combine(misfit * fr, -(misfit * fi))
            cr, ci = hartley(tab, 4, wr, wi, mids.at[s])
            back[s, 0] = win2[s, 0] * cr - win2[s, 1] * ci
            back[s, 1] = win2[s, 0] * ci + win2[s, 1] * cr
            g2 = (moved[s, 0] * cr - moved[s, 1] * ci, -(moved[s, 0] * ci + moved[s, 1] * cr))
            add_window(off_ref, count_ref, s, g2, slides.at[s % 2], acc2)

        def adjoint(s):
            wr, wi = propagate(tab, back[s, 0], back[s, 1], mids.at[s])
            back[s, 0], back[s, 1] = wr, wi
            active = lax.broadcasted_iota(jnp.int32, (256, 128), 1) * 0 + s < count_ref[0, 0]
            sums = (win1[s, 0] * wr - win1[s, 1] * wi, -(win1[s, 0] * wi + win1[s, 1] * wr))
            for h in range(2):
                for t in range(2):
                    part = jnp.where(active, sums[h][:, t * 128 : t * 128 + 128], 0.0)
                    gp[h, 2 * t : 2 * t + 2] += part.reshape(2, 4, 32, 128)

        def first_slice(s):
            wr, wi = back[s, 0], back[s, 1]
            g1 = (probe[0] * wr - probe[1] * wi, -(probe[0] * wi + probe[1] * wr))
            add_window(off_ref, count_ref, s, g1, slides.at[s % 2], acc1)

        each_slot(forward)
        unpack_halo(exchange(p, edges, 4 * it + 1), ext2)
        each_slot(detector)
        fold2, fold1 = exchange(p, edges, 4 * it + 2), exchange(p, edges, 4 * it + 3)
        send_fold(fold2, acc2)
        each_slot(adjoint)

        bufs = [ref.at[it] for ref in (pair, made, parts, cross, whole)]
        s = Summer(p, gp, bufs, (sum_sems.at[it, 0], sum_sems.at[it, 1]))
        s.begin()
        each_slot(first_slice)
        s.over_plane()
        send_fold(fold1, acc1)
        rate = step_size(probe)
        descend_own(acc2, ext2, rate)
        descend_own(acc1, ext1, rate)
        acc1[...] = jnp.zeros_like(acc1)
        acc2[...] = jnp.zeros_like(acc2)
        for i in range(3):
            wait_sent(exchange(p, edges, 4 * it + i))
        descend(fold2, ext2, rate)

        @pl.when(it == ITERS - 1)
        def _():
            stores[2].start()
            stores[3].start()

        s.over_x()
        s.spread()
        descend(fold1, ext1, rate)

        @pl.when(it == 0)
        def _():
            send_halo(exchange(p, edges, 4), core1)
            send_halo(exchange(p, edges, 5), core2)

        @pl.when(it == ITERS - 1)
        def _():
            stores[0].start()
            stores[1].start()

        wait_sent(fold1)
        s.gather_pair()

        @pl.when(it == 0)
        def _():
            unpack_halo(exchange(p, edges, 4), ext1)

        gp[...] = jnp.zeros_like(gp)
        s.finish()
        for h in range(2):
            for t in range(2):
                lanes = slice(t * 128, t * 128 + 128)
                change = (probe_rate / (NTY * NTX)) * s.whole[h, 2 * t : 2 * t + 2].reshape(256, 128)
                probe[h, :, lanes] -= change
        s.sent()
        return carry

    lax.fori_loop(0, ITERS, iteration, 0)
    probe_out[...] = probe[...]
    for store in stores:
        store.wait()


def step_size(probe):
    power = probe[0] * probe[0] + probe[1] * probe[1]
    peak = jnp.max(power, axis=(0, 1), keepdims=True) + 1e-06
    return object_rate / peak


def run(count, off, obj, probe, inten, tab):
    smem = pl.BlockSpec(memory_space=pltpu.SMEM)
    anywhere = pl.BlockSpec(memory_space=pltpu.HBM)
    vm = pltpu.VMEM
    slots = vm((MAXPOS, 2, 256, 256), f32)
    return pl.pallas_call(
        program_kernel,
        out_shape=(jax.ShapeDtypeStruct((4, 256, 256), f32), jax.ShapeDtypeStruct((2, 256, 256), f32)),
        in_specs=[smem] + [anywhere] * 5,
        out_specs=(pl.BlockSpec(memory_space=pl.ANY), V),
        scratch_shapes=[
            vm((6, 2, 256, 256), bf),
            vm((MAXPOS, 256, 256), f32),
            vm((2, 3, 384, 128), f32),
            vm((2, 3, 384, 128), f32),
            vm((2, 3, 384, 128), f32),
            vm((2, 3, 384, 128), f32),
            vm((2, 4, 4, 32, 128), f32),
            vm((2, 2, 3, 512, 128), f32),
            slots,
            slots,
            slots,
            slots,
            slots,
            vm((2, 256, 256), f32),
            vm((EXCHANGES, 2, 2, 2, 2, 64, 128), f32),
            vm((EXCHANGES, 2, 2, 2, 128, 128), f32),
            vm((EXCHANGES, 2, 4, 2, 32, 128), f32),
            pltpu.SemaphoreType.DMA((EXCHANGES, 2, 8)),
            vm((SUMS, 4, 4, 32, 128), f32),
            vm((SUMS, 4, 4, 32, 128), f32),
            vm((SUMS, 4, 4, 32, 128), f32),
            vm((SUMS, 4, 32, 128), f32),
            vm((SUMS, 2, 4, 4, 32, 128), f32),
            pltpu.SemaphoreType.DMA((SUMS, 2, 48)),
            pltpu.SemaphoreType.DMA((12,)),
            pltpu.SMEM((2, MAXPOS), jnp.int32),
        ],
        compiler_params=pltpu.CompilerParams(collective_id=0, has_side_effects=True, vmem_limit_bytes=50 << 20),
        name="iterations",
    )(count, *[pltpu.with_memory_space_constraint(x, pltpu.HBM) for x in (off, obj, probe, inten, tab)])


def body(object_slices, probe, position_count, offsets, intensities):
    obj, probe = run(
        position_count,
        offsets[0, 0].T,
        object_slices.reshape(4, 256, 256),
        probe,
        intensities[0, 0],
        jnp.asarray(tables()),
    )
    return obj.reshape(2, 2, 256, 256), probe


def solution(mesh):
    placed = (
        P(None, None, "ty", "tx"),
        P(),
        P("ty", "tx"),
        P("ty", "tx", None, None),
        P("ty", "tx", None, None, None),
    )
    return jax.shard_map(
        body,
        mesh=mesh,
        in_specs=placed,
        out_specs=(P(None, None, "ty", "tx"), P()),
        check_vma=False,
    )
```

```python
import functools

import jax
import jax.numpy as jnp
import ml_dtypes
import numpy as np
from jax import lax
from jax.experimental import pallas as pl
from jax.experimental.pallas import tpu as pltpu
from jax.sharding import PartitionSpec as P

PROBE = 256
MAXPOS = 5
ITERS = 2
bf = jnp.bfloat16
f32 = jnp.float32

chirp_rate = 0.5
object_rate = 0.5
probe_rate = 2.0


def tables():
    n = PROBE
    k = np.arange(n)
    angle = 2 * np.pi * ((k[:, None] * k[None, :]) % n) / n
    four = np.exp(-1j * angle) / np.sqrt(n)
    c = (((k + n // 2) % n) - n // 2).astype(np.float64)
    prop = (np.conj(four) * np.exp(-1j * chirp_rate * np.pi * c * c / n)[None, :]) @ four
    order = np.concatenate([k[: n // 2], [n // 2], k[: n // 2 : -1]])
    hartley = ((np.cos(angle) + np.sin(angle)) / np.sqrt(2 * n))[order]
    swap = np.eye(n)[order]
    out = []
    for part in (prop.real, prop.imag - prop.real, prop.real + prop.imag, hartley, hartley.T):
        part = part.astype(np.float32)
        high = part.astype(ml_dtypes.bfloat16)
        out.append(np.stack([high, (part - high.astype(np.float32)).astype(ml_dtypes.bfloat16)]))
    out.append(np.stack([swap, swap.T]).astype(ml_dtypes.bfloat16))
    return np.stack(out)


def split(x):
    high = x.astype(bf)
    return high, (x - high.astype(f32)).astype(bf)


def dot(a, b):
    return jnp.dot(a, b, preferred_element_type=f32)


def left(tab, j, x):
    high, low = split(x)
    mat = jnp.concatenate([tab[j, 0], tab[j, 0], tab[j, 1]], axis=1)
    return dot(mat, jnp.concatenate([high, low, high], axis=0))


def right(tab, j, x):
    high, low = split(x)
    mat = jnp.concatenate([tab[j, 0], tab[j, 0], tab[j, 1]], axis=0)
    return dot(jnp.concatenate([high, low, high], axis=1), mat)


def propagate(tab, real, imag, mid):
    shared = left(tab, 0, real + imag)
    mid[1] = shared + left(tab, 1, real)
    mid[0] = shared - left(tab, 2, imag)
    real, imag = mid[0], mid[1]
    shared = right(tab, 0, real + imag)
    return shared - right(tab, 2, imag), shared + right(tab, 1, real)


def hartley(tab, j, real, imag, mid):
    mid[0], mid[1] = left(tab, j, real), left(tab, j, imag)
    return right(tab, 7 - j, mid[0]), right(tab, 7 - j, mid[1])


def mirror_rows(z):
    top, bottom = z[:128], z[128:]
    first = lax.broadcasted_iota(jnp.int32, (8, 256), 0) == 0
    new_top = jnp.where(first, top[:8], bottom[:8])
    new_bottom = jnp.where(first, bottom[:8], top[:8])
    return jnp.concatenate([new_top, bottom[8:], new_bottom, top[8:]], axis=0)


def mirror_columns(z):
    near, far = z[:, :128], z[:, 128:]
    first = lax.broadcasted_iota(jnp.int32, (256, 128), 1) == 0
    return jnp.concatenate([jnp.where(first, near, far), jnp.where(first, far, near)], axis=1)


def combine(real, imag):
    pairs = []
    for z in (real, imag):
        across = mirror_columns(z)
        pairs.append((mirror_rows(z) + across, z - mirror_rows(across)))
    (even_r, odd_r), (even_i, odd_i) = pairs
    return even_r + odd_i, even_i - odd_r


def into_paired_order(tab, x):
    for side in range(2):
        high, low = split(x)
        rest = (x - high.astype(f32) - low.astype(f32)).astype(bf)
        if side == 0:
            x = dot(tab[5, 0], high) + dot(tab[5, 0], low) + dot(tab[5, 0], rest)
        else:
            x = dot(high, tab[5, 1]) + dot(low, tab[5, 1]) + dot(rest, tab[5, 1])
    return x


NTY, NTX = 8, 16
MESH = pl.DeviceIdType.MESH
DIRS = [(1, 0), (-1, 0), (0, 1), (0, -1)]
V = pl.BlockSpec(memory_space=pltpu.VMEM)


def half_lanes(shape):
    return lax.broadcasted_iota(jnp.int32, shape, len(shape) - 1) < 64


def pack(x, side):
    rows = x.shape[1] // 2
    first, second = x[:, :rows], x[:, rows:]
    low = half_lanes(first.shape)
    if side > 0:
        return jnp.where(low, pltpu.roll(first, 64, 2), second)
    return jnp.where(low, first, pltpu.roll(second, 64, 2))


def unpack(buf, side):
    turned = pltpu.roll(buf, 64, 2)
    pair = [turned, buf] if side > 0 else [buf, turned]
    return jnp.concatenate(pair, axis=1)


def keep_side(x, side):
    low = half_lanes(x.shape)
    return jnp.where(low, 0.0, x) if side > 0 else jnp.where(low, x, 0.0)


class Place:
    def __init__(self):
        self.ty, self.tx = lax.axis_index("ty"), lax.axis_index("tx")
        self.x_lo, self.y = self.ty // 4, lax.rem(self.ty, 4)
        self.z, self.core = self.tx // 4, lax.rem(self.tx, 2)
        self.x_hi = lax.rem(self.tx // 2, 2)
        self.x = self.x_hi * 2 + self.x_lo

    def neighbour(self, dy, dx):
        return (lax.rem(self.ty + dy + NTY, NTY), lax.rem(self.tx + dx + NTX, NTX))

    def sibling(self):
        return (self.ty, self.tx + 1 - 2 * self.core)

    def turn(self, axis, k):
        x, y, z = self.x, self.y, self.z
        if axis == "x":
            x = lax.rem(x + k, 4)
        elif axis == "y":
            y = lax.rem(y + k, 4)
        else:
            z = lax.rem(z + k, 4)
        spot = {"x": x, "y": y, "z": z}[axis]
        return spot, (lax.rem(x, 2) * 4 + y, z * 4 + (x // 2) * 2 + self.core)


def remote(src, dst, send, recv, device):
    return pltpu.make_async_remote_copy(
        src_ref=src, dst_ref=dst, send_sem=send, recv_sem=recv, device_id=device, device_id_type=MESH
    )


class Edges:
    def __init__(self, place, bufs, sems):
        self.place, self.bufs = place, bufs
        self.send, self.recv = sems

    def slot(self, kind, way, d):
        return self.bufs[kind].at[way, (d + 1) // 2]

    def copy(self, kind, d):
        i = 2 * kind + (d + 1) // 2
        device = self.place.neighbour(0, d) if kind == COLS else self.place.neighbour(d, 0)
        src, dst = self.slot(kind, 0, d), self.slot(kind, 1, d)
        return remote(src, dst, self.send.at[i], self.recv.at[i], device)

    def post(self, kind, d, values):
        self.slot(kind, 0, d)[...] = values
        self.copy(kind, d).start()

    def get(self, kind, d):
        self.copy(kind, d).wait_recv()
        return self.slot(kind, 1, d)[...]


ROWS, COLS, STRIPS = 0, 1, 2


def send_halo(e, ext):
    for d in (1, -1):
        e.post(COLS, d, pack(ext[:, (d + 1) // 2, 64:320], d))
    for d in (1, -1):
        r0 = 256 if d > 0 else 64
        e.post(ROWS, d, ext[:, 0:2, r0 : r0 + 64])


def halo_strips(e, ext):
    left, right = unpack(e.get(COLS, -1), -1), unpack(e.get(COLS, 1), 1)
    ext[:, 2, 64:320] = jnp.where(half_lanes(left.shape), left, right)
    for d in (1, -1):
        r0 = 256 if d > 0 else 64
        e.post(STRIPS, d, ext[:, 2, r0 : r0 + 64])


def finish_halo(e, ext):
    for d in (1, -1):
        r0 = 320 if d < 0 else 0
        ext[:, 0:2, r0 : r0 + 64] = e.get(ROWS, d)
    for d in (1, -1):
        r0 = 320 if d < 0 else 0
        ext[:, 2, r0 : r0 + 64] = e.get(STRIPS, d)


def send_fold(e, g):
    for kind, t in ((STRIPS, 2), (ROWS, slice(0, 2))):
        for d in (1, -1):
            r0 = 320 if d > 0 else 0
            e.post(kind, d, g[:, t, r0 : r0 + 64])


def fold_columns(e, g):
    for d in (1, -1):
        r0 = 64 if d > 0 else 256
        g[:, 2, r0 : r0 + 64] += e.get(STRIPS, d)
    for d in (1, -1):
        e.post(COLS, d, pack(g[:, 2, 64:320], -d))


def descend_own(g, ext, rate):
    ext[:, 0:2, 64:320] -= rate * g[:, 0:2, 64:320]


def descend(e, ext, rate):
    for d in (1, -1):
        r0 = 64 if d > 0 else 256
        ext[:, 0:2, r0 : r0 + 64] -= rate * e.get(ROWS, d)
    for d in (1, -1):
        ext[:, (1 - d) // 2, 64:320] -= rate * keep_side(unpack(e.get(COLS, d), -d), -d)


def wait_sent(e):
    for kind in (ROWS, COLS, STRIPS):
        for d in (1, -1):
            e.copy(kind, d).wait_send()


class Summer:
    def __init__(self, place, gp, bufs, sems):
        self.p, self.gp = place, gp
        self.pair, self.made, self.parts, self.cross, self.whole = bufs
        self.send, self.recv = sems
        self.zs = [place.turn("z", k)[0] for k in range(4)]
        self.ys = [place.turn("y", k)[0] for k in range(4)]
        self.xs = [place.turn("x", k)[1] for k in range(4)]

    def copy(self, i, src, dst, device):
        return remote(src, dst, self.send.at[i], self.recv.at[i], device)

    def device(self, k, j):
        return (self.p.x_lo * 4 + self.ys[j], self.zs[k] * 4 + self.p.x_hi * 2 + self.p.core)

    def pair_copy(self, k):
        z = self.zs[k]
        return self.copy(k, self.gp.at[1 - self.p.core, z], self.pair.at[z], self.p.sibling())

    def plane_copy(self, k, j):
        return self.copy(8 + 4 * k + j, self.made.at[k, self.ys[j]], self.parts.at[k, j], self.device(k, j))

    def x_copy(self, k):
        own = self.cross.at[self.p.x]
        return self.copy(40 + k, own, own, self.xs[k])

    def back_copy(self, k, j):
        own = self.whole.at[self.p.core, self.p.z, self.p.y]
        return self.copy(24 + 4 * k + j, own, own, self.device(k, j))

    def forward_copy(self, k):
        own = self.whole.at[self.p.core, self.zs[(4 - k) % 4]]
        return self.copy(4 + k, own, own, self.p.sibling())

    def begin(self):
        for k in (2, 1, 3, 0):
            self.pair_copy(k).start()

    def over_plane(self):
        for k in (2, 1, 3, 0):
            z = self.zs[k]
            self.pair_copy(k).wait_recv()
            self.made[k] = self.gp[self.p.core, z] + self.pair[z]
            for j in (2, 1, 3, 0):
                if k or j:
                    self.plane_copy(k, j).start()

    def over_x(self):
        total = self.made[0, self.p.y]
        for k in (0, 1, 3, 2):
            for j in (0, 1, 3, 2):
                if k or j:
                    self.plane_copy(k, j).wait_recv()
                    total = total + self.parts[k, j]
        self.cross[self.p.x] = total
        for k in (2, 1, 3):
            self.x_copy(k).start()
        for k in range(4):
            self.pair_copy(k).wait_send()
            for j in range(4):
                if k or j:
                    self.plane_copy(k, j).wait_send()

    def spread(self):
        for k in (1, 3, 2):
            self.x_copy(k).wait_recv()
        own = (self.cross[0] + self.cross[1]) + (self.cross[2] + self.cross[3])
        self.whole[self.p.core, self.p.z, self.p.y] = own
        for k in (2, 1, 3, 0):
            for j in (2, 1, 3, 0):
                if k or j:
                    self.back_copy(k, j).start()

    def gather_pair(self):
        for k in (1, 2, 3):
            self.x_copy(k).wait_send()
        for k in (0, 1, 3, 2):
            for j in range(4):
                if k or j:
                    self.back_copy(k, j).wait_recv()
            self.forward_copy(k).start()
        for k in range(4):
            for j in range(4):
                if k or j:
                    self.back_copy(k, j).wait_send()

    def finish(self):
        for k in range(4):
            self.forward_copy(k).wait_recv()

    def sent(self):
        for k in range(4):
            self.forward_copy(k).wait_send()


def greet(p):
    barrier = pltpu.get_barrier_semaphore()
    devices = [p.neighbour(dy, dx) for dy, dx in DIRS] + [p.sibling()]
    devices += [p.turn("x", k)[1] for k in (1, 2, 3)]
    for k in range(4):
        z = p.turn("z", k)[0]
        for j in range(4):
            if k or j:
                devices.append((p.x_lo * 4 + p.turn("y", j)[0], z * 4 + p.x_hi * 2 + p.core))
    for device in devices:
        pl.semaphore_signal(barrier, inc=1, device_id=device, device_id_type=MESH)
    return lambda: pl.semaphore_wait(barrier, len(devices))


EXCHANGES = 8
SUMS = ITERS


def exchange(p, refs, i):
    rows, cols, strips, sems = [ref.at[i] for ref in refs]
    return Edges(p, (rows, cols, strips), (sems.at[0], sems.at[1]))


def shifts(off_ref, s):
    top, left_col = off_ref[0, s], off_ref[1, s]
    inner = left_col >= 64
    first = jnp.where(inner, 0, 2)
    second = jnp.where(inner, 1, 0)
    third = jnp.where(inner, 2, 1)
    return top, jnp.where(inner, left_col - 64, left_col + 64), (first, second, third)


def take_window(off_ref, s, ext, win):
    top, shift, tiles = shifts(off_ref, s)
    keep = lax.broadcasted_iota(jnp.int32, (256, 128), 1) < 128 - shift
    for p in range(2):
        a, b, c = [pltpu.roll(ext[p, t, pl.ds(top, 256), :], 128 - shift, 1) for t in tiles]
        win[s, p, :, 0:128] = jnp.where(keep, a, b)
        win[s, p, :, 128:256] = jnp.where(keep, b, c)


def add_window(off_ref, count_ref, s, pair, slide, acc):
    top, shift, (first, second, third) = shifts(off_ref, s)
    lane = lax.broadcasted_iota(jnp.int32, (256, 128), 1)
    before = lane < shift
    active = lane * 0 + s < count_ref[0, 0]
    for p in range(2):
        a, b = [
            pltpu.roll(jnp.where(active, pair[p][:, t * 128 : t * 128 + 128], 0.0), shift, 1) for t in range(2)
        ]
        slide[p, 0, 128:384] = jnp.where(before, 0.0, a)
        slide[p, 1, 128:384] = jnp.where(before, a, b)
        slide[p, 2, 128:384] = jnp.where(before, b, 0.0)
    inner = first == 0
    source = (jnp.where(inner, 0, 1), jnp.where(inner, 1, 2), jnp.where(inner, 2, 0))
    for p in range(2):
        for t in range(3):
            acc[p, t] += slide[p, source[t], pl.ds(128 - top, 384), :]


def each_slot(fn):
    for s in range(MAXPOS):
        fn(s)


def program_kernel(
    count_ref, off_hbm, obj_hbm, probe_hbm, inten_hbm, tab_hbm, obj_out, probe_out,
    tab, inten, ext1, ext2, acc1, acc2, gp, slides, win1, win2, moved, back, mids, probe,
    rows, cols, strips, edge_sems, pair, made, parts, cross, whole, sum_sems, local_sems, off_ref,
):
    p = Place()
    ready = greet(p)
    edges = (rows, cols, strips, edge_sems)
    loads = []
    for k, ext in enumerate((ext1, ext2)):
        for t in range(2):
            src = obj_hbm.at[2 * k : 2 * k + 2, :, t * 128 : t * 128 + 128]
            loads.append(pltpu.make_async_copy(src, ext.at[:, t, 64:320], local_sems.at[2 * k + t]))
    loads.append(pltpu.make_async_copy(probe_hbm, probe, local_sems.at[4]))
    loads.append(pltpu.make_async_copy(tab_hbm, tab, local_sems.at[5]))
    loads.append(pltpu.make_async_copy(inten_hbm, inten, local_sems.at[6]))
    loads.append(pltpu.make_async_copy(off_hbm, off_ref, local_sems.at[7]))
    for load in loads:
        load.start()
    loads[0].wait()
    loads[1].wait()
    ready()
    send_halo(exchange(p, edges, 0), ext1)
    loads[2].wait()
    loads[3].wait()
    send_halo(exchange(p, edges, 1), ext2)
    for ref in (slides, acc1, acc2, gp):
        ref[...] = jnp.zeros_like(ref)
    for load in loads[4:]:
        load.wait()

    halo_strips(exchange(p, edges, 0), ext1)
    for s in range(2):
        inten[s] = into_paired_order(tab, inten[s])
    finish_halo(exchange(p, edges, 0), ext1)

    def reorder(s, carry):
        inten[s] = into_paired_order(tab, inten[s])
        return carry

    lax.fori_loop(2, MAXPOS, reorder, 0)

    stores = []
    for k, ext in enumerate((ext1, ext2)):
        for t in range(2):
            dst = obj_out.at[2 * k : 2 * k + 2, :, t * 128 : t * 128 + 128]
            stores.append(pltpu.make_async_copy(ext.at[:, t, 64:320], dst, local_sems.at[8 + 2 * k + t]))

    def iteration(it, carry):

        def forward(s):
            take_window(off_ref, s, ext1, win1)
            pr, pi, wr, wi = probe[0], probe[1], win1[s, 0], win1[s, 1]
            moved[s, 0], moved[s, 1] = propagate(tab, pr * wr - pi * wi, pr * wi + pi * wr, mids.at[s])

        def detector(s):
            take_window(off_ref, s, ext2, win2)
            er = moved[s, 0] * win2[s, 0] - moved[s, 1] * win2[s, 1]
            ei = moved[s, 0] * win2[s, 1] + moved[s, 1] * win2[s, 0]
            fr, fi = combine(*hartley(tab, 3, er, ei, mids.at[s]))
            misfit = fr * fr + fi * fi - inten[s]
            wr, wi = combine(misfit * fr, -(misfit * fi))
            cr, ci = hartley(tab, 4, wr, wi, mids.at[s])
            back[s, 0] = win2[s, 0] * cr - win2[s, 1] * ci
            back[s, 1] = win2[s, 0] * ci + win2[s, 1] * cr
            g2 = (moved[s, 0] * cr - moved[s, 1] * ci, -(moved[s, 0] * ci + moved[s, 1] * cr))
            add_window(off_ref, count_ref, s, g2, slides.at[s % 2], acc2)

        def adjoint(s):
            wr, wi = propagate(tab, back[s, 0], back[s, 1], mids.at[s])
            back[s, 0], back[s, 1] = wr, wi
            active = lax.broadcasted_iota(jnp.int32, (256, 128), 1) * 0 + s < count_ref[0, 0]
            sums = (win1[s, 0] * wr - win1[s, 1] * wi, -(win1[s, 0] * wi + win1[s, 1] * wr))
            for h in range(2):
                for t in range(2):
                    part = jnp.where(active, sums[h][:, t * 128 : t * 128 + 128], 0.0)
                    gp[h, 2 * t : 2 * t + 2] += part.reshape(2, 4, 32, 128)

        def first_slice(s):
            wr, wi = back[s, 0], back[s, 1]
            g1 = (probe[0] * wr - probe[1] * wi, -(probe[0] * wi + probe[1] * wr))
            add_window(off_ref, count_ref, s, g1, slides.at[s % 2], acc1)

        for s in range(3):
            forward(s)
        halo2 = exchange(p, edges, 4 * it + 1)
        halo_strips(halo2, ext2)
        for s in range(3, MAXPOS):
            forward(s)
        finish_halo(halo2, ext2)
        each_slot(detector)
        fold2, fold1 = exchange(p, edges, 4 * it + 2), exchange(p, edges, 4 * it + 3)
        send_fold(fold2, acc2)
        for s in range(3):
            adjoint(s)
        fold_columns(fold2, acc2)
        for s in range(3, MAXPOS):
            adjoint(s)

        bufs = [ref.at[it] for ref in (pair, made, parts, cross, whole)]
        s = Summer(p, gp, bufs, (sum_sems.at[it, 0], sum_sems.at[it, 1]))
        s.begin()
        each_slot(first_slice)
        s.over_plane()
        send_fold(fold1, acc1)
        rate = step_size(probe)
        descend_own(acc2, ext2, rate)
        descend_own(acc1, ext1, rate)
        fold_columns(fold1, acc1)
        acc1[...] = jnp.zeros_like(acc1)
        acc2[...] = jnp.zeros_like(acc2)
        for i in range(3):
            wait_sent(exchange(p, edges, 4 * it + i))
        descend(fold2, ext2, rate)

        @pl.when(it == ITERS - 1)
        def _():
            stores[2].start()
            stores[3].start()

        s.over_x()
        s.spread()
        descend(fold1, ext1, rate)

        @pl.when(it == 0)
        def _():
            send_halo(exchange(p, edges, 4), ext1)
            send_halo(exchange(p, edges, 5), ext2)
            halo_strips(exchange(p, edges, 4), ext1)

        @pl.when(it == ITERS - 1)
        def _():
            stores[0].start()
            stores[1].start()

        wait_sent(fold1)
        s.gather_pair()

        @pl.when(it == 0)
        def _():
            finish_halo(exchange(p, edges, 4), ext1)

        gp[...] = jnp.zeros_like(gp)
        s.finish()
        for h in range(2):
            for t in range(2):
                lanes = slice(t * 128, t * 128 + 128)
                change = (probe_rate / (NTY * NTX)) * s.whole[h, 2 * t : 2 * t + 2].reshape(256, 128)
                probe[h, :, lanes] -= change
        s.sent()
        return carry

    lax.fori_loop(0, ITERS, iteration, 0)
    probe_out[...] = probe[...]
    for store in stores:
        store.wait()


def step_size(probe):
    power = probe[0] * probe[0] + probe[1] * probe[1]
    peak = jnp.max(power, axis=(0, 1), keepdims=True) + 1e-06
    return object_rate / peak


def run(count, off, obj, probe, inten, tab):
    smem = pl.BlockSpec(memory_space=pltpu.SMEM)
    anywhere = pl.BlockSpec(memory_space=pltpu.HBM)
    vm = pltpu.VMEM
    slots = vm((MAXPOS, 2, 256, 256), f32)
    return pl.pallas_call(
        program_kernel,
        out_shape=(jax.ShapeDtypeStruct((4, 256, 256), f32), jax.ShapeDtypeStruct((2, 256, 256), f32)),
        in_specs=[smem] + [anywhere] * 5,
        out_specs=(pl.BlockSpec(memory_space=pl.ANY), V),
        scratch_shapes=[
            vm((6, 2, 256, 256), bf),
            vm((MAXPOS, 256, 256), f32),
            vm((2, 3, 384, 128), f32),
            vm((2, 3, 384, 128), f32),
            vm((2, 3, 384, 128), f32),
            vm((2, 3, 384, 128), f32),
            vm((2, 4, 4, 32, 128), f32),
            vm((2, 2, 3, 512, 128), f32),
            slots,
            slots,
            slots,
            slots,
            slots,
            vm((2, 256, 256), f32),
            vm((EXCHANGES, 2, 2, 2, 2, 64, 128), f32),
            vm((EXCHANGES, 2, 2, 2, 128, 128), f32),
            vm((EXCHANGES, 2, 2, 2, 64, 128), f32),
            pltpu.SemaphoreType.DMA((EXCHANGES, 2, 6)),
            vm((SUMS, 4, 4, 32, 128), f32),
            vm((SUMS, 4, 4, 32, 128), f32),
            vm((SUMS, 4, 4, 32, 128), f32),
            vm((SUMS, 4, 32, 128), f32),
            vm((SUMS, 2, 4, 4, 32, 128), f32),
            pltpu.SemaphoreType.DMA((SUMS, 2, 48)),
            pltpu.SemaphoreType.DMA((12,)),
            pltpu.SMEM((2, MAXPOS), jnp.int32),
        ],
        compiler_params=pltpu.CompilerParams(collective_id=0, has_side_effects=True, vmem_limit_bytes=50 << 20),
        name="iterations",
    )(count, *[pltpu.with_memory_space_constraint(x, pltpu.HBM) for x in (off, obj, probe, inten, tab)])


def body(object_slices, probe, position_count, offsets, intensities):
    obj, probe = run(
        position_count,
        offsets[0, 0].T,
        object_slices.reshape(4, 256, 256),
        probe,
        intensities[0, 0],
        jnp.asarray(tables()),
    )
    return obj.reshape(2, 2, 256, 256), probe


def solution(mesh):
    placed = (
        P(None, None, "ty", "tx"),
        P(),
        P("ty", "tx"),
        P("ty", "tx", None, None),
        P("ty", "tx", None, None, None),
    )
    return jax.shard_map(
        body,
        mesh=mesh,
        in_specs=placed,
        out_specs=(P(None, None, "ty", "tx"), P()),
        check_vma=False,
    )
```

```python
import functools

import jax
import jax.numpy as jnp
import ml_dtypes
import numpy as np
from jax import lax
from jax.experimental import pallas as pl
from jax.experimental.pallas import tpu as pltpu
from jax.sharding import PartitionSpec as P

PROBE = 256
MAXPOS = 5
ITERS = 2
bf = jnp.bfloat16
f32 = jnp.float32

chirp_rate = 0.5
object_rate = 0.5
probe_rate = 2.0


def tables():
    n = PROBE
    k = np.arange(n)
    angle = 2 * np.pi * ((k[:, None] * k[None, :]) % n) / n
    four = np.exp(-1j * angle) / np.sqrt(n)
    c = (((k + n // 2) % n) - n // 2).astype(np.float64)
    prop = (np.conj(four) * np.exp(-1j * chirp_rate * np.pi * c * c / n)[None, :]) @ four
    order = np.concatenate([k[: n // 2], [n // 2], k[: n // 2 : -1]])
    hartley = ((np.cos(angle) + np.sin(angle)) / np.sqrt(2 * n))[order]
    swap = np.eye(n)[order]
    out = []
    for part in (prop.real, prop.imag - prop.real, prop.real + prop.imag, hartley, hartley.T):
        part = part.astype(np.float32)
        high = part.astype(ml_dtypes.bfloat16)
        out.append(np.stack([high, (part - high.astype(np.float32)).astype(ml_dtypes.bfloat16)]))
    out.append(np.stack([swap, swap.T]).astype(ml_dtypes.bfloat16))
    return np.stack(out)


def split(x):
    high = x.astype(bf)
    return high, (x - high.astype(f32)).astype(bf)


def dot(a, b):
    return jnp.dot(a, b, preferred_element_type=f32)


def left(tab, j, x):
    high, low = split(x)
    mat = jnp.concatenate([tab[j, 0], tab[j, 0], tab[j, 1]], axis=1)
    return dot(mat, jnp.concatenate([high, low, high], axis=0))


def right(tab, j, x):
    high, low = split(x)
    mat = jnp.concatenate([tab[j, 0], tab[j, 0], tab[j, 1]], axis=0)
    return dot(jnp.concatenate([high, low, high], axis=1), mat)


def propagate(tab, real, imag, mid):
    shared = left(tab, 0, real + imag)
    mid[1] = shared + left(tab, 1, real)
    mid[0] = shared - left(tab, 2, imag)
    real, imag = mid[0], mid[1]
    shared = right(tab, 0, real + imag)
    return shared - right(tab, 2, imag), shared + right(tab, 1, real)


def hartley(tab, j, real, imag, mid):
    mid[0], mid[1] = left(tab, j, real), left(tab, j, imag)
    return right(tab, 7 - j, mid[0]), right(tab, 7 - j, mid[1])


def mirror_rows(z):
    top, bottom = z[:128], z[128:]
    first = lax.broadcasted_iota(jnp.int32, (8, 256), 0) == 0
    new_top = jnp.where(first, top[:8], bottom[:8])
    new_bottom = jnp.where(first, bottom[:8], top[:8])
    return jnp.concatenate([new_top, bottom[8:], new_bottom, top[8:]], axis=0)


def mirror_columns(z):
    near, far = z[:, :128], z[:, 128:]
    first = lax.broadcasted_iota(jnp.int32, (256, 128), 1) == 0
    return jnp.concatenate([jnp.where(first, near, far), jnp.where(first, far, near)], axis=1)


def combine(real, imag):
    pairs = []
    for z in (real, imag):
        across = mirror_columns(z)
        pairs.append((mirror_rows(z) + across, z - mirror_rows(across)))
    (even_r, odd_r), (even_i, odd_i) = pairs
    return even_r + odd_i, even_i - odd_r


def into_paired_order(tab, x):
    for side in range(2):
        high, low = split(x)
        rest = (x - high.astype(f32) - low.astype(f32)).astype(bf)
        if side == 0:
            x = dot(tab[5, 0], high) + dot(tab[5, 0], low) + dot(tab[5, 0], rest)
        else:
            x = dot(high, tab[5, 1]) + dot(low, tab[5, 1]) + dot(rest, tab[5, 1])
    return x


NTY, NTX = 8, 16
MESH = pl.DeviceIdType.MESH
DIRS = [(dy, dx) for dy in (-1, 0, 1) for dx in (-1, 0, 1) if (dy, dx) != (0, 0)]
V = pl.BlockSpec(memory_space=pltpu.VMEM)


def half_lanes(shape):
    return lax.broadcasted_iota(jnp.int32, shape, len(shape) - 1) < 64


def pack(x, side):
    rows = x.shape[1] // 2
    first, second = x[:, :rows], x[:, rows:]
    low = half_lanes(first.shape)
    if side > 0:
        return jnp.where(low, pltpu.roll(first, 64, 2), second)
    return jnp.where(low, first, pltpu.roll(second, 64, 2))


def unpack(buf, side):
    turned = pltpu.roll(buf, 64, 2)
    pair = [turned, buf] if side > 0 else [buf, turned]
    return jnp.concatenate(pair, axis=1)


def keep_side(x, side):
    low = half_lanes(x.shape)
    return jnp.where(low, 0.0, x) if side > 0 else jnp.where(low, x, 0.0)


class Place:
    def __init__(self):
        self.ty, self.tx = lax.axis_index("ty"), lax.axis_index("tx")
        self.x_lo, self.y = self.ty // 4, lax.rem(self.ty, 4)
        self.z, self.core = self.tx // 4, lax.rem(self.tx, 2)
        self.x_hi = lax.rem(self.tx // 2, 2)
        self.x = self.x_hi * 2 + self.x_lo

    def neighbour(self, dy, dx):
        return (lax.rem(self.ty + dy + NTY, NTY), lax.rem(self.tx + dx + NTX, NTX))

    def sibling(self):
        return (self.ty, self.tx + 1 - 2 * self.core)

    def turn(self, axis, k):
        x, y, z = self.x, self.y, self.z
        if axis == "x":
            x = lax.rem(x + k, 4)
        elif axis == "y":
            y = lax.rem(y + k, 4)
        else:
            z = lax.rem(z + k, 4)
        spot = {"x": x, "y": y, "z": z}[axis]
        return spot, (lax.rem(x, 2) * 4 + y, z * 4 + (x // 2) * 2 + self.core)


def remote(src, dst, send, recv, device):
    return pltpu.make_async_remote_copy(
        src_ref=src, dst_ref=dst, send_sem=send, recv_sem=recv, device_id=device, device_id_type=MESH
    )


class Edges:
    def __init__(self, place, rows, cols, corners, sems):
        self.place, self.rows, self.cols, self.corners = place, rows, cols, corners
        self.send, self.recv = sems

    def slot(self, bufs, dy, dx):
        if dx == 0:
            return bufs[0].at[(dy + 1) // 2]
        if dy == 0:
            return bufs[1].at[(dx + 1) // 2]
        return bufs[2].at[(dy + 1) + (dx + 1) // 2]

    def out(self, dy, dx):
        return self.slot((self.rows[0], self.cols[0], self.corners[0]), dy, dx)

    def inc(self, dy, dx):
        return self.slot((self.rows[1], self.cols[1], self.corners[1]), dy, dx)

    def copy(self, dy, dx):
        i = DIRS.index((dy, dx))
        return remote(self.out(dy, dx), self.inc(dy, dx), self.send.at[i], self.recv.at[i], self.place.neighbour(dy, dx))


ORDER = [(1, 1), (1, -1), (-1, 1), (-1, -1), (0, 1), (0, -1), (1, 0), (-1, 0)]


def send_halo(e, core, ready=None):
    for dy, dx in ORDER:
        r0, r1 = {-1: (0, 64), 0: (0, 256), 1: (192, 256)}[dy]
        if dx == 0:
            for t in range(2):
                e.out(dy, dx)[:, t] = core(t, r0, r1)
        else:
            e.out(dy, dx)[...] = pack(core((dx + 1) // 2, r0, r1), dx)
        if ready is None:
            e.copy(dy, dx).start()
    if ready is not None:
        ready()
        for dy, dx in ORDER:
            e.copy(dy, dx).start()


def unpack_halo(e, ext):
    for dy in (-1, 1):
        e.copy(dy, 0).wait_recv()
        r0 = 320 if dy < 0 else 0
        for t in range(2):
            ext[:, t, r0 : r0 + 64] = e.inc(dy, 0)[:, t]
    for dy in (0, -1, 1):
        e.copy(dy, -1).wait_recv()
        e.copy(dy, 1).wait_recv()
        r0, r1 = {-1: (320, 384), 0: (64, 320), 1: (0, 64)}[dy]
        left, right = unpack(e.inc(dy, -1)[...], -1), unpack(e.inc(dy, 1)[...], 1)
        ext[:, 2, r0:r1] = jnp.where(half_lanes(left.shape), left, right)


def send_fold(e, g):
    for dy, dx in ORDER:
        r0, r1 = {-1: (0, 64), 0: (64, 320), 1: (320, 384)}[dy]
        if dx == 0:
            for t in range(2):
                e.out(dy, dx)[:, t] = g[:, t, r0:r1]
        else:
            e.out(dy, dx)[...] = pack(g[:, 2, r0:r1], -dx)
        e.copy(dy, dx).start()


def step_down(ext, t, r0, r1, change):
    ext[:, t, 64 + r0 : 64 + r1] -= change


def descend_own(g, ext, rate):
    for t in range(2):
        step_down(ext, t, 0, 256, rate * g[:, t, 64:320])


def descend(e, ext, rate):
    for dy, dx in ORDER[4:] + ORDER[:4]:
        e.copy(dy, dx).wait_recv()
        r0, r1 = {-1: (192, 256), 0: (0, 256), 1: (0, 64)}[dy]
        if dx == 0:
            for t in range(2):
                step_down(ext, t, r0, r1, rate * e.inc(dy, dx)[:, t])
        else:
            values = keep_side(unpack(e.inc(dy, dx)[...], -dx), -dx)
            step_down(ext, (1 - dx) // 2, r0, r1, rate * values)


def wait_sent(e):
    for dy, dx in ORDER:
        e.copy(dy, dx).wait_send()


class Summer:
    def __init__(self, place, gp, bufs, sems):
        self.p, self.gp = place, gp
        self.pair, self.made, self.parts, self.cross, self.whole = bufs
        self.send, self.recv = sems
        self.zs = [place.turn("z", k)[0] for k in range(4)]
        self.ys = [place.turn("y", k)[0] for k in range(4)]
        self.xs = [place.turn("x", k)[1] for k in range(4)]

    def copy(self, i, src, dst, device):
        return remote(src, dst, self.send.at[i], self.recv.at[i], device)

    def device(self, k, j):
        return (self.p.x_lo * 4 + self.ys[j], self.zs[k] * 4 + self.p.x_hi * 2 + self.p.core)

    def pair_copy(self, k):
        z = self.zs[k]
        return self.copy(k, self.gp.at[1 - self.p.core, z], self.pair.at[z], self.p.sibling())

    def plane_copy(self, k, j):
        return self.copy(8 + 4 * k + j, self.made.at[k, self.ys[j]], self.parts.at[k, j], self.device(k, j))

    def x_copy(self, k):
        own = self.cross.at[self.p.x]
        return self.copy(40 + k, own, own, self.xs[k])

    def back_copy(self, k, j):
        own = self.whole.at[self.p.core, self.p.z, self.p.y]
        return self.copy(24 + 4 * k + j, own, own, self.device(k, j))

    def forward_copy(self, k):
        own = self.whole.at[self.p.core, self.zs[(4 - k) % 4]]
        return self.copy(4 + k, own, own, self.p.sibling())

    def begin(self):
        for k in (2, 1, 3, 0):
            self.pair_copy(k).start()

    def over_plane(self):
        for k in (2, 1, 3, 0):
            z = self.zs[k]
            self.pair_copy(k).wait_recv()
            self.made[k] = self.gp[self.p.core, z] + self.pair[z]
            for j in (2, 1, 3, 0):
                if k or j:
                    self.plane_copy(k, j).start()

    def over_x(self):
        total = self.made[0, self.p.y]
        for k in (0, 1, 3, 2):
            for j in (0, 1, 3, 2):
                if k or j:
                    self.plane_copy(k, j).wait_recv()
                    total = total + self.parts[k, j]
        self.cross[self.p.x] = total
        for k in (2, 1, 3):
            self.x_copy(k).start()
        for k in range(4):
            self.pair_copy(k).wait_send()
            for j in range(4):
                if k or j:
                    self.plane_copy(k, j).wait_send()

    def spread(self):
        for k in (1, 3, 2):
            self.x_copy(k).wait_recv()
        own = (self.cross[0] + self.cross[1]) + (self.cross[2] + self.cross[3])
        self.whole[self.p.core, self.p.z, self.p.y] = own
        for k in (2, 1, 3, 0):
            for j in (2, 1, 3, 0):
                if k or j:
                    self.back_copy(k, j).start()

    def gather_pair(self):
        for k in (1, 2, 3):
            self.x_copy(k).wait_send()
        for k in (0, 1, 3, 2):
            for j in range(4):
                if k or j:
                    self.back_copy(k, j).wait_recv()
            self.forward_copy(k).start()
        for k in range(4):
            for j in range(4):
                if k or j:
                    self.back_copy(k, j).wait_send()

    def finish(self):
        for k in range(4):
            self.forward_copy(k).wait_recv()

    def sent(self):
        for k in range(4):
            self.forward_copy(k).wait_send()


def greet(p):
    barrier = pltpu.get_barrier_semaphore()
    devices = [p.neighbour(dy, dx) for dy, dx in DIRS] + [p.sibling()]
    devices += [p.turn("x", k)[1] for k in (1, 2, 3)]
    for k in range(4):
        z = p.turn("z", k)[0]
        for j in range(4):
            if k or j:
                devices.append((p.x_lo * 4 + p.turn("y", j)[0], z * 4 + p.x_hi * 2 + p.core))
    for device in devices:
        pl.semaphore_signal(barrier, inc=1, device_id=device, device_id_type=MESH)
    return lambda: pl.semaphore_wait(barrier, len(devices))


EXCHANGES = 8
SUMS = ITERS


def exchange(p, refs, i):
    rows, cols, corners, sems = [ref.at[i] for ref in refs]
    pair = lambda ref: (ref.at[0], ref.at[1])
    return Edges(p, pair(rows), pair(cols), pair(corners), pair(sems))


def shifts(off_ref, s):
    top, left_col = off_ref[0, s], off_ref[1, s]
    inner = left_col >= 64
    first = jnp.where(inner, 0, 2)
    second = jnp.where(inner, 1, 0)
    third = jnp.where(inner, 2, 1)
    return top, jnp.where(inner, left_col - 64, left_col + 64), (first, second, third)


def take_window(off_ref, s, ext, win):
    top, shift, tiles = shifts(off_ref, s)
    keep = lax.broadcasted_iota(jnp.int32, (256, 128), 1) < 128 - shift
    for p in range(2):
        a, b, c = [pltpu.roll(ext[p, t, pl.ds(top, 256), :], 128 - shift, 1) for t in tiles]
        win[s, p, :, 0:128] = jnp.where(keep, a, b)
        win[s, p, :, 128:256] = jnp.where(keep, b, c)


def add_window(off_ref, count_ref, s, pair, slide, acc):
    top, shift, (first, second, third) = shifts(off_ref, s)
    lane = lax.broadcasted_iota(jnp.int32, (256, 128), 1)
    before = lane < shift
    active = lane * 0 + s < count_ref[0, 0]
    for p in range(2):
        a, b = [
            pltpu.roll(jnp.where(active, pair[p][:, t * 128 : t * 128 + 128], 0.0), shift, 1) for t in range(2)
        ]
        slide[p, 0, 128:384] = jnp.where(before, 0.0, a)
        slide[p, 1, 128:384] = jnp.where(before, a, b)
        slide[p, 2, 128:384] = jnp.where(before, b, 0.0)
    inner = first == 0
    source = (jnp.where(inner, 0, 1), jnp.where(inner, 1, 2), jnp.where(inner, 2, 0))
    for p in range(2):
        for t in range(3):
            acc[p, t] += slide[p, source[t], pl.ds(128 - top, 384), :]


def each_slot(fn):
    for s in range(MAXPOS):
        fn(s)


def program_kernel(
    count_ref, off_hbm, obj_hbm, probe_hbm, inten_hbm, tab_hbm, obj_out, probe_out,
    tab, inten, ext1, ext2, acc1, acc2, gp, slides, win1, win2, moved, back, mids, probe,
    rows, cols, corners, edge_sems, pair, made, parts, cross, whole, sum_sems, local_sems, off_ref,
):
    p = Place()
    ready = greet(p)
    edges = (rows, cols, corners, edge_sems)
    loads = []
    for k, ext in enumerate((ext1, ext2)):
        for t in range(2):
            src = obj_hbm.at[2 * k : 2 * k + 2, :, t * 128 : t * 128 + 128]
            loads.append(pltpu.make_async_copy(src, ext.at[:, t, 64:320], local_sems.at[2 * k + t]))
    loads.append(pltpu.make_async_copy(probe_hbm, probe, local_sems.at[4]))
    loads.append(pltpu.make_async_copy(tab_hbm, tab, local_sems.at[5]))
    loads.append(pltpu.make_async_copy(inten_hbm, inten, local_sems.at[6]))
    loads.append(pltpu.make_async_copy(off_hbm, off_ref, local_sems.at[7]))
    for load in loads:
        load.start()
    core1 = lambda t, r0, r1: ext1[:, t, 64 + r0 : 64 + r1]
    core2 = lambda t, r0, r1: ext2[:, t, 64 + r0 : 64 + r1]
    loads[0].wait()
    loads[1].wait()
    send_halo(exchange(p, edges, 0), core1, ready)
    loads[2].wait()
    loads[3].wait()
    send_halo(exchange(p, edges, 1), core2)
    for ref in (slides, acc1, acc2, gp):
        ref[...] = jnp.zeros_like(ref)
    for load in loads[4:]:
        load.wait()

    def reorder(s, carry):
        inten[s] = into_paired_order(tab, inten[s])
        return carry

    lax.fori_loop(0, MAXPOS, reorder, 0)
    unpack_halo(exchange(p, edges, 0), ext1)

    stores = []
    for k, ext in enumerate((ext1, ext2)):
        for t in range(2):
            dst = obj_out.at[2 * k : 2 * k + 2, :, t * 128 : t * 128 + 128]
            stores.append(pltpu.make_async_copy(ext.at[:, t, 64:320], dst, local_sems.at[8 + 2 * k + t]))

    def iteration(it, carry):

        def forward(s):
            take_window(off_ref, s, ext1, win1)
            pr, pi, wr, wi = probe[0], probe[1], win1[s, 0], win1[s, 1]
            moved[s, 0], moved[s, 1] = propagate(tab, pr * wr - pi * wi, pr * wi + pi * wr, mids.at[s])

        def detector(s):
            take_window(off_ref, s, ext2, win2)
            er = moved[s, 0] * win2[s, 0] - moved[s, 1] * win2[s, 1]
            ei = moved[s, 0] * win2[s, 1] + moved[s, 1] * win2[s, 0]
            fr, fi = combine(*hartley(tab, 3, er, ei, mids.at[s]))
            misfit = fr * fr + fi * fi - inten[s]
            wr, wi = combine(misfit * fr, -(misfit * fi))
            cr, ci = hartley(tab, 4, wr, wi, mids.at[s])
            back[s, 0] = win2[s, 0] * cr - win2[s, 1] * ci
            back[s, 1] = win2[s, 0] * ci + win2[s, 1] * cr
            g2 = (moved[s, 0] * cr - moved[s, 1] * ci, -(moved[s, 0] * ci + moved[s, 1] * cr))
            add_window(off_ref, count_ref, s, g2, slides.at[s % 2], acc2)

        def adjoint(s):
            wr, wi = propagate(tab, back[s, 0], back[s, 1], mids.at[s])
            back[s, 0], back[s, 1] = wr, wi
            active = lax.broadcasted_iota(jnp.int32, (256, 128), 1) * 0 + s < count_ref[0, 0]
            sums = (win1[s, 0] * wr - win1[s, 1] * wi, -(win1[s, 0] * wi + win1[s, 1] * wr))
            for h in range(2):
                for t in range(2):
                    part = jnp.where(active, sums[h][:, t * 128 : t * 128 + 128], 0.0)
                    gp[h, 2 * t : 2 * t + 2] += part.reshape(2, 4, 32, 128)

        def first_slice(s):
            wr, wi = back[s, 0], back[s, 1]
            g1 = (probe[0] * wr - probe[1] * wi, -(probe[0] * wi + probe[1] * wr))
            add_window(off_ref, count_ref, s, g1, slides.at[s % 2], acc1)

        each_slot(forward)
        unpack_halo(exchange(p, edges, 4 * it + 1), ext2)
        each_slot(detector)
        fold2, fold1 = exchange(p, edges, 4 * it + 2), exchange(p, edges, 4 * it + 3)
        send_fold(fold2, acc2)
        each_slot(adjoint)

        bufs = [ref.at[it] for ref in (pair, made, parts, cross, whole)]
        s = Summer(p, gp, bufs, (sum_sems.at[it, 0], sum_sems.at[it, 1]))
        s.begin()
        each_slot(first_slice)
        s.over_plane()

        @pl.when(it == 0)
        def _():
            send_fold(fold1, acc1)

        rate = step_size(probe)
        descend_own(acc2, ext2, rate)
        descend_own(acc1, ext1, rate)
        acc2[...] = jnp.zeros_like(acc2)
        for i in range(3):
            wait_sent(exchange(p, edges, 4 * it + i))
        descend(fold2, ext2, rate)

        @pl.when(it == ITERS - 1)
        def _():
            stores[2].start()
            stores[3].start()

        s.over_x()

        @pl.when(it == ITERS - 1)
        def _():
            send_fold(fold1, acc1)

        acc1[...] = jnp.zeros_like(acc1)
        s.spread()
        descend(fold1, ext1, rate)

        @pl.when(it == 0)
        def _():
            send_halo(exchange(p, edges, 4), core1)
            send_halo(exchange(p, edges, 5), core2)

        @pl.when(it == ITERS - 1)
        def _():
            stores[0].start()
            stores[1].start()

        wait_sent(fold1)
        s.gather_pair()

        @pl.when(it == 0)
        def _():
            unpack_halo(exchange(p, edges, 4), ext1)

        gp[...] = jnp.zeros_like(gp)
        s.finish()
        for h in range(2):
            for t in range(2):
                lanes = slice(t * 128, t * 128 + 128)
                change = (probe_rate / (NTY * NTX)) * s.whole[h, 2 * t : 2 * t + 2].reshape(256, 128)
                probe[h, :, lanes] -= change
        s.sent()
        return carry

    lax.fori_loop(0, ITERS, iteration, 0)
    probe_out[...] = probe[...]
    for store in stores:
        store.wait()


def step_size(probe):
    power = probe[0] * probe[0] + probe[1] * probe[1]
    peak = jnp.max(power, axis=(0, 1), keepdims=True) + 1e-06
    return object_rate / peak


def run(count, off, obj, probe, inten, tab):
    smem = pl.BlockSpec(memory_space=pltpu.SMEM)
    anywhere = pl.BlockSpec(memory_space=pltpu.HBM)
    vm = pltpu.VMEM
    slots = vm((MAXPOS, 2, 256, 256), f32)
    return pl.pallas_call(
        program_kernel,
        out_shape=(jax.ShapeDtypeStruct((4, 256, 256), f32), jax.ShapeDtypeStruct((2, 256, 256), f32)),
        in_specs=[smem] + [anywhere] * 5,
        out_specs=(pl.BlockSpec(memory_space=pl.ANY), V),
        scratch_shapes=[
            vm((6, 2, 256, 256), bf),
            vm((MAXPOS, 256, 256), f32),
            vm((2, 3, 384, 128), f32),
            vm((2, 3, 384, 128), f32),
            vm((2, 3, 384, 128), f32),
            vm((2, 3, 384, 128), f32),
            vm((2, 4, 4, 32, 128), f32),
            vm((2, 2, 3, 512, 128), f32),
            slots,
            slots,
            slots,
            slots,
            slots,
            vm((2, 256, 256), f32),
            vm((EXCHANGES, 2, 2, 2, 2, 64, 128), f32),
            vm((EXCHANGES, 2, 2, 2, 128, 128), f32),
            vm((EXCHANGES, 2, 4, 2, 32, 128), f32),
            pltpu.SemaphoreType.DMA((EXCHANGES, 2, 8)),
            vm((SUMS, 4, 4, 32, 128), f32),
            vm((SUMS, 4, 4, 32, 128), f32),
            vm((SUMS, 4, 4, 32, 128), f32),
            vm((SUMS, 4, 32, 128), f32),
            vm((SUMS, 2, 4, 4, 32, 128), f32),
            pltpu.SemaphoreType.DMA((SUMS, 2, 48)),
            pltpu.SemaphoreType.DMA((12,)),
            pltpu.SMEM((2, MAXPOS), jnp.int32),
        ],
        compiler_params=pltpu.CompilerParams(collective_id=0, has_side_effects=True, vmem_limit_bytes=50 << 20),
        name="iterations",
    )(count, *[pltpu.with_memory_space_constraint(x, pltpu.HBM) for x in (off, obj, probe, inten, tab)])


def body(object_slices, probe, position_count, offsets, intensities):
    obj, probe = run(
        position_count,
        offsets[0, 0].T,
        object_slices.reshape(4, 256, 256),
        probe,
        intensities[0, 0],
        jnp.asarray(tables()),
    )
    return obj.reshape(2, 2, 256, 256), probe


def solution(mesh):
    placed = (
        P(None, None, "ty", "tx"),
        P(),
        P("ty", "tx"),
        P("ty", "tx", None, None),
        P("ty", "tx", None, None, None),
    )
    return jax.shard_map(
        body,
        mesh=mesh,
        in_specs=placed,
        out_specs=(P(None, None, "ty", "tx"), P()),
        check_vma=False,
    )
```
